32 devices in a mesh: fsdp: 8 (over y, x, core), tensor: 4 (over z).
Axes of the slice: x: 2, y: 2, z: 4, core: 2. Of those that a mesh axis runs over, the one named last changes fastest.
Arguments:
- tokens: bfloat16 [16384, 768], P(('fsdp', 'tensor')), may hold values from -6 to 6
- segments: int32 [8, 2048], P('fsdp'), may hold values from 0 to 8, as said below
- query_weight: bfloat16 [768, 768], P('fsdp', 'tensor'), may hold values from -0.21875 to 0.21875
- query_bias: float32 [768], replicated, may hold values from -3 to 3
- key_weight: bfloat16 [768, 768], P('fsdp', 'tensor'), may hold values from -0.21875 to 0.21875
- value_weight: bfloat16 [768, 768], P('fsdp', 'tensor'), may hold values from -0.21875 to 0.21875
- value_bias: float32 [768], replicated, may hold values from -3 to 3
- mix_weight: bfloat16 [768, 768], P('tensor', 'fsdp'), may hold values from -1.75 to 1.75
- mix_bias: float32 [768], replicated, may hold values from -3 to 3
- norm_gain: float32 [768], replicated, may hold values from 0.25 to 1.75
- norm_shift: float32 [768], replicated, may hold values from -3 to 3
- up_weight: bfloat16 [768, 3072], P('fsdp', 'tensor'), may hold values from -0.21875 to 0.21875
- up_bias: float32 [3072], replicated, may hold values from -3 to 3
- down_weight: bfloat16 [3072, 768], P('tensor', 'fsdp'), may hold values from -0.109375 to 0.109375
- down_bias: float32 [768], replicated, may hold values from -3 to 3
- final_gain: float32 [768], replicated, may hold values from 0.25 to 1.75
- final_shift: float32 [768], replicated, may hold values from -3 to 3
- out_grad: bfloat16 [16384, 768], P(('fsdp', 'tensor')), may hold values from -6 to 6
Outputs:
- layer_out: bfloat16 [16384, 768], P(('fsdp', 'tensor'))
- tokens_grad: float32 [16384, 768], P(('fsdp', 'tensor'))
- query_weight_grad: float32 [768, 768], P('fsdp', 'tensor')
- query_bias_grad: float32 [768], replicated
- key_weight_grad: float32 [768, 768], P('fsdp', 'tensor')
- value_weight_grad: float32 [768, 768], P('fsdp', 'tensor')
- value_bias_grad: float32 [768], replicated
- mix_weight_grad: float32 [768, 768], P('tensor', 'fsdp')
- mix_bias_grad: float32 [768], replicated
- norm_gain_grad: float32 [768], replicated
- norm_shift_grad: float32 [768], replicated
- up_weight_grad: float32 [768, 3072], P('fsdp', 'tensor')
- up_bias_grad: float32 [3072], replicated
- down_weight_grad: float32 [3072, 768], P('tensor', 'fsdp')
- down_bias_grad: float32 [768], replicated
- final_gain_grad: float32 [768], replicated
- final_shift_grad: float32 [768], replicated
The draws below stay inside these ranges and needn't reach their ends.
Inputs may be any that keep to these rules, and one draw needn't show every extreme that they name: `segments`: each row is one sequence: its live part begins at the first position and its ids never decrease along it, running from 1 to 8, with 8 reached in every row and some ids possibly skipped; after it come 1 to 256 padding positions with id 0.
All inputs are finite; a program needn't handle non-finite values.
Results may differ from the reference program's by a relative error of at most 0.013.
The reference program's roundings to bfloat16 on the way count: a program that leaves them out, or rounds other values in their place, can miss the bound.
Values may be sent and summed in bfloat16 or wider, within the bound.
No kernel may reach another device: no remote copies, remote signals or barrier semaphores. Data moves between devices by JAX's collectives and lax.ppermute only.
A program may use at most 128 MiB of HBM per device.

```python
import jax
import jax.numpy as jnp
from jax import lax

D = 768
HEADS = 12
HD = 64
FF = 3072
LEN = 2048
DOCS = 8
NSEQ = 8
TOKENS = 16384


def draw_segments(key, part):
    row_keys = jax.random.split(jax.random.fold_in(key, 7), NSEQ)

    def one_row(row_key):
        pad_key, cut_key = jax.random.split(row_key)
        padding = jax.random.randint(pad_key, (), 1, LEN // 8 + 1)
        live_count = LEN - padding
        roots = jax.random.randint(cut_key, (DOCS - 1,), 0, 256)
        cuts = 1 + roots * roots * (live_count - 1) // 65536
        position = jnp.arange(LEN, dtype=jnp.int32)
        ids_live = 1 + jnp.sum((position[:, None] >= cuts[None, :]).astype(jnp.int32), axis=1)
        return jnp.where(position < live_count, ids_live, 0).astype(jnp.int32)
    return jax.vmap(one_row)(row_keys)


def shard_levels(rng, shape, pieces, smallest, high):
    def one(dim, shards_of):
        steps = jax.random.uniform(jax.random.fold_in(jax.random.fold_in(rng, 6), dim), (shards_of,), jnp.float32, smallest / len(pieces), high / len(pieces))
        return jnp.repeat(jnp.exp(steps), shape[dim] // shards_of).reshape((-1,) + (1,) * (len(shape) - dim - 1))

    loudness = one(*pieces[0])
    for cut in pieces[1:]:
        loudness = loudness * one(*cut)
    return loudness


def bell_draw(rng, dims, scale, bound, cuts=(), kind=jnp.bfloat16):
    result = jax.random.normal(rng, dims, jnp.float32) * scale
    if len(cuts) > 0:
        result = shard_levels(rng, dims, cuts, -0.22, 0.18) * result
    return jnp.clip(result, min=-bound, max=bound).astype(kind)


def setup_inputs(seed: int = 0) -> dict:
    keys = jax.random.split(jax.random.key(seed), 19)
    tokens = bell_draw(keys[0], (TOKENS, D), 1.0, 6.0, ((0, 32),))
    segments = draw_segments(jax.random.fold_in(keys[18], 71), 0)
    query_weight = bell_draw(keys[2], (D, D), D ** -0.5, 0.21875, ((0, 8), (1, 4)))
    query_bias = bell_draw(keys[3], (D,), 0.5, 3.0, (), jnp.float32)
    key_weight = bell_draw(keys[4], (D, D), D ** -0.5, 0.21875, ((0, 8), (1, 4)))
    value_weight = bell_draw(keys[5], (D, D), D ** -0.5, 0.21875, ((0, 8), (1, 4)))
    value_bias = bell_draw(keys[6], (D,), 0.5, 3.0, (), jnp.float32)
    mix_weight = bell_draw(keys[7], (D, D), (max(D // 64, 1)) ** -0.5, 1.75, ((0, 4), (1, 8)))
    mix_bias = bell_draw(keys[8], (D,), 0.5, 3.0, (), jnp.float32)
    norm_gain = jnp.clip(1.0 + 0.15 * jax.random.normal(keys[9], (D,), jnp.float32), 0.25, 1.75)
    norm_shift = bell_draw(keys[10], (D,), 0.5, 3.0, (), jnp.float32)
    up_weight = bell_draw(keys[11], (D, FF), D ** -0.5, 0.21875, ((0, 8), (1, 4)))
    up_bias = bell_draw(keys[12], (FF,), 0.5, 3.0, (), jnp.float32)
    down_weight = bell_draw(keys[13], (FF, D), FF ** -0.5, 0.109375, ((0, 4), (1, 8)))
    down_bias = bell_draw(keys[14], (D,), 0.5, 3.0, (), jnp.float32)
    final_gain = jnp.clip(1.0 + 0.15 * jax.random.normal(keys[15], (D,), jnp.float32), 0.25, 1.75)
    final_shift = bell_draw(keys[16], (D,), 0.5, 3.0, (), jnp.float32)
    out_grad = bell_draw(keys[17], (TOKENS, D), 1.0, 6.0, ((0, 32),))
    return {"tokens": tokens, "segments": segments, "query_weight": query_weight, "query_bias": query_bias, "key_weight": key_weight, "value_weight": value_weight, "value_bias": value_bias, "mix_weight": mix_weight, "mix_bias": mix_bias, "norm_gain": norm_gain, "norm_shift": norm_shift, "up_weight": up_weight, "up_bias": up_bias, "down_weight": down_weight, "down_bias": down_bias, "final_gain": final_gain, "final_shift": final_shift, "out_grad": out_grad}


EPSILON = 1e-05
MASKED = -1e+30

@jax.custom_vjp
def low(v):
    return lax.optimization_barrier(v.astype(jnp.bfloat16)).astype(jnp.float32)

@jax.custom_vjp
def low_back(v):
    return v

def low_keep(v):
    return (low(v), None)

def low_pass(kept, grad):
    return (grad,)

def back_keep(v):
    return (v, None)

def back_low(kept, grad):
    return (low(grad),)
low.defvjp(low_keep, low_pass)
low_back.defvjp(back_keep, back_low)

def product(left_rows, right_matrix):
    return jnp.dot(left_rows, right_matrix, precision=lax.Precision.HIGHEST)

def norm_rows(rows_in, gain_row, shift_row):
    row_mean = lax.optimization_barrier(jnp.mean(rows_in, axis=-1, keepdims=True))
    centred = rows_in - row_mean
    spread = lax.optimization_barrier(jnp.mean(centred * centred, axis=-1, keepdims=True))
    return centred * lax.rsqrt(spread + EPSILON) * gain_row + shift_row

def attend(query_heads, key_heads, value_heads, seg_row):
    query_rows = min(512, LEN)
    blocks = LEN // query_rows
    query_blocks = query_heads.reshape(blocks, query_rows, HEADS, HD)
    seg_blocks = seg_row.reshape(blocks, query_rows)

    def one_block(block_item):
        query_block, seg_block = block_item
        scores = jnp.einsum('qhd,khd->hqk', query_block, key_heads, precision=lax.Precision.HIGHEST) * HD ** (-0.5)
        scores = low_back(scores)
        same_doc = (seg_block[:, None] == seg_row[None, :])[None]
        scores = jnp.where(same_doc, scores, MASKED)
        attn_probs = low(jax.nn.softmax(scores, axis=-1))
        return jnp.einsum('hqk,khd->qhd', attn_probs, value_heads, precision=lax.Precision.HIGHEST)
    mixed_out = lax.map(jax.checkpoint(one_block), (query_blocks, seg_blocks))
    return mixed_out.reshape(LEN, HEADS * HD)

def layer(rows_seq, seg_row, query_weight, query_bias, key_weight, value_weight, value_bias, mix_weight, mix_bias, norm_gain, norm_shift, up_weight, up_bias, down_weight, down_bias, final_gain, final_shift):
    head_shape = (LEN, HEADS, HD)
    query_heads = low(low_back(product(rows_seq, query_weight) + query_bias)).reshape(head_shape)
    key_heads = low(low_back(product(rows_seq, key_weight))).reshape(head_shape)
    value_heads = low(low_back(product(rows_seq, value_weight) + value_bias)).reshape(head_shape)
    context = low(low_back(attend(query_heads, key_heads, value_heads, seg_row)))
    first_sum = rows_seq + low_back(product(context, mix_weight)) + mix_bias
    normed = norm_rows(first_sum, norm_gain, norm_shift)
    pre_act = low_back(product(low(normed), up_weight) + up_bias)
    activated = low(jax.nn.gelu(pre_act, approximate=True))
    second_sum = normed + low_back(product(activated, down_weight)) + down_bias
    return norm_rows(second_sum, final_gain, final_shift)

def reference(tokens, segments, query_weight, query_bias, key_weight, value_weight, value_bias, mix_weight, mix_bias, norm_gain, norm_shift, up_weight, up_bias, down_weight, down_bias, final_gain, final_shift, out_grad):
    weights = tuple((entry.astype(jnp.float32) for entry in (query_weight, query_bias, key_weight, value_weight, value_bias, mix_weight, mix_bias, norm_gain, norm_shift, up_weight, up_bias, down_weight, down_bias, final_gain, final_shift)))
    seqs_in = tokens.astype(jnp.float32).reshape(-1, LEN, D)
    live_rows = (segments > 0).astype(jnp.float32)
    cotangents = out_grad.astype(jnp.float32).reshape(-1, LEN, D) * live_rows[:, :, None]

    def one_sequence(carried, seq_item):
        rows_in, seg_row, cot_row = seq_item

        def forward(rows_seq, *params):
            return layer(rows_seq, seg_row, *params)
        value_out, pullback = jax.vjp(forward, rows_in, *weights)
        all_grads = pullback(cot_row)
        carried = tuple((running + fresh for running, fresh in zip(carried, all_grads[1:])))
        return (carried, (value_out.astype(jnp.bfloat16), all_grads[0]))
    start_sums = tuple((jnp.zeros(entry.shape, jnp.float32) for entry in weights))
    sums_out, (outs_seq, grads_seq) = lax.scan(one_sequence, start_sums, (seqs_in, segments, cotangents))
    return (outs_seq.reshape(-1, D), grads_seq.reshape(-1, D), sums_out[0], sums_out[1], sums_out[2], sums_out[3], sums_out[4], sums_out[5], sums_out[6], sums_out[7], sums_out[8], sums_out[9], sums_out[10], sums_out[11], sums_out[12], sums_out[13], sums_out[14])
```

```python
from functools import partial

import jax
import jax.numpy as jnp
from jax import lax
from jax.experimental import pallas as pl
from jax.experimental.pallas import tpu as pltpu
from jax.sharding import PartitionSpec as P

HD = 64
LANES = 128
EPSILON = 1e-05
MASKED = -1e30
BLOCK = 256
LOG2E = 1.4426950408889634
BF = jnp.bfloat16
F32 = jnp.float32


def gather_line(own):
    t = lax.axis_index("tensor")
    below = lax.ppermute(own, "tensor", [(0, 1), (1, 2), (2, 3)])
    above = lax.ppermute(own, "tensor", [(1, 0), (2, 1), (3, 2)])
    slot_a = jnp.where(t < 3, above, below)
    below2 = lax.ppermute(below, "tensor", [(1, 2), (2, 3)])
    above2 = lax.ppermute(above, "tensor", [(2, 1), (1, 0)])
    slot_c = jnp.where(t < 2, above2, below2)
    far = lax.ppermute(slot_c, "tensor", [(1, 0), (2, 3)])
    slot_b = jnp.where((t == 0) | (t == 3), far, below)
    return own, slot_a, slot_c, slot_b


def slot_owner(t):
    return (
        t,
        jnp.where(t < 3, t + 1, 2),
        lax.rem(t + 2, 4),
        jnp.where(t == 3, 0, lax.rem(t + 3, 4)),
    )


def line_order(slots):
    t = lax.axis_index("tensor")
    own, a, c, b = slots

    def pick(v0, v1, v2, v3):
        return jnp.where(t == 0, v0, jnp.where(t == 1, v1, jnp.where(t == 2, v2, v3)))

    return [
        pick(own, b, c, b),
        pick(a, own, b, c),
        pick(c, a, own, a),
        pick(b, c, a, own),
    ]


def reduce_line(part):
    t = lax.axis_index("tensor")
    ends = [(0, 1), (3, 2)]
    b, c, a, own = part("B"), part("C"), part("A"), part("own")
    r1 = lax.ppermute(b.astype(BF), "tensor", ends).astype(F32)
    c = (c.astype(F32) + r1).astype(BF)
    rx = lax.ppermute(c, "tensor", ends).astype(F32)
    ry = lax.ppermute(c, "tensor", [(1, 2), (2, 1)]).astype(F32)
    up = (a.astype(F32) + jnp.where(t == 1, rx, ry)).astype(BF)
    down = jnp.where(t == 3, a.astype(F32), b.astype(F32) + jnp.where(t == 1, ry, rx)).astype(BF)
    from_below = lax.ppermute(up, "tensor", [(0, 1), (1, 2), (2, 3)])
    from_above = lax.ppermute(down, "tensor", [(1, 0), (2, 1), (3, 2)])
    return own.astype(F32) + from_below.astype(F32) + from_above.astype(F32)


def partner(bit):
    n = lax.axis_size("fsdp")
    return [(i, i ^ bit) for i in range(n)]


def fsdp_bits():
    n = lax.axis_size("fsdp")
    bits = [1 << k for k in range(n.bit_length() - 1)]
    return bits


def grow(block, bit):
    f = lax.axis_index("fsdp")
    other = lax.ppermute(block, "fsdp", partner(bit))
    high = (f & bit) != 0
    return jnp.stack([jnp.where(high, other, block), jnp.where(high, block, other)])


def gather_fsdp(block):
    n = lax.axis_size("fsdp")
    bits = fsdp_bits()
    m, r, c = block.shape
    half = m // 2
    outer = bits[1:]
    pieces = []
    for rows, order in ((block[:half], outer), (block[half:], outer[::-1])):
        done = []
        for bit in order:
            rows = grow(rows, bit)
            done.insert(0, bit)
        rows = grow(rows, bits[0])
        done.insert(0, bits[0])
        k = len(done)
        want = sorted(done, reverse=True)
        axes = [k] + [done.index(b) for b in want] + [k + 1, k + 2]
        pieces.append(rows.transpose(axes).reshape(half, n * r, c))
    return jnp.concatenate(pieces, axis=0)


def halve(block, axis, bit):
    f = lax.axis_index("fsdp")
    mine = jnp.where((f & bit) != 0, 1, 0)
    keep = lax.dynamic_index_in_dim(block, mine, axis, keepdims=False)
    send = lax.dynamic_index_in_dim(block, 1 - mine, axis, keepdims=False)
    got = lax.ppermute(send, "fsdp", partner(bit))
    return (keep.astype(F32) + got.astype(F32)).astype(BF)


def reduce_fsdp(block):
    n = lax.axis_size("fsdp")
    bits = fsdp_bits()
    k = len(bits)
    m, rows, c = block.shape
    block = block.reshape((m,) + (2,) * k + (rows // n, c))
    block = halve(block, k, bits[0])
    half = m // 2
    pieces = []
    for part, order in ((block[:half], bits[1:]), (block[half:], bits[:0:-1])):
        left = sorted(bits[1:], reverse=True)
        for bit in order:
            part = halve(part, 1 + left.index(bit), bit)
            left.remove(bit)
        pieces.append(part)
    return jnp.concatenate(pieces, axis=0)


def sum_everywhere(vector):
    for bit in fsdp_bits():
        vector = vector + lax.ppermute(vector, "fsdp", partner(bit))
    for bit in (1, 2):
        vector = vector + lax.ppermute(vector, "tensor", [(i, i ^ bit) for i in range(4)])
    return vector


def nt(a, b):
    return lax.dot_general(a, b, (((1,), (1,)), ((), ())), preferred_element_type=F32)


def nn(a, b):
    return lax.dot_general(a, b, (((1,), (0,)), ((), ())), preferred_element_type=F32)


def tn(a, b):
    return lax.dot_general(a, b, (((0,), (0,)), ((), ())), preferred_element_type=F32)


def head_mask(shape, h):
    lane = lax.broadcasted_iota(jnp.int32, shape, len(shape) - 1)
    return (lane < HD) if h == 0 else (lane >= HD)


def forward_kernel(flags, q_ref, k_ref, v_ref, sq_ref, sk_ref, o_ref, lse_ref, m_s, l_s, acc_s):
    j = pl.program_id(1)
    nk = k_ref.shape[0] // BLOCK
    m_s[...] = jnp.full_like(m_s, MASKED)
    l_s[...] = jnp.zeros_like(l_s)
    acc_s[...] = jnp.zeros_like(acc_s)
    q = q_ref[...]
    seg_q = sq_ref[...]
    q_heads = [jnp.where(head_mask(q.shape, h), q, jnp.zeros_like(q)) for h in range(2)]
    for kb in range(nk):

        @pl.when(flags[j * nk + kb] != 0)
        def _():
            rows = pl.ds(kb * BLOCK, BLOCK)
            k = k_ref[rows, :]
            v = v_ref[rows, :]
            same = seg_q == sk_ref[:, rows]
            for h in range(2):
                s = nt(q_heads[h], k) * (HD**-0.5 * LOG2E)
                s = jnp.where(same, s, MASKED)
                m_old = m_s[h]
                m_new = jnp.maximum(m_old, jnp.max(s, axis=1, keepdims=True))
                alpha = jnp.exp2(m_old - m_new)
                p = jnp.exp2(s - m_new)
                l_s[h] = alpha * l_s[h] + jnp.sum(p, axis=1, keepdims=True)
                acc_s[h] = alpha * acc_s[h] + nn(p.astype(BF), v)
                m_s[h] = m_new

    out = [acc_s[h] / l_s[h] for h in range(2)]
    o_ref[...] = jnp.where(head_mask(out[0].shape, 0), out[0], out[1]).astype(o_ref.dtype)
    for h in range(2):
        lse = m_s[h] + jnp.log2(l_s[h])
        wide = jnp.broadcast_to(lse, (BLOCK, LANES)).T
        lse_ref[0, h : h + 1, :] = wide[0:1, :]


def attend_forward(q, k, v, seg_q, seg_k, flags):
    rows, width = q.shape
    keys = k.shape[0]
    pairs = width // LANES
    return pl.pallas_call(
        forward_kernel,
        out_shape=(
            jax.ShapeDtypeStruct((rows, width), BF),
            jax.ShapeDtypeStruct((pairs, 2, rows), F32),
        ),
        grid_spec=pltpu.PrefetchScalarGridSpec(
            num_scalar_prefetch=1,
            grid=(pairs, rows // BLOCK),
            in_specs=[
                pl.BlockSpec((BLOCK, LANES), lambda i, j, f: (j, i)),
                pl.BlockSpec((keys, LANES), lambda i, j, f: (0, i)),
                pl.BlockSpec((keys, LANES), lambda i, j, f: (0, i)),
                pl.BlockSpec((BLOCK, 1), lambda i, j, f: (j, 0)),
                pl.BlockSpec((1, keys), lambda i, j, f: (0, 0)),
            ],
            out_specs=[
                pl.BlockSpec((BLOCK, LANES), lambda i, j, f: (j, i)),
                pl.BlockSpec((1, 2, BLOCK), lambda i, j, f: (i, 0, j)),
            ],
            scratch_shapes=[
                pltpu.VMEM((2, BLOCK, 1), F32),
                pltpu.VMEM((2, BLOCK, 1), F32),
                pltpu.VMEM((2, BLOCK, LANES), F32),
            ],
        ),
        cost_estimate=pl.CostEstimate(
            flops=4 * rows * keys * width, bytes_accessed=4 * keys * width, transcendentals=rows * keys * width // HD
        ),
        name="attend_forward",
    )(flags, q, k, v, seg_q[:, None], seg_k[None, :])


def backward_kernel(
    flags, q_ref, k_ref, v_ref, do_ref, o_ref, lse_ref, sq_ref, sk_ref, dq_ref, dk_ref, dv_ref, dk_s, dv_s, dq_s
):
    j = pl.program_id(1)
    nk = k_ref.shape[0] // BLOCK

    @pl.when(j == 0)
    def _():
        dk_s[...] = jnp.zeros_like(dk_s)
        dv_s[...] = jnp.zeros_like(dv_s)

    dq_s[...] = jnp.zeros_like(dq_s)
    q = q_ref[...]
    do = do_ref[...]
    zero = jnp.zeros_like(q)
    masks = [head_mask(q.shape, h) for h in range(2)]
    q_heads = [jnp.where(m, q, zero) for m in masks]
    do_heads = [jnp.where(m, do, zero) for m in masks]
    prod = (do.astype(F32) * o_ref[...].astype(F32)).T
    delta = [jnp.sum(prod[h * HD : (h + 1) * HD], axis=0, keepdims=True) for h in range(2)]
    lse = [lse_ref[0, h : h + 1, :] for h in range(2)]
    seg_q = sq_ref[...]
    for kb in range(nk):

        @pl.when(flags[j * nk + kb] != 0)
        def _():
            rows = pl.ds(kb * BLOCK, BLOCK)
            k = k_ref[rows, :]
            v = v_ref[rows, :]
            same = sk_ref[rows, :] == seg_q
            dk = dk_s[rows, :]
            dv = dv_s[rows, :]
            dq = [None, None]
            for h in range(2):
                s = nt(k, q_heads[h]) * (HD**-0.5 * LOG2E)
                p = jnp.exp2(jnp.where(same, s - lse[h], MASKED))
                dp = nt(v, do_heads[h])
                ds = (p * (dp - delta[h])).astype(BF)
                dv = dv + nn(p.astype(BF), do_heads[h])
                dk = dk + nn(ds, q_heads[h])
                dq[h] = tn(ds, k)
            dk_s[rows, :] = dk
            dv_s[rows, :] = dv
            dq_s[...] += jnp.where(masks[0], dq[0], dq[1])

    dq_ref[...] = (dq_s[...] * HD**-0.5).astype(BF)

    @pl.when(j == pl.num_programs(1) - 1)
    def _():
        dk_ref[...] = (dk_s[...] * HD**-0.5).astype(BF)
        dv_ref[...] = dv_s[...].astype(BF)


def attend_backward(q, k, v, do, o, lse, seg_q, seg_k, flags):
    rows, width = q.shape
    keys = k.shape[0]
    pairs = width // LANES
    q_spec = pl.BlockSpec((BLOCK, LANES), lambda i, j, f: (j, i))
    k_spec = pl.BlockSpec((keys, LANES), lambda i, j, f: (0, i))
    return pl.pallas_call(
        backward_kernel,
        out_shape=(
            jax.ShapeDtypeStruct((rows, width), BF),
            jax.ShapeDtypeStruct((keys, width), BF),
            jax.ShapeDtypeStruct((keys, width), BF),
        ),
        grid_spec=pltpu.PrefetchScalarGridSpec(
            num_scalar_prefetch=1,
            grid=(pairs, rows // BLOCK),
            in_specs=[
                q_spec,
                k_spec,
                k_spec,
                q_spec,
                q_spec,
                pl.BlockSpec((1, 2, BLOCK), lambda i, j, f: (i, 0, j)),
                pl.BlockSpec((1, BLOCK), lambda i, j, f: (0, j)),
                pl.BlockSpec((keys, 1), lambda i, j, f: (0, 0)),
            ],
            out_specs=[q_spec, k_spec, k_spec],
            scratch_shapes=[
                pltpu.VMEM((keys, LANES), F32),
                pltpu.VMEM((keys, LANES), F32),
                pltpu.VMEM((BLOCK, LANES), F32),
            ],
        ),
        cost_estimate=pl.CostEstimate(
            flops=10 * rows * keys * width, bytes_accessed=8 * keys * width, transcendentals=rows * keys * width // HD
        ),
        name="attend_backward",
    )(flags, q, k, v, do, o, lse, seg_q[None, :], seg_k[:, None])


def overlap_flags(seg_q, seg_k):
    qb = seg_q.reshape(-1, BLOCK)
    kb = seg_k.reshape(-1, BLOCK)
    q_lo, q_hi = qb.min(axis=1), qb.max(axis=1)
    k_lo, k_hi = kb.min(axis=1), kb.max(axis=1)
    meet = (q_lo[:, None] <= k_hi[None, :]) & (k_lo[None, :] <= q_hi[:, None])
    return meet.astype(jnp.int32).reshape(-1)


def norm_parts(rows_in):
    mean = jnp.mean(rows_in, axis=-1, keepdims=True)
    centred = rows_in - mean
    spread = jnp.mean(centred * centred, axis=-1, keepdims=True)
    r = lax.rsqrt(spread + EPSILON)
    return centred * r, r


def norm_back(g_y, n, r, gain):
    e = g_y * gain
    g_s = r * (e - jnp.mean(e, axis=-1, keepdims=True) - n * jnp.mean(e * n, axis=-1, keepdims=True))
    return g_s, jnp.sum(g_y * n, axis=0), jnp.sum(g_y, axis=0)


def gelu_parts(u):
    c = 0.7978845608028654
    th = jnp.tanh(c * (u + 0.044715 * u * u * u))
    act = 0.5 * u * (1.0 + th)
    slope = 0.5 * (1.0 + th) + 0.5 * u * (1.0 - th * th) * c * (1.0 + 3 * 0.044715 * u * u)
    return act, slope


def on_device(
    tokens,
    segments,
    query_weight,
    query_bias,
    key_weight,
    value_weight,
    value_bias,
    mix_weight,
    mix_bias,
    norm_gain,
    norm_shift,
    up_weight,
    up_bias,
    down_weight,
    down_bias,
    final_gain,
    final_shift,
    out_grad,
):
    t = lax.axis_index("tensor")
    rows, width = tokens.shape
    units = up_weight.shape[1]
    parts = 4

    attn_shard = jnp.stack([query_weight, key_weight, value_weight, mix_weight.T])
    attn_line = jnp.concatenate(line_order(gather_line(attn_shard)), axis=2)
    x_slots = gather_line(tokens)
    up_line = jnp.stack(line_order(gather_line(up_weight)))
    down_line = jnp.stack(line_order(gather_line(down_weight.T)))
    attn_w = gather_fsdp(attn_line)
    up_w = gather_fsdp(up_line)
    down_w = gather_fsdp(down_line)

    x_all = jnp.concatenate(x_slots, axis=0)
    seg = jnp.where(segments == 0, 9, segments).reshape(parts, rows)
    slot_ids = slot_owner(t)
    seg_q = lax.dynamic_index_in_dim(seg, t, 0, keepdims=False)
    seg_k = jnp.concatenate([lax.dynamic_index_in_dim(seg, i, 0, keepdims=False) for i in slot_ids])
    flags = overlap_flags(seg_q, seg_k)
    wq, wk, wv, wm_t = (attn_w[i] for i in range(4))
    q = (nn(tokens, wq) + query_bias).astype(BF)
    k = nn(x_all, wk).astype(BF)
    v = (nn(x_all, wv) + value_bias).astype(BF)
    ctx, lse = attend_forward(q, k, v, seg_q, seg_k, flags)

    first_sum = tokens.astype(F32) + nt(ctx, wm_t) + mix_bias
    n1, r1 = norm_parts(first_sum)
    normed = n1 * norm_gain + norm_shift
    normed_low = normed.astype(BF)
    bias_blocks = up_bias.reshape(parts, units)
    pre = [nn(normed_low, up_w[i]) + bias_blocks[i] for i in range(parts)]
    act = [gelu_parts(u)[0].astype(BF) for u in pre]
    ffn = sum(nt(a, down_w[i]) for i, a in enumerate(act))
    second_sum = normed + ffn + down_bias
    n2, r2 = norm_parts(second_sum)
    layer_out = (n2 * final_gain + final_shift).astype(BF)

    g_out = out_grad.astype(F32) * jnp.where(seg_q < 9, 1.0, 0.0)[:, None]
    g_second, d_final_gain, d_final_shift = norm_back(g_out, n2, r2, final_gain)
    second_low = g_second.astype(BF)
    d_down = jnp.stack([tn(second_low, a).astype(BF) for a in act])
    g_pre = [
        (nn(second_low, down_w[i]) * gelu_parts(pre[i])[1]).astype(BF) for i in range(parts)
    ]
    d_up = jnp.stack([tn(normed_low, g).astype(BF) for g in g_pre])
    g_normed = g_second + sum(nt(g, up_w[i]) for i, g in enumerate(g_pre))
    g_first, d_norm_gain, d_norm_shift = norm_back(g_normed, n1, r1, norm_gain)
    first_low = g_first.astype(BF)
    g_ctx = nn(first_low, wm_t).astype(BF)
    d_mix = tn(first_low, ctx).astype(BF)

    d_down_f = reduce_fsdp(d_down)
    d_up_f = reduce_fsdp(d_up)

    early = sum_everywhere(
        jnp.concatenate(
            [
                jnp.sum(g_first, axis=0),
                d_norm_gain,
                d_norm_shift,
                jnp.sum(g_second, axis=0),
                d_final_gain,
                d_final_shift,
            ]
            + [jnp.sum(g.astype(F32), axis=0) for g in g_pre]
        )
    )

    dq, dk, dv = attend_backward(q, k, v, g_ctx, ctx, lse, seg_q, seg_k, flags)
    dx_part = nt(dk, wk) + nt(dv, wv)

    def dx_slot(slot):
        at = {"own": 0, "A": 1, "C": 2, "B": 3}[slot]
        block = dx_part[at * rows : (at + 1) * rows]
        if slot == "own":
            return block + g_first + nt(dq, wq)
        return block.astype(BF)

    tokens_grad = reduce_line(dx_slot)
    d_attn = jnp.stack(
        [tn(tokens, dq).astype(BF), tn(x_all, dk).astype(BF), tn(x_all, dv).astype(BF), d_mix]
    )
    d_attn_f = reduce_fsdp(d_attn)
    late = sum_everywhere(
        jnp.concatenate(
            [jnp.sum(dq.astype(F32), axis=0), jnp.sum(dv.astype(F32), axis=0)]
        )
    )

    def line_sum(blocks):
        ids = dict(zip(("own", "A", "C", "B"), slot_ids))
        return reduce_line(lambda s: lax.dynamic_index_in_dim(blocks, ids[s], 0, keepdims=False))

    down_grad = line_sum(d_down_f).T
    up_grad = line_sum(d_up_f)
    cols = width // parts
    attn_blocks = jnp.stack([d_attn_f[:, :, i * cols : (i + 1) * cols] for i in range(parts)])
    attn_grad = line_sum(attn_blocks)

    names = [
        early[i * width : (i + 1) * width] for i in range(6)
    ]
    return (
        layer_out,
        tokens_grad,
        attn_grad[0],
        late[:width],
        attn_grad[1],
        attn_grad[2],
        late[width:],
        attn_grad[3].T,
        names[0],
        names[1],
        names[2],
        up_grad,
        early[6 * width :],
        down_grad,
        names[3],
        names[4],
        names[5],
    )


def solution(mesh):
    both, rows_f, square, flipped = (
        P(("fsdp", "tensor"), None),
        P("fsdp", None),
        P("fsdp", "tensor"),
        P("tensor", "fsdp"),
    )
    return jax.shard_map(
        on_device,
        mesh=mesh,
        in_specs=(
            both, rows_f, square, P(), square, square, P(), flipped, P(), P(), P(),
            square, P(), flipped, P(), P(), P(), both,
        ),
        out_specs=(
            both, both, square, P(), square, square, P(), flipped, P(), P(), P(),
            square, P(), flipped, P(), P(), P(),
        ),
        check_vma=False,
    )
```

```python
from functools import partial

import jax
import jax.numpy as jnp
from jax import lax
from jax.experimental import pallas as pl
from jax.experimental.pallas import tpu as pltpu
from jax.sharding import PartitionSpec as P

HD = 64
GROUP = 256
BLOCK = 256
EPSILON = 1e-05
MASKED = -1e30
LOG2E = 1.4426950408889634
SCORE = HD**-0.5 * LOG2E
FEW = 1000
BF = jnp.bfloat16
F32 = jnp.float32


def after(value, *others):
    return lax.optimization_barrier((value,) + others)[0] if others else value


def nt(a, b):
    return lax.dot_general(a, b, (((1,), (1,)), ((), ())), preferred_element_type=F32)


def nn(a, b):
    return lax.dot_general(a, b, (((1,), (0,)), ((), ())), preferred_element_type=F32)


def line_first(own):
    below = lax.ppermute(own, "tensor", [(0, 1), (1, 2), (2, 3)])
    above = lax.ppermute(own, "tensor", [(1, 0), (2, 1), (3, 2)])
    return jnp.where(lax.axis_index("tensor") < 3, above, below), below, above


def line_second(below, above, *gate):
    below2 = lax.ppermute(below, "tensor", [(1, 2), (2, 3)])
    above2 = lax.ppermute(above, "tensor", [(2, 1), (1, 0)])
    below2, above2 = after((below2, above2), *gate)
    return jnp.where(lax.axis_index("tensor") < 2, above2, below2)


def line_third(slot_c, below, *gate):
    far = after(lax.ppermute(slot_c, "tensor", [(1, 0), (2, 3)]), *gate)
    t = lax.axis_index("tensor")
    return jnp.where((t == 0) | (t == 3), far, below)


def slot_owner(t):
    return jnp.stack([t, jnp.where(t < 3, t + 1, 2), lax.rem(t + 2, 4), jnp.where(t == 3, 0, lax.rem(t + 3, 4))])


def owner_slot(t):
    owner = slot_owner(t)
    places = jnp.arange(4)
    return [jnp.sum(jnp.where(owner == j, places, 0)) for j in range(4)]


def in_line_order(slots, t):
    return jnp.concatenate([lax.dynamic_slice_in_dim(slots, s, 1, axis=0) for s in owner_slot(t)])


def spread(blocks):
    arrived = lax.all_to_all(blocks, "tensor", split_axis=0, concat_axis=0, tiled=True)
    return jnp.sum(arrived.astype(F32), axis=0)


def partner(bit):
    n = lax.axis_size("fsdp")
    return [(i, i ^ bit) for i in range(n)]


def sum_everywhere(vector):
    for k in range(lax.axis_size("fsdp").bit_length() - 1):
        vector = vector + lax.ppermute(vector, "fsdp", partner(1 << k))
    for bit in (1, 2):
        vector = vector + lax.ppermute(vector, "tensor", [(i, i ^ bit) for i in range(4)])
    return vector


def outer_bits():
    n = lax.axis_size("fsdp")
    return [1 << k for k in range(1, n.bit_length() - 1)]


def joined(block, other, bit, have, ordered):
    have = sorted(have + [bit], reverse=True)
    pair = [block, other]
    if ordered:
        high = (lax.axis_index("fsdp") & bit) != 0
        pair = [jnp.where(high, other, block), jnp.where(high, block, other)]
    return jnp.stack(pair, axis=1 + have.index(bit)), have


def gather_outer(halves, ordered, gate):
    bits = outer_bits()
    have = [[], []]
    for step, pair in enumerate(zip(bits, bits[::-1])):
        others = tuple(lax.ppermute(h, "fsdp", partner(bit)) for h, bit in zip(halves, pair))
        others = gate(step, others)
        grown = [joined(h, o, bit, hv, ordered) for h, o, bit, hv in zip(halves, others, pair, have)]
        halves, have = [g[0] for g in grown], [g[1] for g in grown]
    return [h.reshape(h.shape[0], -1, *h.shape[-2:]) for h in halves]


def in_place(near, far):
    high = (lax.axis_index("fsdp") & 1) != 0
    full = jnp.stack([jnp.where(high, far, near), jnp.where(high, near, far)], axis=2)
    return full.reshape(near.shape[0], -1, near.shape[-1])


def from_relative(near, far):
    n = lax.axis_size("fsdp")
    f = lax.axis_index("fsdp")
    blocks = []
    for a in range(n):
        rel = f ^ a
        pair = [lax.dynamic_slice_in_dim(w, rel >> 1, 1, axis=1) for w in (near, far)]
        blocks.append(jnp.where((rel & 1) == 0, pair[0], pair[1]))
    full = jnp.concatenate(blocks, axis=1)
    return full.reshape(full.shape[0], -1, full.shape[-1])


def halve(block, axis, bit):
    keep = lax.index_in_dim(block, 0, axis, keepdims=False)
    send = lax.index_in_dim(block, 1, axis, keepdims=False)
    got = lax.ppermute(send, "fsdp", partner(bit))
    return (keep.astype(F32) + got.astype(F32)).astype(BF)


def reduce_outer(one, two):
    n = lax.axis_size("fsdp")
    bits = outer_bits()
    blocks, left = [], [sorted(bits, reverse=True), sorted(bits, reverse=True)]
    for b in (one, two):
        blocks.append(b.reshape((2,) * len(bits) + (b.shape[0] // (n // 2), b.shape[1])))
    first = None
    for pair in zip(bits, bits[::-1]):
        for i, bit in enumerate(pair):
            blocks[i] = halve(blocks[i], left[i].index(bit), bit)
            left[i].remove(bit)
        first = first or tuple(blocks)
    return blocks[0], blocks[1], first


def stack_heads(x):
    lane = lax.broadcasted_iota(jnp.int32, (BLOCK, x.shape[1]), 1)
    zero = jnp.zeros((BLOCK, x.shape[1]), x.dtype)
    heads = x.shape[1] // HD
    return jnp.concatenate(
        [
            jnp.where((lane >= h * HD) & (lane < (h + 1) * HD), x[j * BLOCK : (j + 1) * BLOCK], zero)
            for j in range(x.shape[0] // BLOCK)
            for h in range(heads)
        ],
        axis=0,
    )


def block_kind(seg, q_at, k_at):
    q_lo, q_hi = seg[q_at], seg[q_at + BLOCK - 1]
    k_lo, k_hi = seg[k_at], seg[k_at + BLOCK - 1]
    meet = (q_lo <= k_hi) & (k_lo <= q_hi)
    one = (q_lo == q_hi) & (k_lo == q_lo) & (k_hi == q_lo)
    return jnp.where(one, 2, jnp.where(meet, 1, 0))


def ids_down(ids_refs, col_s):
    rows = ids_refs[0].shape[1]

    @pl.when(pl.program_id(0) == 0)
    def _():
        for j, ids in enumerate(ids_refs):
            wide = jnp.broadcast_to(ids[...].astype(F32), (col_s.shape[1], rows))
            col_s[j * rows : (j + 1) * rows, :] = wide.T


def each_block(seg, where, slots, rows, visit):
    per = rows // BLOCK
    for j, slot in enumerate(slots):

        def step(i, _, j=j, slot=slot):
            kb, qb = i // per, lax.rem(i, per)
            at = pl.ds(pl.multiple_of(kb * BLOCK, BLOCK), BLOCK)
            kind = block_kind(seg, where[0] * rows + qb * BLOCK, where[1 + slot] * rows + kb * BLOCK)
            visit(j, at, kb, qb, kind)
            return 0

        lax.fori_loop(0, per * per, step, 0)


def lanes(index, size):
    return pl.ds(pl.multiple_of(index * size, size), size)


def forward_kernel(seg, where, *refs, slots):
    refs = list(refs)

    def take(count):
        taken, refs[:] = refs[:count], refs[count:]
        return taken

    x_refs = take(len(slots))
    ids_refs = take(len(slots))
    wq_ref, wk_ref, wv_ref, bq_ref, bv_ref, sq_ref = take(6)
    q_ref, k_ref, v_ref, o_ref, lse_ref, q_s, col_s, m_s, l_s, acc_s, ids_s = refs
    rows, width = q_ref.shape
    heads = width // HD
    wide = heads * BLOCK
    q_ref[...] = (nn(x_refs[0][...], wq_ref[...]) + bq_ref[...]).astype(BF)
    m_s[...] = jnp.full(m_s.shape, MASKED, F32)
    l_s[...] = jnp.zeros(l_s.shape, F32)
    acc_s[...] = jnp.zeros(acc_s.shape, F32)
    for j, x_ref in enumerate(x_refs):
        at = slice(j * rows, (j + 1) * rows)
        k_ref[at, :] = nn(x_ref[...], wk_ref[...]).astype(BF)
        v_ref[at, :] = (nn(x_ref[...], wv_ref[...]) + bv_ref[...]).astype(BF)
    q_s[...] = stack_heads(q_ref[...])
    ids_down(ids_refs, col_s)
    ids_s[...] = sq_ref[...].astype(F32)

    def block(at, qb, masked):
        stacked, part = lanes(qb, wide), lanes(qb, BLOCK)
        s = nt(k_ref[at, :], q_s[stacked, :])
        if masked:
            same = col_s[at, 0:1] == ids_s[:, part]
            s = jnp.where(jnp.concatenate([same] * heads, axis=1), s, MASKED)
        m_old = m_s[:, stacked]
        m_new = jnp.maximum(m_old, jnp.max(s, axis=0, keepdims=True))
        alpha = jnp.exp2((m_old - m_new) * SCORE)
        p = jnp.exp2((s - m_new) * SCORE)
        p_low = p.astype(BF)
        l_s[:, stacked] = alpha * l_s[:, stacked] + jnp.sum(p, axis=0, keepdims=True)
        m_s[:, stacked] = m_new
        v_t = v_ref[at, :].T
        for h in range(heads):
            hs, qs = slice(h * HD, (h + 1) * HD), slice(h * BLOCK, (h + 1) * BLOCK)
            acc_s[hs, part] = acc_s[hs, part] * alpha[:, qs] + nn(v_t[hs], p_low[:, qs])

    def visit(j, _, kb, qb, kind):
        at = pl.ds(pl.multiple_of(j * rows + kb * BLOCK, BLOCK), BLOCK)
        pl.when(kind == 1)(lambda: block(at, qb, True))
        pl.when(kind == 2)(lambda: block(at, qb, False))

    each_block(seg, where, slots, rows, visit)
    for j in range(rows // BLOCK):
        inverse = 1.0 / l_s[:, j * wide : (j + 1) * wide]
        spread_out = jnp.concatenate(
            [jnp.broadcast_to(inverse[:, h * BLOCK : (h + 1) * BLOCK], (HD, BLOCK)) for h in range(heads)], axis=0
        )
        at = slice(j * BLOCK, (j + 1) * BLOCK)
        o_ref[at, :] = (acc_s[:, at] * spread_out).T.astype(BF)
    lse_ref[0] = m_s[...] * SCORE + jnp.log2(l_s[...])


def attend_forward(xs, weights, biases, seg, where):
    rows, width = xs[0].shape
    slots = tuple(range(len(xs)))
    keys = rows * len(xs)
    groups, wide = width // GROUP, GROUP // HD * rows
    block_spec = pl.BlockSpec((rows, GROUP), lambda i, s, w: (0, i))
    keys_spec = pl.BlockSpec((keys, GROUP), lambda i, s, w: (0, i))
    w_spec = pl.BlockSpec((width, GROUP), lambda i, s, w: (0, i))
    b_spec = pl.BlockSpec((1, GROUP), lambda i, s, w: (0, i))
    row_spec = pl.BlockSpec((1, 1, wide), lambda i, s, w: (i, 0, 0))
    block_shape = jax.ShapeDtypeStruct((rows, width), BF)
    keys_shape = jax.ShapeDtypeStruct((keys, width), BF)

    def ids_spec(entry):
        return pl.BlockSpec((1, rows), lambda i, s, w: (0, w[entry]))

    in_specs = [pl.BlockSpec((rows, width), lambda i, s, w: (0, 0))] * len(xs)
    in_specs += [ids_spec(1 + s) for s in slots] + [w_spec] * 3 + [b_spec] * 2 + [ids_spec(0)]
    return pl.pallas_call(
        partial(forward_kernel, slots=slots),
        out_shape=(
            block_shape,
            keys_shape,
            keys_shape,
            block_shape,
            jax.ShapeDtypeStruct((groups, 1, wide), F32),
        ),
        grid_spec=pltpu.PrefetchScalarGridSpec(
            num_scalar_prefetch=2,
            grid=(groups,),
            in_specs=in_specs,
            out_specs=[block_spec, keys_spec, keys_spec, block_spec, row_spec],
            scratch_shapes=[
                pltpu.VMEM((wide, GROUP), BF),
                pltpu.VMEM((keys, 128), F32),
                pltpu.VMEM((1, wide), F32),
                pltpu.VMEM((1, wide), F32),
                pltpu.VMEM((GROUP, rows), F32),
                pltpu.VMEM((1, rows), F32),
            ],
        ),
        cost_estimate=pl.CostEstimate(flops=FEW, bytes_accessed=FEW, transcendentals=0),
        name="attend_forward",
    )(seg[0], where, *xs, *([seg] * len(slots)), *weights, *(b[None, :] for b in biases), seg)


def backward_kernel(seg, where, *refs, slots, first, others, block_rows):
    refs = list(refs)

    def take(count):
        taken, refs[:] = refs[:count], refs[count:]
        return taken

    last = others is not None
    q_ref, do_ref, o_ref, lse_ref, wk_ref, wv_ref, sq_ref = take(7)
    k_refs, v_refs, ids_refs = take(len(slots)), take(len(slots)), take(len(slots))
    if not first:
        (dq_in,) = take(1)
    if last:
        wq_ref, base_ref = take(2)
        dk_refs, dv_refs = take(len(others)), take(len(others))
        x_refs = take(len(slots) + sum(len(o) for o in others))
        dq_ref, sums_ref, dx_ref = take(3)
        grad_refs = take(2 if block_rows else 1)
        q_s, do_s, delta_s, col_s, ids_s, dx_s, dk_s, dv_s, dq_s, x_s, w_s = refs
    else:
        dk_s, dv_s, dq_s, dx_ref, q_s, do_s, delta_s, col_s, ids_s, dx_s = refs
    g = pl.program_id(0)
    ids_down(ids_refs, col_s)
    ids_s[...] = sq_ref[...].astype(F32)
    rows, width = q_ref.shape
    heads = width // HD
    wide = heads * BLOCK
    q_s[...] = stack_heads(q_ref[...])
    do_s[...] = stack_heads(do_ref[...])
    prod = (do_ref[...].astype(F32) * o_ref[...].astype(F32)).T
    for j in range(rows // BLOCK):
        for h in range(heads):
            piece = prod[h * HD : (h + 1) * HD, j * BLOCK : (j + 1) * BLOCK]
            delta_s[:, j * wide + h * BLOCK : j * wide + (h + 1) * BLOCK] = jnp.sum(piece, axis=0, keepdims=True)
    dq_s[...] = jnp.zeros_like(dq_s) if first else dq_in[...]

    def block(j, at, out_at, qb, masked):
        stacked, part = lanes(qb, wide), lanes(qb, BLOCK)
        k = k_refs[j][at, :]
        k_t = k.T
        s = nt(k, q_s[stacked, :]) * SCORE - lse_ref[0, :, stacked]
        if masked:
            same = col_s[out_at, 0:1] == ids_s[:, part]
            s = jnp.where(jnp.concatenate([same] * heads, axis=1), s, MASKED)
        p = jnp.exp2(s)
        dp = nt(v_refs[j][at, :], do_s[stacked, :])
        ds = (p * (dp - delta_s[:, stacked])).astype(BF)
        dv = nn(p.astype(BF), do_s[stacked, :])
        dk = nn(ds, q_s[stacked, :])
        for h in range(heads):
            hs = slice(h * HD, (h + 1) * HD)
            dq_s[hs, part] += nn(k_t[hs], ds[:, h * BLOCK : (h + 1) * BLOCK])
        return dk, dv

    def visit(j, at, kb, qb, kind):
        out_at = pl.ds(pl.multiple_of(j * rows + kb * BLOCK, BLOCK), BLOCK)

        @pl.when(qb == 0)
        def _():
            acc_k[...] = jnp.zeros(acc_k.shape, F32)
            acc_v[...] = jnp.zeros(acc_v.shape, F32)

        def add(masked):
            dk, dv = block(j, at, out_at, qb, masked)
            acc_k[...] += dk
            acc_v[...] += dv

        pl.when(kind == 1)(lambda: add(True))
        pl.when(kind == 2)(lambda: add(False))

        @pl.when(qb == rows // BLOCK - 1)
        def _():
            dk_s[out_at, :] = (acc_k[...] * HD**-0.5).astype(BF)
            dv_s[out_at, :] = acc_v[...].astype(BF)

    def scoped(acc_k_ref, acc_v_ref):
        nonlocal acc_k, acc_v
        acc_k, acc_v = acc_k_ref, acc_v_ref
        each_block(seg, where, slots, rows, visit)

    acc_k = acc_v = None
    pl.run_scoped(scoped, pltpu.VMEM((BLOCK, width), F32), pltpu.VMEM((BLOCK, width), F32))

    if last:
        dq_ref[...] = (dq_s[...] * HD**-0.5).T.astype(BF)
        sums_ref[0:1, :] = jnp.sum(dq_ref[...].astype(F32), axis=0, keepdims=True)
        sums_ref[1:2, :] = sum(
            jnp.sum(d[...].astype(F32), axis=0, keepdims=True) for d in (dv_s, *dv_refs)
        )
    for j in range(len(slots)):
        at = slice(j * rows, (j + 1) * rows)
        dx = nt(dk_s[at, :], wk_ref[...]) + nt(dv_s[at, :], wv_ref[...])
        if last and j == 0:
            dx = dx + nt(dq_ref[...], wq_ref[...])

        @pl.when(g == 0)
        def _(at=at, dx=dx, j=j):
            dx_s[at, :] = dx + base_ref[...] if last and j == 0 else dx

        @pl.when(g > 0)
        def _(at=at, dx=dx):
            dx_s[at, :] += dx

    @pl.when(g == pl.num_programs(0) - 1)
    def _():
        dx_ref[...] = dx_s[...].astype(dx_ref.dtype)

    if last:

        @pl.when(g == 0)
        def _():
            for j, x_ref in enumerate(x_refs):
                x_s[:, j * rows : (j + 1) * rows] = x_ref[...].T

        def over_keys(own, earlier):
            total, start = nn(x_s[:, : own.shape[0]], own[...]), own.shape[0]
            for d in earlier:
                total = total + nn(x_s[:, start : start + d.shape[0]], d[...])
                start += d.shape[0]
            return total

        grads = (
            lambda: nn(x_s[:, :rows], dq_ref[...]),
            lambda: over_keys(dk_s, dk_refs),
            lambda: over_keys(dv_s, dv_refs),
        )
        for m, grad in enumerate(grads):
            if block_rows:
                w_s[...] = grad()
                sent_ref, kept_ref = grad_refs
                core = where[5]
                for b in range(sent_ref.shape[0]):
                    far = pl.multiple_of((2 * b + 1 - core) * block_rows, block_rows)
                    near = pl.multiple_of((2 * b + core) * block_rows, block_rows)
                    sent_ref[b, m] = w_s[pl.ds(far, block_rows), :].astype(BF)
                    kept_ref[b, m] = w_s[pl.ds(near, block_rows), :]
            else:
                grad_refs[0][m] = grad()


def attend_backward(q, k, v, do, o, lse, slots, weights, seg, where, dq=None, tail=None, n=1):
    rows, width = q.shape
    keys = rows * len(slots)
    first, last = dq is None, tail is not None
    block_rows = width // n if (width // n) % 16 == 0 else 0
    groups, wide = width // GROUP, GROUP // HD * rows
    q_spec = pl.BlockSpec((rows, GROUP), lambda i, s, w: (0, i))
    w_spec = pl.BlockSpec((width, GROUP), lambda i, s, w: (0, i))
    all_spec = pl.BlockSpec((rows, width), lambda i, s, w: (0, 0))
    row_spec = pl.BlockSpec((1, 1, wide), lambda i, s, w: (i, 0, 0))
    acc_spec = pl.BlockSpec((GROUP, rows), lambda i, s, w: (i, 0))

    def ids_spec(entry):
        return pl.BlockSpec((1, rows), lambda i, s, w: (0, w[entry]))

    def slot_spec(slot):
        return pl.BlockSpec((rows, GROUP), lambda i, s, w: (slot, i))

    def keys_spec(array):
        return pl.BlockSpec((array.shape[0], GROUP), lambda i, s, w: (0, i))

    wq, wk, wv = weights
    count = len(slots)
    ins = [q, do, o, lse, wk, wv, seg] + [k] * count + [v] * count + [seg] * count
    in_specs = [q_spec, q_spec, q_spec, row_spec, w_spec, w_spec, ids_spec(0)]
    in_specs += [slot_spec(s) for s in slots] * 2 + [ids_spec(1 + s) for s in slots]
    if not first:
        ins.append(dq)
        in_specs.append(acc_spec)
    scratch = [pltpu.VMEM((wide, GROUP), BF), pltpu.VMEM((wide, GROUP), BF), pltpu.VMEM((1, wide), F32)]
    scratch += [pltpu.VMEM((keys, 128), F32), pltpu.VMEM((1, rows), F32), pltpu.VMEM((keys, width), F32)]
    others = None
    if last:
        base, earlier, xs, others = tail
        dks, dvs = zip(*earlier)
        ins += [wq, base, *dks, *dvs, *xs]
        in_specs += [w_spec, all_spec] + [keys_spec(d) for d in dks + dvs] + [all_spec] * len(xs)
        results = [
            (q_spec, jax.ShapeDtypeStruct((rows, width), BF)),
            (pl.BlockSpec((2, GROUP), lambda i, s, w: (0, i)), jax.ShapeDtypeStruct((2, width), F32)),
            (all_spec, jax.ShapeDtypeStruct((rows, width), F32)),
        ]
        if block_rows:
            shape = (n // 2, 3, block_rows)
            spec = pl.BlockSpec((*shape, GROUP), lambda i, s, w: (0, 0, 0, i))
            results += [
                (spec, jax.ShapeDtypeStruct((*shape, width), BF)),
                (spec, jax.ShapeDtypeStruct((*shape, width), F32)),
            ]
        else:
            spec = pl.BlockSpec((3, width, GROUP), lambda i, s, w: (0, 0, i))
            results.append((spec, jax.ShapeDtypeStruct((3, width, width), F32)))
        scratch += [pltpu.VMEM((keys, GROUP), BF), pltpu.VMEM((keys, GROUP), BF), pltpu.VMEM((GROUP, rows), F32)]
        scratch += [pltpu.VMEM((width, rows * len(xs)), BF), pltpu.VMEM((width, GROUP), F32)]
    else:
        keys_shape = jax.ShapeDtypeStruct((keys, width), BF)
        results = [
            (keys_spec(keys_shape), keys_shape),
            (keys_spec(keys_shape), keys_shape),
            (acc_spec, jax.ShapeDtypeStruct((width, rows), F32)),
            (pl.BlockSpec((keys, width), lambda i, s, w: (0, 0)), keys_shape),
        ]
    return pl.pallas_call(
        partial(backward_kernel, slots=slots, first=first, others=others, block_rows=block_rows),
        out_shape=tuple(r[1] for r in results),
        grid_spec=pltpu.PrefetchScalarGridSpec(
            num_scalar_prefetch=2,
            grid=(groups,),
            in_specs=in_specs,
            out_specs=[r[0] for r in results],
            scratch_shapes=scratch,
        ),
        compiler_params=pltpu.CompilerParams(vmem_limit_bytes=63 << 20),
        cost_estimate=pl.CostEstimate(flops=FEW, bytes_accessed=FEW, transcendentals=0),
        name="attend_backward",
    )(seg[0], where, *ins)


def norm_parts(rows_in):
    mean = jnp.mean(rows_in, axis=-1, keepdims=True)
    centred = rows_in - mean
    spread = jnp.mean(centred * centred, axis=-1, keepdims=True)
    r = lax.rsqrt(spread + EPSILON)
    return centred * r, r


def norm_back(g_y, n, r, gain):
    e = g_y * gain
    return r * (e - jnp.mean(e, axis=-1, keepdims=True) - n * jnp.mean(e * n, axis=-1, keepdims=True))


def gelu_parts(u):
    c = 0.7978845608028654
    square = u * u
    th = jnp.tanh(c * u * (1.0 + 0.044715 * square))
    half = 0.5 * (1.0 + th)
    slope = half + 0.5 * u * (1.0 - th * th) * (c + 3 * 0.044715 * c * square)
    return u * half, slope


def down_rows(x):
    return jnp.sum(x, axis=0, keepdims=True)


def middle_kernel(known, *refs, count):
    w_refs, refs = (refs[:count], refs[count : 2 * count]), refs[2 * count :]
    ctx_ref, x_ref, grad_ref, mix_ref, vec_ref, bias_ref = refs[:6]
    out_ref, first_ref, gctx_ref, lefts_ref, rights_ref, sums_ref, bias_grad_ref = refs[6:13]
    w_s, slope_s, n1_s, r1_s, acc_s, sems = refs[13:]
    parts, per, r, units = w_refs[0][0].shape
    blocks = per * count
    rows, width = x_ref.shape

    def copy(which, t, j):
        core, place = j // per, j % per
        block = known[1] ^ (place * count + core) if blocks > 1 else 0
        at = pl.ds(pl.multiple_of(block * r, r), r)
        return pltpu.make_async_copy(
            w_refs[which][core].at[t, place], w_s.at[which, t, at, :], sems.at[which, t, j]
        )

    for which in range(2):
        for t in range(parts):
            for j in range(blocks):
                copy(which, t, j).start()

    def cols(t):
        return pl.ds(pl.multiple_of(t * units, units), units)

    first_sum = x_ref[...].astype(F32) + nt(ctx_ref[...], mix_ref[...]) + vec_ref[0:1, :]
    n1, r1 = norm_parts(first_sum)
    n1_s[...] = n1
    r1_s[...] = jnp.broadcast_to(r1, r1_s.shape)
    acc_s[...] = n1 * vec_ref[1:2, :] + vec_ref[2:3, :]
    lefts_ref[1] = acc_s[...].astype(BF)

    for t in range(parts):
        for j in range(blocks):
            copy(0, t, j).wait()
    for t in range(parts):
        for j in range(blocks):
            copy(1, t, j).wait()

    def up(t, _):
        pre = nn(lefts_ref[1], w_s[0, t]) + bias_ref[pl.ds(t, 1), :]
        act, slope = gelu_parts(pre)
        slope_s[t] = slope
        low = act.astype(BF)
        rights_ref[:, cols(t)] = low
        acc_s[...] += nt(low, w_s[1, t])
        return 0

    lax.fori_loop(0, parts, up, 0)
    n2, r2 = norm_parts(acc_s[...] + vec_ref[3:4, :])
    out_ref[...] = (n2 * vec_ref[4:5, :] + vec_ref[5:6, :]).astype(BF)
    row = lax.broadcasted_iota(jnp.int32, (rows, width), 0)
    g_out = jnp.where(row < known[0], grad_ref[...].astype(F32), 0.0)
    g_second = norm_back(g_out, n2, r2, vec_ref[4:5, :])
    sums_ref[3:4, :] = down_rows(g_second)
    sums_ref[4:5, :] = down_rows(g_out * n2)
    sums_ref[5:6, :] = down_rows(g_out)
    lefts_ref[0] = g_second.astype(BF)
    acc_s[...] = g_second

    def back(t, _):
        g_pre = (nn(lefts_ref[0], w_s[1, t]) * slope_s[t]).astype(BF)
        rights_ref[:, cols(parts + t)] = g_pre
        bias_grad_ref[pl.ds(t, 1), :] = down_rows(g_pre.astype(F32))
        acc_s[...] += nt(g_pre, w_s[0, t])
        return 0

    lax.fori_loop(0, parts, back, 0)
    g_normed = acc_s[...]
    n1 = n1_s[...]
    g_first = norm_back(g_normed, n1, r1_s[:, 0:1], vec_ref[1:2, :])
    sums_ref[0:1, :] = down_rows(g_first)
    sums_ref[1:2, :] = down_rows(g_normed * n1)
    sums_ref[2:3, :] = down_rows(g_normed)
    sums_ref[6:8, :] = jnp.zeros((2, width), F32)
    first_ref[...] = g_first
    low = g_first.astype(BF)
    lefts_ref[2] = low
    gctx_ref[...] = nn(low, mix_ref[...]).astype(BF)
    rights_ref[:, 2 * parts * units :] = ctx_ref[...]


def middle(known, ups, downs, ctx, x, grad, mix, vectors, bias):
    rows, width = x.shape
    parts, per, r, units = ups[0].shape
    count = len(ups)
    blocks = per * count
    vmem = pl.BlockSpec(memory_space=pltpu.VMEM)
    shapes = [
        ((rows, width), BF),
        ((rows, width), F32),
        ((rows, width), BF),
        ((3, rows, width), BF),
        ((rows, 2 * parts * units + width), BF),
        ((8, width), F32),
        ((parts, units), F32),
    ]
    return pl.pallas_call(
        partial(middle_kernel, count=count),
        out_shape=tuple(jax.ShapeDtypeStruct(*s) for s in shapes),
        in_specs=[pl.BlockSpec(memory_space=pltpu.SMEM)] + [pl.BlockSpec(memory_space=pl.ANY)] * (2 * count) + [vmem] * 6,
        out_specs=[vmem] * len(shapes),
        scratch_shapes=[
            pltpu.VMEM((2, parts, blocks * r, units), BF),
            pltpu.VMEM((parts, rows, units), F32),
            pltpu.VMEM((rows, width), F32),
            pltpu.VMEM((rows, 128), F32),
            pltpu.VMEM((rows, width), F32),
            pltpu.SemaphoreType.DMA((2, parts, blocks)),
        ],
        compiler_params=pltpu.CompilerParams(vmem_limit_bytes=63 << 20),
        cost_estimate=pl.CostEstimate(flops=FEW, bytes_accessed=FEW, transcendentals=0),
        name="middle",
    )(known, *ups, *downs, ctx, x, grad, mix, vectors, bias)


def ffn_grad_kernel(place, left_ref, right_ref, *refs, core):
    out_ref, left_s, chosen_s = refs[-3:]

    @pl.when(pl.program_id(0) % 4 == 0)
    def _():
        left_s[...] = left_ref[0].T
        if core is not None:
            size = left_s.shape[0] // core[1]
            for q in range(core[1] // 2):
                block = place[0] ^ (2 * q + core[0])
                chosen_s[q * size : (q + 1) * size, :] = left_s[pl.ds(pl.multiple_of(block * size, size), size), :]

    total = nn((left_s if core is None else chosen_s)[...], right_ref[...])
    if len(refs) == 4:
        total = total + refs[0][...].astype(F32)
    out_ref[...] = total.astype(BF)


def ffn_grads(place, lefts, rights, core=None, got=None):
    _, rows, width = lefts.shape
    units = rights.shape[1] // 9
    out_rows = width if core is None else width // 2
    out_spec = pl.BlockSpec((out_rows, units), lambda i, p: (0, i))
    return pl.pallas_call(
        partial(ffn_grad_kernel, core=core),
        out_shape=jax.ShapeDtypeStruct((out_rows, rights.shape[1]), BF),
        grid_spec=pltpu.PrefetchScalarGridSpec(
            num_scalar_prefetch=1,
            grid=(9,),
            in_specs=[
                pl.BlockSpec((1, rows, width), lambda i, p: (i // 4, 0, 0)),
                pl.BlockSpec((rows, units), lambda i, p: (0, i)),
            ]
            + ([] if got is None else [out_spec]),
            out_specs=out_spec,
            scratch_shapes=[pltpu.VMEM((width, rows), BF), pltpu.VMEM((width // 2, rows), BF)],
        ),
        cost_estimate=pl.CostEstimate(flops=FEW, bytes_accessed=FEW, transcendentals=0),
        name="ffn_grads",
    )(place, lefts, rights, *(() if got is None else (got,)))


def on_device(
    tokens,
    segments,
    query_weight,
    query_bias,
    key_weight,
    value_weight,
    value_bias,
    mix_weight,
    mix_bias,
    norm_gain,
    norm_shift,
    up_weight,
    up_bias,
    down_weight,
    down_bias,
    final_gain,
    final_shift,
    out_grad,
):
    t = lax.axis_index("tensor")
    f = lax.axis_index("fsdp")
    n = lax.axis_size("fsdp")
    rows, width = tokens.shape
    r, units = up_weight.shape
    cols = query_weight.shape[1]
    owner = slot_owner(t)

    shard = jnp.concatenate([query_weight, key_weight, value_weight, mix_weight.T], axis=1)
    w_a, w_below, w_above = line_first(shard)
    f_own = jnp.stack([up_weight, down_weight.T])
    f_a, f_below, f_above = line_first(f_own)
    w_c = line_second(w_below, w_above)
    f_c = line_second(f_below, f_above)
    x_a, x_below, x_above = line_first(after(tokens, f_a))
    w_slots = (shard, w_a, w_c, line_third(w_c, w_below))
    f_slots = (f_own, f_a, f_c, line_third(f_c, f_below))
    line = [jnp.concatenate([w[:, m * cols : (m + 1) * cols] for w in w_slots], axis=1) for m in range(4)]
    seen = []

    def attn_gate(step, others):
        if step == 0:
            others = after(others, x_a)
            seen.append(others)
        return others

    attn_near = jnp.concatenate(
        gather_outer([jnp.stack(line[:2]), jnp.stack(line[2:])], True, attn_gate)
    )
    attn_w = in_place(attn_near, lax.ppermute(attn_near, "fsdp", partner(1)))
    weights = tuple(attn_w[m] for m in range(3))
    wm_t = attn_w[3]
    x_c = line_second(x_below, x_above, attn_near)

    def ffn_gate(step, others):
        return after(others, x_c) if step == 0 else others

    f_line = after([jnp.stack([w[i] for w in f_slots]) for i in range(2)], *seen[0])
    f_near = gather_outer(f_line, False, ffn_gate)
    f_far = [lax.ppermute(w, "fsdp", partner(1)) for w in f_near]
    ups, downs = zip(f_near, f_far)
    if r % 16:
        ups, downs = (
            (from_relative(w, o).reshape(4, 1, width, units),) for w, o in zip(f_near, f_far)
        )

    def by_slot(vector):
        parts = vector.reshape(4, -1)
        return jnp.concatenate([lax.dynamic_slice_in_dim(parts, owner[i], 1, axis=0)[0] for i in range(4)])

    seg = jnp.where(segments == 0, 9, segments)
    where = jnp.concatenate([t[None], owner, (f & 1)[None]]).astype(jnp.int32)
    xs = (tokens, x_a, x_c, line_third(x_c, x_below))
    xs = after(xs, *f_near)
    q, k, v, ctx, lse = attend_forward(xs, weights, (by_slot(query_bias), by_slot(value_bias)), seg, where)

    own_ids = lax.dynamic_slice_in_dim(seg[0], t * rows, rows)
    known = jnp.stack([jnp.sum((own_ids < 9).astype(jnp.int32)), f.astype(jnp.int32)])
    vectors = jnp.stack([mix_bias, norm_gain, norm_shift, down_bias, final_gain, final_shift])
    layer_out, g_first, g_ctx, lefts, rights, sums, up_sums = middle(
        known, ups, downs, ctx, tokens, out_grad, wm_t, vectors, by_slot(up_bias).reshape(4, units)
    )
    place = f.astype(jnp.int32)[None]
    if r % 16:
        full = ffn_grads(place, lefts, rights).reshape(n, r, -1)
        kept, sent = (
            jnp.concatenate([lax.dynamic_slice_in_dim(full, f ^ (2 * q + c), 1)[0] for q in range(n // 2)])
            for c in range(2)
        )
    else:
        sent = ffn_grads(place, lefts, rights, (1, n))
    got = lax.ppermute(sent, "fsdp", partner(1))
    g_ctx = after(g_ctx, sent)

    args = (q, k, v, g_ctx, ctx, lse)
    dk_b, dv_b, dq, dx_b = attend_backward(*args, (3,), weights, seg, where)
    r1 = lax.ppermute(dx_b, "tensor", [(0, 1), (3, 2)])
    lefts = after(lefts, dx_b)
    if r % 16:
        near = (kept.astype(F32) + got.astype(F32)).astype(BF)
    else:
        near = ffn_grads(place, lefts, rights, (0, n), got)
    d_one, d_two, d_first = reduce_outer(near[:, : 4 * units], near[:, 4 * units :])
    dk_n, dv_n, dq, dx_n = attend_backward(*args, (2, 1), weights, seg, where, after(dq, near))
    dx_c, dx_a = dx_n[:rows], dx_n[rows:]
    middle_x = (dx_c.astype(F32) + r1.astype(F32)).astype(BF)
    rx = lax.ppermute(middle_x, "tensor", [(0, 1), (3, 2)]).astype(F32)
    ry = lax.ppermute(middle_x, "tensor", [(1, 2), (2, 1)]).astype(F32)
    tail = (g_first, ((dk_n, dv_n), (dk_b, dv_b)), (xs[0], xs[2], xs[1], xs[3]), ((2, 1), (3,)))
    out = attend_backward(*args, (0,), weights, seg, where, after(dq, middle_x, *d_first), tail, n)
    dq, qv_sums, dx_own = out[:3]
    if len(out) == 5:
        sent, kept = out[3:]
    else:
        split = out[3].reshape(3, n // 2, 2, r, width)
        sent, kept = (
            lax.dynamic_index_in_dim(split, c, 2, keepdims=False).transpose(1, 0, 2, 3) for c in (1 - (f & 1), f & 1)
        )
        sent = sent.astype(BF)

    early = jnp.stack(
        [
            jnp.concatenate(
                [
                    d_one[:, i * units : (i + 1) * units],
                    d_two[:, i * units : (i + 1) * units],
                    d_two[:, 4 * units + i * cols : 4 * units + (i + 1) * cols],
                ],
                axis=1,
            )
            for i in range(4)
        ]
    )
    early = spread(in_line_order(early, t))

    got = lax.ppermute(sent, "fsdp", partner(1))
    up_x = (dx_a.astype(F32) + jnp.where(t == 1, rx, ry)).astype(BF)
    down_x = jnp.where(t == 3, dx_a.astype(F32), dx_b.astype(F32) + jnp.where(t == 1, ry, rx)).astype(BF)
    from_below = lax.ppermute(up_x, "tensor", [(0, 1), (1, 2), (2, 3)])
    from_above = lax.ppermute(down_x, "tensor", [(1, 0), (2, 1), (3, 2)])
    near = (kept + got.astype(F32)).astype(BF)
    same_core = [list(range(c, n, 2)) for c in range(2)]
    arrived = lax.all_to_all(near, "fsdp", split_axis=0, concat_axis=0, axis_index_groups=same_core, tiled=True)

    qv = in_line_order(qv_sums.reshape(2, 4, cols).transpose(1, 0, 2), t).transpose(1, 0, 2)
    small = jnp.concatenate([sums[:6].reshape(-1), in_line_order(up_sums, t).reshape(-1), qv.reshape(-1)])
    small = sum_everywhere(after(small, near))
    sums = small[: 6 * width].reshape(6, width)
    up_sums = small[6 * width : 6 * width + 4 * units]
    qv = small[6 * width + 4 * units :].reshape(2, width)

    arrived = after(arrived, small, from_below, from_above)
    late = jnp.sum(arrived.astype(F32), axis=0).astype(BF)
    late = jnp.stack([late[:, :, i * cols : (i + 1) * cols] for i in range(4)])
    late = spread(in_line_order(late, t))
    tokens_grad = dx_own + from_below.astype(F32) + from_above.astype(F32)

    return (
        layer_out,
        tokens_grad,
        late[0],
        qv[0],
        late[1],
        late[2],
        qv[1],
        early[:, 2 * units :].T,
        sums[0],
        sums[1],
        sums[2],
        early[:, units : 2 * units],
        up_sums,
        early[:, :units].T,
        sums[3],
        sums[4],
        sums[5],
    )


def solution(mesh):
    both, rows_f, square, flipped = (
        P(("fsdp", "tensor"), None),
        P("fsdp", None),
        P("fsdp", "tensor"),
        P("tensor", "fsdp"),
    )
    return jax.shard_map(
        on_device,
        mesh=mesh,
        in_specs=(
            both, rows_f, square, P(), square, square, P(), flipped, P(), P(), P(),
            square, P(), flipped, P(), P(), P(), both,
        ),
        out_specs=(
            both, both, square, P(), square, square, P(), flipped, P(), P(), P(),
            square, P(), flipped, P(), P(), P(),
        ),
        check_vma=False,
    )
```

```python
from functools import partial

import jax
import jax.numpy as jnp
from jax import lax
from jax.experimental import pallas as pl
from jax.experimental.pallas import tpu as pltpu
from jax.sharding import PartitionSpec as P

HD = 64
GROUP = 256
BLOCK = 256
EPSILON = 1e-05
MASKED = -1e30
LOG2E = 1.4426950408889634
SCORE = HD**-0.5 * LOG2E
EXTRA = 16
FEW = 1000
BF = jnp.bfloat16
F32 = jnp.float32


def after(value, *others):
    return lax.optimization_barrier((value,) + others)[0] if others else value


def nt(a, b):
    return lax.dot_general(a, b, (((1,), (1,)), ((), ())), preferred_element_type=F32)


def nn(a, b):
    return lax.dot_general(a, b, (((1,), (0,)), ((), ())), preferred_element_type=F32)


def line_first(own):
    below = lax.ppermute(own, "tensor", [(0, 1), (1, 2), (2, 3)])
    above = lax.ppermute(own, "tensor", [(1, 0), (2, 1), (3, 2)])
    return jnp.where(lax.axis_index("tensor") < 3, above, below), below, above


def line_second(below, above, *gate):
    below2 = lax.ppermute(below, "tensor", [(1, 2), (2, 3)])
    above2 = lax.ppermute(above, "tensor", [(2, 1), (1, 0)])
    below2, above2 = after((below2, above2), *gate)
    return jnp.where(lax.axis_index("tensor") < 2, above2, below2)


def line_third(slot_c, below, *gate):
    far = after(lax.ppermute(slot_c, "tensor", [(1, 0), (2, 3)]), *gate)
    t = lax.axis_index("tensor")
    return jnp.where((t == 0) | (t == 3), far, below)


def slot_owner(t):
    return jnp.stack([t, jnp.where(t < 3, t + 1, 2), lax.rem(t + 2, 4), jnp.where(t == 3, 0, lax.rem(t + 3, 4))])


def owner_slot(t):
    owner = slot_owner(t)
    places = jnp.arange(4)
    return [jnp.sum(jnp.where(owner == j, places, 0)) for j in range(4)]


def in_line_order(slots, t):
    return jnp.concatenate([lax.dynamic_slice_in_dim(slots, s, 1, axis=0) for s in owner_slot(t)])


def spread(slots, t):
    owner = slot_owner(t)
    arrived = []
    for shift in (1, 3, 2):
        goal = lax.rem(t + shift, 4)
        slot = sum(jnp.where(owner[j] == goal, j, 0) for j in range(4))
        block = lax.dynamic_index_in_dim(slots, slot, 0, keepdims=False)
        arrived.append(lax.ppermute(block, "tensor", [(i, (i + shift) % 4) for i in range(4)]))
    return arrived


def total(own, arrived):
    return own.astype(F32) + sum(a.astype(F32) for a in arrived)


def partner(bit):
    n = lax.axis_size("fsdp")
    return [(i, i ^ bit) for i in range(n)]


def outer_bits():
    n = lax.axis_size("fsdp")
    return [1 << k for k in range(1, n.bit_length() - 1)]


def assembled(pieces):
    n = len(pieces)
    f = lax.axis_index("fsdp")
    stacked = jnp.stack(pieces).reshape(2, n // 2, *pieces[0].shape)
    blocks = []
    for a in range(n):
        rel = f ^ a
        block = lax.dynamic_slice_in_dim(stacked, rel & 1, 1, axis=0)
        blocks.append(lax.dynamic_slice_in_dim(block, rel >> 1, 1, axis=1)[0, 0])
    return jnp.concatenate(blocks)


def outer_axes(block):
    n = lax.axis_size("fsdp")
    bits = outer_bits()
    return block.reshape((2,) * len(bits) + (block.shape[0] // (n // 2), block.shape[1])), sorted(bits, reverse=True)


def start_halving(blocks, lefts, pair):
    kept, arrived, rest = [], [], []
    for block, left, bit in zip(blocks, lefts, pair):
        axis = left.index(bit)
        kept.append(lax.index_in_dim(block, 0, axis, keepdims=False))
        arrived.append(lax.ppermute(lax.index_in_dim(block, 1, axis, keepdims=False), "fsdp", partner(bit)))
        rest.append([b for b in left if b != bit])
    return kept, arrived, rest


def add_low(kept, arrived):
    return [(a.astype(F32) + b.astype(F32)).astype(BF) for a, b in zip(kept, arrived)]


def stack_heads(x):
    lane = lax.broadcasted_iota(jnp.int32, (BLOCK, x.shape[1]), 1)
    zero = jnp.zeros((BLOCK, x.shape[1]), x.dtype)
    heads = x.shape[1] // HD
    return jnp.concatenate(
        [
            jnp.where((lane >= h * HD) & (lane < (h + 1) * HD), x[j * BLOCK : (j + 1) * BLOCK], zero)
            for j in range(x.shape[0] // BLOCK)
            for h in range(heads)
        ],
        axis=0,
    )


def block_kind(seg, q_at, k_at):
    q_lo, q_hi = seg[q_at], seg[q_at + BLOCK - 1]
    k_lo, k_hi = seg[k_at], seg[k_at + BLOCK - 1]
    meet = (q_lo <= k_hi) & (k_lo <= q_hi)
    one = (q_lo == q_hi) & (k_lo == q_lo) & (k_hi == q_lo)
    return jnp.where(one, 2, jnp.where(meet, 1, 0))


def ids_down(ids_refs, col_s):
    rows = ids_refs[0].shape[1]

    @pl.when(pl.program_id(0) == 0)
    def _():
        for j, ids in enumerate(ids_refs):
            wide = jnp.broadcast_to(ids[...].astype(F32), (col_s.shape[1], rows))
            col_s[j * rows : (j + 1) * rows, :] = wide.T


def each_block(seg, where, slots, rows, visit):
    per = rows // BLOCK
    for j, slot in enumerate(slots):

        def step(i, _, j=j, slot=slot):
            kb, qb = i // per, lax.rem(i, per)
            at = pl.ds(pl.multiple_of(kb * BLOCK, BLOCK), BLOCK)
            kind = block_kind(seg, where[0] * rows + qb * BLOCK, where[1 + slot] * rows + kb * BLOCK)
            visit(j, at, kb, qb, kind)
            return 0

        lax.fori_loop(0, per * per, step, 0)


def piece_copy(pieces, j, f, column, width, target, sem):
    r = pieces[0].shape[0]
    place = 0
    if len(pieces) > 1:
        core, outer = j // (len(pieces) // 2), j % (len(pieces) // 2)
        place = f ^ (2 * outer + core)
    rows = pl.ds(pl.multiple_of(place * r, r), r)
    return pltpu.make_async_copy(
        pieces[j].at[:, column * width : (column + 1) * width], target.at[rows, :], sem
    )


def lanes(index, size):
    return pl.ds(pl.multiple_of(index * size, size), size)


def forward_kernel(seg, where, *refs, slots, count):
    refs = list(refs)

    def take(count):
        taken, refs[:] = refs[:count], refs[count:]
        return taken

    x_refs = take(len(slots))
    ids_refs = take(len(slots))
    pieces = (take(count), take(count))
    bq_ref, bv_ref, sq_ref = take(3)
    q_ref, k_ref, v_ref, o_ref, lse_ref, w_ref, q_s, col_s, m_s, l_s, acc_s, ids_s, w_s, sems = refs

    @pl.when(pl.program_id(0) == 0)
    def _():
        copies = [
            piece_copy(pieces[m // 2], j, where[6], m % 2, w_s.shape[2], w_s.at[m], sems.at[m, j])
            for m in range(3)
            for j in range(count)
        ]
        for copy in copies:
            copy.start()
        for copy in copies:
            copy.wait()

    w_ref[...] = w_s[:, :, lanes(pl.program_id(0), q_ref.shape[1])]
    wq_ref, wk_ref, wv_ref = (w_ref.at[m] for m in range(3))
    rows, width = q_ref.shape
    heads = width // HD
    wide = heads * BLOCK
    q_ref[...] = (nn(x_refs[0][...], wq_ref[...]) + bq_ref[...]).astype(BF)
    m_s[...] = jnp.full(m_s.shape, MASKED, F32)
    l_s[...] = jnp.zeros(l_s.shape, F32)
    acc_s[...] = jnp.zeros(acc_s.shape, F32)
    for j, x_ref in enumerate(x_refs):
        at = slice(j * rows, (j + 1) * rows)
        k_ref[at, :] = nn(x_ref[...], wk_ref[...]).astype(BF)
        v_ref[at, :] = (nn(x_ref[...], wv_ref[...]) + bv_ref[...]).astype(BF)
    q_s[...] = stack_heads(q_ref[...])
    ids_down(ids_refs, col_s)
    ids_s[...] = sq_ref[...].astype(F32)

    def block(at, qb, masked):
        stacked, part = lanes(qb, wide), lanes(qb, BLOCK)
        s = nt(k_ref[at, :], q_s[stacked, :])
        if masked:
            same = col_s[at, 0:1] == ids_s[:, part]
            s = jnp.where(jnp.concatenate([same] * heads, axis=1), s, MASKED)
        m_old = m_s[:, stacked]
        m_new = jnp.maximum(m_old, jnp.max(s, axis=0, keepdims=True))
        alpha = jnp.exp2((m_old - m_new) * SCORE)
        p = jnp.exp2((s - m_new) * SCORE)
        p_low = p.astype(BF)
        l_s[:, stacked] = alpha * l_s[:, stacked] + jnp.sum(p, axis=0, keepdims=True)
        m_s[:, stacked] = m_new
        v_t = v_ref[at, :].T
        for h in range(heads):
            hs, qs = slice(h * HD, (h + 1) * HD), slice(h * BLOCK, (h + 1) * BLOCK)
            acc_s[hs, part] = acc_s[hs, part] * alpha[:, qs] + nn(v_t[hs], p_low[:, qs])

    def visit(j, _, kb, qb, kind):
        at = pl.ds(pl.multiple_of(j * rows + kb * BLOCK, BLOCK), BLOCK)
        pl.when(kind == 1)(lambda: block(at, qb, True))
        pl.when(kind == 2)(lambda: block(at, qb, False))

    each_block(seg, where, slots, rows, visit)
    for j in range(rows // BLOCK):
        inverse = 1.0 / l_s[:, j * wide : (j + 1) * wide]
        spread_out = jnp.concatenate(
            [jnp.broadcast_to(inverse[:, h * BLOCK : (h + 1) * BLOCK], (HD, BLOCK)) for h in range(heads)], axis=0
        )
        at = slice(j * BLOCK, (j + 1) * BLOCK)
        o_ref[at, :] = (acc_s[:, at] * spread_out).T.astype(BF)
    lse_ref[0] = m_s[...] * SCORE + jnp.log2(l_s[...])


def attend_forward(xs, pieces, biases, seg, where):
    rows, width = xs[0].shape
    slots = tuple(range(len(xs)))
    keys = rows * len(xs)
    count = len(pieces[0])
    groups, wide = width // GROUP, GROUP // HD * rows
    block_spec = pl.BlockSpec((rows, GROUP), lambda i, s, w: (0, i))
    keys_spec = pl.BlockSpec((keys, GROUP), lambda i, s, w: (0, i))
    b_spec = pl.BlockSpec((1, GROUP), lambda i, s, w: (0, i))
    row_spec = pl.BlockSpec((1, 1, wide), lambda i, s, w: (i, 0, 0))
    block_shape = jax.ShapeDtypeStruct((rows, width), BF)
    keys_shape = jax.ShapeDtypeStruct((keys, width), BF)

    def ids_spec(entry):
        return pl.BlockSpec((1, rows), lambda i, s, w: (0, w[entry]))

    in_specs = [pl.BlockSpec((rows, width), lambda i, s, w: (0, 0))] * len(xs)
    in_specs += [ids_spec(1 + s) for s in slots] + [pl.BlockSpec(memory_space=pl.ANY)] * (2 * count) + [b_spec] * 2 + [ids_spec(0)]
    return pl.pallas_call(
        partial(forward_kernel, slots=slots, count=count),
        out_shape=(
            block_shape,
            keys_shape,
            keys_shape,
            block_shape,
            jax.ShapeDtypeStruct((groups, 1, wide), F32),
            jax.ShapeDtypeStruct((3, width, width), BF),
        ),
        grid_spec=pltpu.PrefetchScalarGridSpec(
            num_scalar_prefetch=2,
            grid=(groups,),
            in_specs=in_specs,
            out_specs=[
                block_spec, keys_spec, keys_spec, block_spec, row_spec,
                pl.BlockSpec((3, width, GROUP), lambda i, s, w: (0, 0, i)),
            ],
            scratch_shapes=[
                pltpu.VMEM((wide, GROUP), BF),
                pltpu.VMEM((keys, 128), F32),
                pltpu.VMEM((1, wide), F32),
                pltpu.VMEM((1, wide), F32),
                pltpu.VMEM((GROUP, rows), F32),
                pltpu.VMEM((1, rows), F32),
                pltpu.VMEM((3, width, width), BF),
                pltpu.SemaphoreType.DMA((3, count)),
            ],
        ),
        cost_estimate=pl.CostEstimate(flops=FEW, bytes_accessed=FEW, transcendentals=0),
        name="attend_forward",
    )(seg[0], where, *xs, *([seg] * len(slots)), *pieces[0], *pieces[1], *(b[None, :] for b in biases), seg)


def backward_kernel(seg, where, *refs, slots, first, last):
    refs = list(refs)

    def take(count):
        taken, refs[:] = refs[:count], refs[count:]
        return taken

    q_ref, do_ref, o_ref, lse_ref, wk_ref, wv_ref, sq_ref = take(7)
    k_refs, v_refs, ids_refs = take(len(slots)), take(len(slots)), take(len(slots))
    if not first:
        (dq_in,) = take(1)
    if last:
        wq_ref, base_ref = take(2)
        dk_s, dv_s, dq_ref, dx_ref, q_s, do_s, delta_s, col_s, ids_s, dx_s, dq_s = refs
    else:
        dk_s, dv_s, dq_s, dx_ref, q_s, do_s, delta_s, col_s, ids_s, dx_s = refs
    g = pl.program_id(0)
    ids_down(ids_refs, col_s)
    ids_s[...] = sq_ref[...].astype(F32)
    rows, width = q_ref.shape
    heads = width // HD
    wide = heads * BLOCK
    q_s[...] = stack_heads(q_ref[...])
    do_s[...] = stack_heads(do_ref[...])
    prod = (do_ref[...].astype(F32) * o_ref[...].astype(F32)).T
    for j in range(rows // BLOCK):
        for h in range(heads):
            piece = prod[h * HD : (h + 1) * HD, j * BLOCK : (j + 1) * BLOCK]
            delta_s[:, j * wide + h * BLOCK : j * wide + (h + 1) * BLOCK] = jnp.sum(piece, axis=0, keepdims=True)
    dq_s[...] = jnp.zeros_like(dq_s) if first else dq_in[...]

    def block(j, at, out_at, qb, masked):
        stacked, part = lanes(qb, wide), lanes(qb, BLOCK)
        k = k_refs[j][at, :]
        k_t = k.T
        s = nt(k, q_s[stacked, :]) * SCORE - lse_ref[0, :, stacked]
        if masked:
            same = col_s[out_at, 0:1] == ids_s[:, part]
            s = jnp.where(jnp.concatenate([same] * heads, axis=1), s, MASKED)
        p = jnp.exp2(s)
        dp = nt(v_refs[j][at, :], do_s[stacked, :])
        ds = (p * (dp - delta_s[:, stacked])).astype(BF)
        dv = nn(p.astype(BF), do_s[stacked, :])
        dk = nn(ds, q_s[stacked, :])
        for h in range(heads):
            hs = slice(h * HD, (h + 1) * HD)
            dq_s[hs, part] += nn(k_t[hs], ds[:, h * BLOCK : (h + 1) * BLOCK])
        return dk, dv

    def visit(j, at, kb, qb, kind):
        out_at = pl.ds(pl.multiple_of(j * rows + kb * BLOCK, BLOCK), BLOCK)

        @pl.when(qb == 0)
        def _():
            acc_k[...] = jnp.zeros(acc_k.shape, F32)
            acc_v[...] = jnp.zeros(acc_v.shape, F32)

        def add(masked):
            dk, dv = block(j, at, out_at, qb, masked)
            acc_k[...] += dk
            acc_v[...] += dv

        pl.when(kind == 1)(lambda: add(True))
        pl.when(kind == 2)(lambda: add(False))

        @pl.when(qb == rows // BLOCK - 1)
        def _():
            dk_s[out_at, :] = (acc_k[...] * HD**-0.5).astype(BF)
            dv_s[out_at, :] = acc_v[...].astype(BF)

    def scoped(acc_k_ref, acc_v_ref):
        nonlocal acc_k, acc_v
        acc_k, acc_v = acc_k_ref, acc_v_ref
        each_block(seg, where, slots, rows, visit)

    acc_k = acc_v = None
    pl.run_scoped(scoped, pltpu.VMEM((BLOCK, width), F32), pltpu.VMEM((BLOCK, width), F32))

    if last:
        dq_ref[...] = (dq_s[...] * HD**-0.5).T.astype(BF)
    for j in range(len(slots)):
        at = slice(j * rows, (j + 1) * rows)
        dx = nt(dk_s[at, :], wk_ref[...]) + nt(dv_s[at, :], wv_ref[...])
        if last and j == 0:
            dx = dx + nt(dq_ref[...], wq_ref[...])

        @pl.when(g == 0)
        def _(at=at, dx=dx, j=j):
            dx_s[at, :] = dx + base_ref[...] if last and j == 0 else dx

        @pl.when(g > 0)
        def _(at=at, dx=dx):
            dx_s[at, :] += dx

    @pl.when(g == pl.num_programs(0) - 1)
    def _():
        dx_ref[...] = dx_s[...].astype(dx_ref.dtype)


def attend_backward(q, k, v, do, o, lse, slots, weights, seg, where, dq=None, base=None):
    rows, width = q.shape
    keys = rows * len(slots)
    first, last = dq is None, base is not None
    groups, wide = width // GROUP, GROUP // HD * rows
    q_spec = pl.BlockSpec((rows, GROUP), lambda i, s, w: (0, i))
    wq_spec, wk_spec, wv_spec = (
        pl.BlockSpec((None, width, GROUP), lambda i, s, w, m=m: (m, 0, i)) for _, m in weights
    )
    row_spec = pl.BlockSpec((1, 1, wide), lambda i, s, w: (i, 0, 0))
    acc_spec = pl.BlockSpec((GROUP, rows), lambda i, s, w: (i, 0))
    keys_spec = pl.BlockSpec((keys, GROUP), lambda i, s, w: (0, i))

    def ids_spec(entry):
        return pl.BlockSpec((1, rows), lambda i, s, w: (0, w[entry]))

    def slot_spec(slot):
        return pl.BlockSpec((rows, GROUP), lambda i, s, w: (slot, i))

    wq, wk, wv = (a for a, _ in weights)
    count = len(slots)
    ins = [q, do, o, lse, wk, wv, seg] + [k] * count + [v] * count + [seg] * count
    in_specs = [q_spec, q_spec, q_spec, row_spec, wk_spec, wv_spec, ids_spec(0)]
    in_specs += [slot_spec(s) for s in slots] * 2 + [ids_spec(1 + s) for s in slots]
    if not first:
        ins.append(dq)
        in_specs.append(acc_spec)
    scratch = [pltpu.VMEM((wide, GROUP), BF), pltpu.VMEM((wide, GROUP), BF), pltpu.VMEM((1, wide), F32)]
    scratch += [pltpu.VMEM((keys, 128), F32), pltpu.VMEM((1, rows), F32), pltpu.VMEM((keys, width), F32)]
    if last:
        ins += [wq, base]
        in_specs += [wq_spec, pl.BlockSpec((rows, width), lambda i, s, w: (0, 0))]
        scratch.append(pltpu.VMEM((GROUP, rows), F32))
    keys_shape = jax.ShapeDtypeStruct((keys, width), BF)
    results = [
        (keys_spec, keys_shape),
        (keys_spec, keys_shape),
        (q_spec, jax.ShapeDtypeStruct((rows, width), BF))
        if last
        else (acc_spec, jax.ShapeDtypeStruct((width, rows), F32)),
        (
            pl.BlockSpec((keys, width), lambda i, s, w: (0, 0)),
            jax.ShapeDtypeStruct((keys, width), F32 if last else BF),
        ),
    ]
    return pl.pallas_call(
        partial(backward_kernel, slots=slots, first=first, last=last),
        out_shape=tuple(r[1] for r in results),
        grid_spec=pltpu.PrefetchScalarGridSpec(
            num_scalar_prefetch=2,
            grid=(groups,),
            in_specs=in_specs,
            out_specs=[r[0] for r in results],
            scratch_shapes=scratch,
        ),
        cost_estimate=pl.CostEstimate(flops=FEW, bytes_accessed=FEW, transcendentals=0),
        name="attend_backward",
    )(seg[0], where, *ins)


def attn_grad_kernel(core_ref, *refs, calls, slots, block_rows):
    x_refs, dq_ref, extra_ref, refs = refs[:slots], refs[slots], refs[slots + 1], refs[slots + 2 :]
    dk_refs, dv_refs, refs = refs[:calls], refs[calls : 2 * calls], refs[2 * calls :]
    first_ref, second_ref, x_s, w_s = refs
    rows = dq_ref.shape[0]

    @pl.when(pl.program_id(0) == 0)
    def _():
        for j, x_ref in enumerate(x_refs):
            x_s[:, j * rows : (j + 1) * rows] = x_ref[...].T

    sums = [
        jnp.sum(dq_ref[...].astype(F32), axis=0, keepdims=True),
        sum(jnp.sum(d[...].astype(F32), axis=0, keepdims=True) for d in dv_refs),
        extra_ref[...],
        jnp.zeros((EXTRA - 2 - extra_ref.shape[0], w_s.shape[1]), F32),
    ]
    sums = jnp.concatenate(sums, axis=0)

    def over_keys(parts):
        total, start = 0.0, 0
        for d in parts:
            total = total + nn(x_s[:, start : start + d.shape[0]], d[...])
            start += d.shape[0]
        return total

    for m, parts in enumerate(((dq_ref,), dk_refs, dv_refs)):
        if not block_rows:
            first_ref[m] = over_keys(parts)
            continue
        w_s[...] = over_keys(parts)
        core = core_ref[0]
        at = slice(m * block_rows, (m + 1) * block_rows)
        for b in range(first_ref.shape[0]):
            far = pl.multiple_of((2 * b + 1 - core) * block_rows, block_rows)
            near = pl.multiple_of((2 * b + core) * block_rows, block_rows)
            first_ref[b, at] = w_s[pl.ds(far, block_rows), :].astype(BF)
            second_ref[b, at] = w_s[pl.ds(near, block_rows), :]
    if block_rows:
        for b in range(first_ref.shape[0]):
            first_ref[b, 3 * block_rows :] = sums.astype(BF)
            second_ref[b, 3 * block_rows :] = sums
    else:
        second_ref[...] = sums


def attn_grads(core, xs, dq, extra, dks, dvs, n):
    rows, width = dq.shape
    block_rows = width // n if (width // n) % 16 == 0 else 0
    x_spec = pl.BlockSpec((rows, width), lambda i, c: (0, 0))

    def d_spec(d):
        return pl.BlockSpec((d.shape[0], GROUP), lambda i, c: (0, i))

    if block_rows:
        shape = (n // 2, 3 * block_rows + EXTRA)
        spec = pl.BlockSpec((*shape, GROUP), lambda i, c: (0, 0, i))
        results = [(spec, jax.ShapeDtypeStruct((*shape, width), t)) for t in (BF, F32)]
    else:
        spec = pl.BlockSpec((3, width, GROUP), lambda i, c: (0, 0, i))
        results = [(spec, jax.ShapeDtypeStruct((3, width, width), F32))]
        spec = pl.BlockSpec((EXTRA, GROUP), lambda i, c: (0, i))
        results.append((spec, jax.ShapeDtypeStruct((EXTRA, width), F32)))
    return pl.pallas_call(
        partial(attn_grad_kernel, calls=len(dks), slots=len(xs), block_rows=block_rows),
        out_shape=tuple(r[1] for r in results),
        grid_spec=pltpu.PrefetchScalarGridSpec(
            num_scalar_prefetch=1,
            grid=(width // GROUP,),
            in_specs=[x_spec] * len(xs) + [d_spec(d) for d in (dq, extra, *dks, *dvs)],
            out_specs=[r[0] for r in results],
            scratch_shapes=[pltpu.VMEM((width, rows * len(xs)), BF), pltpu.VMEM((width, GROUP), F32)],
        ),
        cost_estimate=pl.CostEstimate(flops=FEW, bytes_accessed=FEW, transcendentals=0),
        name="attn_grads",
    )(core, *xs, dq, extra, *dks, *dvs)


def norm_parts(rows_in):
    mean = jnp.mean(rows_in, axis=-1, keepdims=True)
    centred = rows_in - mean
    spread = jnp.mean(centred * centred, axis=-1, keepdims=True)
    r = lax.rsqrt(spread + EPSILON)
    return centred * r, r


def norm_back(g_y, n, r, gain):
    e = g_y * gain
    return r * (e - jnp.mean(e, axis=-1, keepdims=True) - n * jnp.mean(e * n, axis=-1, keepdims=True))


def gelu_parts(u):
    c = 0.7978845608028654
    square = u * u
    th = jnp.tanh(c * u * (1.0 + 0.044715 * square))
    half = 0.5 * (1.0 + th)
    slope = half + 0.5 * u * (1.0 - th * th) * (c + 3 * 0.044715 * c * square)
    return u * half, slope


def down_rows(x):
    return jnp.sum(x, axis=0, keepdims=True)


def middle_kernel(known, *refs, count):
    w_refs, refs = (refs[:count], refs[count : 2 * count]), refs[2 * count :]
    ctx_ref, x_ref, grad_ref, vec_ref, bias_ref = refs[:5]
    out_ref, first_ref, gctx_ref, lefts_ref, rights_ref, sums_ref, bias_grad_ref = refs[5:12]
    w_s, mix_ref, slope_s, n1_s, r1_s, acc_s, sems, mix_sems = refs[12:]
    parts, units = bias_ref.shape
    rows, width = x_ref.shape

    def copy(which, t, j):
        return piece_copy(
            w_refs[which], j, known[1], 2 * width // units + t, units, w_s.at[which, t], sems.at[which, t, j]
        )

    mix_copies = [
        piece_copy(w_refs[1], j, known[1], 1, width, mix_ref, mix_sems.at[j]) for j in range(count)
    ]
    for mix_copy in mix_copies:
        mix_copy.start()
    for which in range(2):
        for t in range(parts):
            for j in range(count):
                copy(which, t, j).start()
    for mix_copy in mix_copies:
        mix_copy.wait()

    def cols(t):
        return pl.ds(pl.multiple_of(t * units, units), units)

    first_sum = x_ref[...].astype(F32) + nt(ctx_ref[...], mix_ref[...]) + vec_ref[0:1, :]
    n1, r1 = norm_parts(first_sum)
    n1_s[...] = n1
    r1_s[...] = jnp.broadcast_to(r1, r1_s.shape)
    acc_s[...] = n1 * vec_ref[1:2, :] + vec_ref[2:3, :]
    lefts_ref[1] = acc_s[...].astype(BF)

    for which in range(2):
        for t in range(parts):
            for j in range(count):
                copy(which, t, j).wait()

    def up(t, _):
        pre = nn(lefts_ref[1], w_s[0, t]) + bias_ref[pl.ds(t, 1), :]
        act, slope = gelu_parts(pre)
        slope_s[t] = slope
        low = act.astype(BF)
        rights_ref[:, cols(t)] = low
        acc_s[...] += nt(low, w_s[1, t])
        return 0

    lax.fori_loop(0, parts, up, 0)
    n2, r2 = norm_parts(acc_s[...] + vec_ref[3:4, :])
    out_ref[...] = (n2 * vec_ref[4:5, :] + vec_ref[5:6, :]).astype(BF)
    row = lax.broadcasted_iota(jnp.int32, (rows, width), 0)
    g_out = jnp.where(row < known[0], grad_ref[...].astype(F32), 0.0)
    g_second = norm_back(g_out, n2, r2, vec_ref[4:5, :])
    sums_ref[3:4, :] = down_rows(g_second)
    sums_ref[4:5, :] = down_rows(g_out * n2)
    sums_ref[5:6, :] = down_rows(g_out)
    lefts_ref[0] = g_second.astype(BF)
    acc_s[...] = g_second

    def back(t, _):
        g_pre = (nn(lefts_ref[0], w_s[1, t]) * slope_s[t]).astype(BF)
        rights_ref[:, cols(parts + t)] = g_pre
        bias_grad_ref[pl.ds(t, 1), :] = down_rows(g_pre.astype(F32))
        acc_s[...] += nt(g_pre, w_s[0, t])
        return 0

    lax.fori_loop(0, parts, back, 0)
    g_normed = acc_s[...]
    n1 = n1_s[...]
    g_first = norm_back(g_normed, n1, r1_s[:, 0:1], vec_ref[1:2, :])
    sums_ref[0:1, :] = down_rows(g_first)
    sums_ref[1:2, :] = down_rows(g_normed * n1)
    sums_ref[2:3, :] = down_rows(g_normed)
    sums_ref[6:8, :] = jnp.zeros((2, width), F32)
    first_ref[...] = g_first
    low = g_first.astype(BF)
    lefts_ref[2] = low
    gctx_ref[...] = nn(low, mix_ref[...]).astype(BF)
    rights_ref[:, 2 * parts * units :] = ctx_ref[...]


def middle(known, pieces, ctx, x, grad, vectors, bias):
    rows, width = x.shape
    parts, units = bias.shape
    count = len(pieces[0])
    vmem = pl.BlockSpec(memory_space=pltpu.VMEM)
    shapes = [
        ((rows, width), BF),
        ((rows, width), F32),
        ((rows, width), BF),
        ((3, rows, width), BF),
        ((rows, 2 * parts * units + width), BF),
        ((8, width), F32),
        ((parts, units), F32),
    ]
    return pl.pallas_call(
        partial(middle_kernel, count=count),
        out_shape=tuple(jax.ShapeDtypeStruct(*s) for s in shapes),
        in_specs=[pl.BlockSpec(memory_space=pltpu.SMEM)] + [pl.BlockSpec(memory_space=pl.ANY)] * (2 * count) + [vmem] * 5,
        out_specs=[vmem] * len(shapes),
        scratch_shapes=[
            pltpu.VMEM((2, parts, width, units), BF),
            pltpu.VMEM((width, width), BF),
            pltpu.VMEM((parts, rows, units), F32),
            pltpu.VMEM((rows, width), F32),
            pltpu.VMEM((rows, 128), F32),
            pltpu.VMEM((rows, width), F32),
            pltpu.SemaphoreType.DMA((2, parts, count)),
            pltpu.SemaphoreType.DMA((count,)),
        ],
        compiler_params=pltpu.CompilerParams(vmem_limit_bytes=63 << 20),
        cost_estimate=pl.CostEstimate(flops=FEW, bytes_accessed=FEW, transcendentals=0),
        name="middle",
    )(known, *pieces[0], *pieces[1], ctx, x, grad, vectors, bias)


def ffn_grad_kernel(place, left_ref, right_ref, *refs, core):
    out_ref, left_s, chosen_s = refs[-3:]

    @pl.when(pl.program_id(0) % 4 == 0)
    def _():
        left_s[...] = left_ref[0].T
        if core is not None:
            size = left_s.shape[0] // core[1]
            for q in range(core[1] // 2):
                block = place[0] ^ (2 * q + core[0])
                chosen_s[q * size : (q + 1) * size, :] = left_s[pl.ds(pl.multiple_of(block * size, size), size), :]

    total = nn((left_s if core is None else chosen_s)[...], right_ref[...])
    if len(refs) == 4:
        total = total + refs[0][...].astype(F32)
    out_ref[...] = total.astype(BF)


def ffn_grads(place, lefts, rights, core=None, got=None):
    _, rows, width = lefts.shape
    units = rights.shape[1] // 9
    out_rows = width if core is None else width // 2
    out_spec = pl.BlockSpec((out_rows, units), lambda i, p: (0, i))
    return pl.pallas_call(
        partial(ffn_grad_kernel, core=core),
        out_shape=jax.ShapeDtypeStruct((out_rows, rights.shape[1]), BF),
        grid_spec=pltpu.PrefetchScalarGridSpec(
            num_scalar_prefetch=1,
            grid=(9,),
            in_specs=[
                pl.BlockSpec((1, rows, width), lambda i, p: (i // 4, 0, 0)),
                pl.BlockSpec((rows, units), lambda i, p: (0, i)),
            ]
            + ([] if got is None else [out_spec]),
            out_specs=out_spec,
            scratch_shapes=[pltpu.VMEM((width, rows), BF), pltpu.VMEM((width // 2, rows), BF)],
        ),
        cost_estimate=pl.CostEstimate(flops=FEW, bytes_accessed=FEW, transcendentals=0),
        name="ffn_grads",
    )(place, lefts, rights, *(() if got is None else (got,)))


def on_device(
    tokens,
    segments,
    query_weight,
    query_bias,
    key_weight,
    value_weight,
    value_bias,
    mix_weight,
    mix_bias,
    norm_gain,
    norm_shift,
    up_weight,
    up_bias,
    down_weight,
    down_bias,
    final_gain,
    final_shift,
    out_grad,
):
    t = lax.axis_index("tensor")
    f = lax.axis_index("fsdp")
    n = lax.axis_size("fsdp")
    rows, width = tokens.shape
    r, units = up_weight.shape
    cols = query_weight.shape[1]
    owner = slot_owner(t)

    shard = jnp.stack(
        [
            jnp.concatenate([query_weight, key_weight, value_weight, mix_weight.T], axis=1),
            up_weight,
            down_weight.T,
        ]
    )
    w_a, w_below, w_above = line_first(shard)
    w_c = line_second(w_below, w_above)
    x_a, x_below, x_above = line_first(after(tokens, w_c))
    w_slots = (shard, w_a, w_c, line_third(w_c, w_below))

    def half(first, last):
        line = [w[0][:, m * cols : (m + 1) * cols] for m in (first, first + 1) for w in w_slots]
        return jnp.concatenate(line + [w[last] for w in w_slots], axis=1)

    own = (half(0, 1), half(2, 2))
    bits = outer_bits()
    orders = (bits, bits[::-1])
    held = [{0: own[0]}, {0: own[1]}]
    passed = []

    def pass_on(step):
        arrived = []
        for i in range(2):
            bit = orders[i][step]
            for place in sorted(held[i]):
                got = lax.ppermute(held[i][place], "fsdp", partner(bit))
                arrived.append((i, place | (bit >> 1), got))
        return arrived

    def keep(arrived, *gate):
        values = after(tuple(a[2] for a in arrived), *gate)
        for (i, place, _), value in zip(arrived, values):
            held[i][place] = value
        passed.append(values)

    def to_partner(values, *gate):
        return after(tuple(lax.ppermute(v, "fsdp", partner(1)) for v in values), *gate)

    first = pass_on(0)
    direct = []
    if len(bits) == 2:
        direct = [
            (i, orders[i][1] >> 1, lax.ppermute(own[i], "fsdp", partner(orders[i][1]))) for i in range(2)
        ]
    far_own = to_partner(own)
    keep(first, x_a)
    x_c = line_second(*after((x_below, x_above), *passed[0]))
    if direct:
        forwarded = [
            (i, 3, lax.ppermute(held[i][orders[i][0] >> 1], "fsdp", partner(orders[i][1]))) for i in range(2)
        ]
        far_first = to_partner(passed[0])
        keep(direct, x_c, *far_own)
        x_b = line_third(after(x_c, *passed[1]), x_below, *far_first)
        far_direct = to_partner(passed[1])
        keep(forwarded)
        far_last = to_partner(passed[2])
        far = [{0: far_own[i], orders[i][0] >> 1: far_first[i]} for i in range(2)]
        for i in range(2):
            far[i][orders[i][1] >> 1], far[i][3] = far_direct[i], far_last[i]
    else:
        x_b = line_third(x_c, x_below)
        for step in range(1, len(bits)):
            keep(pass_on(step))
        far = [dict(zip(sorted(h), to_partner([h[p] for p in sorted(h)]))) for h in held]
    pieces = [[h[p] for h in (near, away) for p in sorted(near)] for near, away in zip(held, far)]
    if r % 16:
        pieces = [[assembled(p)] for p in pieces]

    def by_slot(vector):
        parts = vector.reshape(4, -1)
        return jnp.concatenate([lax.dynamic_slice_in_dim(parts, owner[i], 1, axis=0)[0] for i in range(4)])

    seg = jnp.where(segments == 0, 9, segments)
    where = jnp.concatenate([t[None], owner, (f & 1)[None], f[None]]).astype(jnp.int32)
    xs = (tokens, x_a, x_c, x_b)
    q, k, v, ctx, lse, w_all = attend_forward(xs, pieces, (by_slot(query_bias), by_slot(value_bias)), seg, where)
    weights = tuple((w_all, m) for m in range(3))

    own_ids = lax.dynamic_slice_in_dim(seg[0], t * rows, rows)
    known = jnp.stack([jnp.sum((own_ids < 9).astype(jnp.int32)), f.astype(jnp.int32)])
    vectors = jnp.stack([mix_bias, norm_gain, norm_shift, down_bias, final_gain, final_shift])
    layer_out, g_first, g_ctx, lefts, rights, sums, up_sums = middle(
        known, pieces, ctx, tokens, out_grad, vectors, by_slot(up_bias).reshape(4, units)
    )
    place = f.astype(jnp.int32)[None]
    if r % 16:
        full = ffn_grads(place, lefts, rights).reshape(n, r, -1)
        kept, sent = (
            jnp.concatenate([lax.dynamic_slice_in_dim(full, f ^ (2 * q + c), 1)[0] for q in range(n // 2)])
            for c in range(2)
        )
    else:
        sent = ffn_grads(place, lefts, rights, (1, n))
    got = lax.ppermute(sent, "fsdp", partner(1))
    g_ctx = after(g_ctx, sent)

    args = (q, k, v, g_ctx, ctx, lse)
    dk_b, dv_b, dq, dx_b = attend_backward(*args, (3,), weights, seg, where)
    r1 = lax.ppermute(dx_b, "tensor", [(0, 1), (3, 2)])
    lefts = after(lefts, dx_b)
    if r % 16:
        near = (kept.astype(F32) + got.astype(F32)).astype(BF)
    else:
        near = ffn_grads(place, lefts, rights, (0, n), got)
    steps = list(zip(outer_bits(), outer_bits()[::-1]))
    blocks, lefts = zip(*(outer_axes(b) for b in (near[:, : 4 * units], near[:, 4 * units :])))
    halves = start_halving(blocks, lefts, steps[0])
    dk_n, dv_n, dq, dx_n = attend_backward(*args, (2, 1), weights, seg, where, after(dq, near))
    dx_c, dx_a = dx_n[:rows], dx_n[rows:]
    blocks = add_low(halves[0], after(halves[1], dx_n))
    halves = start_halving(blocks, halves[2], steps[1])
    middle_x = (dx_c.astype(F32) + r1.astype(F32)).astype(BF)
    rx = lax.ppermute(middle_x, "tensor", [(0, 1), (3, 2)])
    ry = lax.ppermute(middle_x, "tensor", [(1, 2), (2, 1)])
    dk_o, dv_o, dq, dx_own = attend_backward(
        *args, (0,), weights, seg, where, after(dq, middle_x, *blocks), g_first
    )
    rx, ry = (a.astype(F32) for a in after((rx, ry), dx_own))
    up_x = (dx_a.astype(F32) + jnp.where(t == 1, rx, ry)).astype(BF)
    down_x = jnp.where(t == 3, dx_a.astype(F32), dx_b.astype(F32) + jnp.where(t == 1, ry, rx)).astype(BF)
    from_below = lax.ppermute(up_x, "tensor", [(0, 1), (1, 2), (2, 3)])
    from_above = lax.ppermute(down_x, "tensor", [(1, 0), (2, 1), (3, 2)])

    d_one, d_two = add_low(halves[0], after(halves[1], dx_own))
    for pair in steps[2:]:
        halves = start_halving([d_one, d_two], halves[2], pair)
        d_one, d_two = add_low(halves[0], halves[1])
    early = jnp.stack(
        [
            jnp.concatenate(
                [
                    d_one[:, i * units : (i + 1) * units],
                    d_two[:, i * units : (i + 1) * units],
                    d_two[:, 4 * units + i * cols : 4 * units + (i + 1) * cols],
                ],
                axis=1,
            )
            for i in range(4)
        ]
    )

    xs = (xs[0], xs[2], xs[1], xs[3])
    extra = jnp.concatenate([sums[:6], in_line_order(up_sums, t)])
    dq = after(dq, up_x, down_x, early)
    sent, kept = attn_grads(where[5:6], xs, dq, extra, (dk_o, dk_n, dk_b), (dv_o, dv_n, dv_b), n)
    if r % 16:
        split = sent.reshape(3, n // 2, 2, r, width)
        sums = jnp.broadcast_to(kept, (n // 2, EXTRA, width))
        sent, kept = (
            jnp.concatenate(
                [
                    lax.dynamic_index_in_dim(split, c, 2, keepdims=False)
                    .transpose(1, 0, 2, 3)
                    .reshape(n // 2, 3 * r, width),
                    sums,
                ],
                axis=1,
            )
            for c in (1 - (f & 1), f & 1)
        )
        sent = sent.astype(BF)
    sent = after(sent, from_below, from_above)
    early_own, early = early[0], spread(early, t)
    got = lax.ppermute(sent, "fsdp", partner(1))
    near = (kept + after(got, early[0]).astype(F32)).astype(BF)
    same_core = [list(range(c, n, 2)) for c in range(2)]
    arrived = lax.all_to_all(near, "fsdp", split_axis=0, concat_axis=0, axis_index_groups=same_core, tiled=True)
    arrived = after(arrived, *early)
    late = jnp.sum(arrived.astype(F32), axis=0).astype(BF)
    count = 12
    by_head = jnp.stack([late[3 * r : 3 * r + 2, i * cols : (i + 1) * cols] for i in range(4)])
    by_head = in_line_order(by_head, t).reshape(8, cols)
    whole = [late[3 * r + 2 : 3 * r + count, i * cols : (i + 1) * cols] for i in range(4)]
    below = jnp.concatenate([by_head, *whole])
    late = jnp.stack(
        [jnp.concatenate([late[: 3 * r, i * cols : (i + 1) * cols], below]) for i in range(4)]
    )
    late = total(late[0], spread(late, t))
    early = total(early_own, early)
    tokens_grad = dx_own + from_below.astype(F32) + from_above.astype(F32)
    qv = late[3 * r : 3 * r + 8].reshape(4, 2, cols).transpose(1, 0, 2).reshape(2, width)
    sums = late[3 * r + 8 :].reshape(4, count - 2, cols).transpose(1, 0, 2).reshape(count - 2, width)
    up_sums = sums[6:].reshape(-1)
    late = late[: 3 * r].reshape(3, r, cols)

    return (
        layer_out,
        tokens_grad,
        late[0],
        qv[0],
        late[1],
        late[2],
        qv[1],
        early[:, 2 * units :].T,
        sums[0],
        sums[1],
        sums[2],
        early[:, units : 2 * units],
        up_sums,
        early[:, :units].T,
        sums[3],
        sums[4],
        sums[5],
    )


def solution(mesh):
    both, rows_f, square, flipped = (
        P(("fsdp", "tensor"), None),
        P("fsdp", None),
        P("fsdp", "tensor"),
        P("tensor", "fsdp"),
    )
    return jax.shard_map(
        on_device,
        mesh=mesh,
        in_specs=(
            both, rows_f, square, P(), square, square, P(), flipped, P(), P(), P(),
            square, P(), flipped, P(), P(), P(), both,
        ),
        out_specs=(
            both, both, square, P(), square, square, P(), flipped, P(), P(), P(),
            square, P(), flipped, P(), P(), P(),
        ),
        check_vma=False,
    )
```

```python
from functools import partial

import jax
import jax.numpy as jnp
from jax import lax
from jax.experimental import pallas as pl
from jax.experimental.pallas import tpu as pltpu
from jax.sharding import PartitionSpec as P

HD = 64
GROUP = 256
BLOCK = 256
EPSILON = 1e-05
MASKED = -1e30
LOG2E = 1.4426950408889634
SCORE = HD**-0.5 * LOG2E
EXTRA = 16
SHIFTS = (1, 3, 2)
FEW = 1000
BF = jnp.bfloat16
F32 = jnp.float32


def after(value, *others):
    return lax.optimization_barrier((value,) + others)[0] if others else value


def nt(a, b):
    return lax.dot_general(a, b, (((1,), (1,)), ((), ())), preferred_element_type=F32)


def nn(a, b):
    return lax.dot_general(a, b, (((1,), (0,)), ((), ())), preferred_element_type=F32)


def line_first(own):
    below = lax.ppermute(own, "tensor", [(0, 1), (1, 2), (2, 3)])
    above = lax.ppermute(own, "tensor", [(1, 0), (2, 1), (3, 2)])
    return jnp.where(lax.axis_index("tensor") < 3, above, below), below, above


def line_second(below, above, *gate):
    below2 = lax.ppermute(below, "tensor", [(1, 2), (2, 3)])
    above2 = lax.ppermute(above, "tensor", [(2, 1), (1, 0)])
    below2, above2 = after((below2, above2), *gate)
    return jnp.where(lax.axis_index("tensor") < 2, above2, below2)


def line_third(slot_c, below, *gate):
    far = after(lax.ppermute(slot_c, "tensor", [(1, 0), (2, 3)]), *gate)
    t = lax.axis_index("tensor")
    return jnp.where((t == 0) | (t == 3), far, below)


def slot_owner(t):
    return jnp.stack([t, jnp.where(t < 3, t + 1, 2), lax.rem(t + 2, 4), jnp.where(t == 3, 0, lax.rem(t + 3, 4))])


def owner_slot(t):
    owner = slot_owner(t)
    return [sum(jnp.where(owner[k] == j, k, 0) for k in range(4)) for j in range(4)]


def in_line_order(slots, slot_of):
    return jnp.concatenate([lax.dynamic_slice_in_dim(slots, s, 1, axis=0) for s in slot_of])


def spread(slots, goals):
    arrived = []
    for shift, slot in zip(SHIFTS, goals):
        block = lax.dynamic_index_in_dim(slots, slot, 0, keepdims=False)
        arrived.append(lax.ppermute(block, "tensor", [(i, (i + shift) % 4) for i in range(4)]))
    return arrived


def total(own, arrived):
    return own.astype(F32) + sum(a.astype(F32) for a in arrived)


def partner(bit):
    n = lax.axis_size("fsdp")
    return [(i, i ^ bit) for i in range(n)]


def outer_bits():
    n = lax.axis_size("fsdp")
    return [1 << k for k in range(1, n.bit_length() - 1)]


def assembled(pieces):
    n = len(pieces)
    f = lax.axis_index("fsdp")
    stacked = jnp.stack(pieces).reshape(2, n // 2, *pieces[0].shape)
    blocks = []
    for a in range(n):
        rel = f ^ a
        block = lax.dynamic_slice_in_dim(stacked, rel & 1, 1, axis=0)
        blocks.append(lax.dynamic_slice_in_dim(block, rel >> 1, 1, axis=1)[0, 0])
    return jnp.concatenate(blocks)


def outer_axes(block):
    n = lax.axis_size("fsdp")
    bits = outer_bits()
    return block.reshape((2,) * len(bits) + (block.shape[0] // (n // 2), block.shape[1])), sorted(bits, reverse=True)


def start_halving(blocks, lefts, pair):
    kept, arrived, rest, sent = [], [], [], []
    for block, left, bit in zip(blocks, lefts, pair):
        axis = left.index(bit)
        kept.append(lax.index_in_dim(block, 0, axis, keepdims=False))
        sent.append(lax.index_in_dim(block, 1, axis, keepdims=False))
        arrived.append(lax.ppermute(sent[-1], "fsdp", partner(bit)))
        rest.append([b for b in left if b != bit])
    return (kept, arrived, rest), sent


def add_low(kept, arrived):
    return [(a.astype(F32) + b.astype(F32)).astype(BF) for a, b in zip(kept, arrived)]


def stack_heads(x):
    lane = lax.broadcasted_iota(jnp.int32, (BLOCK, x.shape[1]), 1)
    zero = jnp.zeros((BLOCK, x.shape[1]), x.dtype)
    heads = x.shape[1] // HD
    return jnp.concatenate(
        [
            jnp.where((lane >= h * HD) & (lane < (h + 1) * HD), x[j * BLOCK : (j + 1) * BLOCK], zero)
            for j in range(x.shape[0] // BLOCK)
            for h in range(heads)
        ],
        axis=0,
    )


def block_kind(seg, q_at, k_at):
    q_lo, q_hi = seg[q_at], seg[q_at + BLOCK - 1]
    k_lo, k_hi = seg[k_at], seg[k_at + BLOCK - 1]
    meet = (q_lo <= k_hi) & (k_lo <= q_hi)
    one = (q_lo == q_hi) & (k_lo == q_lo) & (k_hi == q_lo)
    return jnp.where(one, 2, jnp.where(meet, 1, 0))


def ids_down(ids_refs, col_s):
    rows = ids_refs[0].shape[1]

    @pl.when(pl.program_id(0) == 0)
    def _():
        for j, ids in enumerate(ids_refs):
            wide = jnp.broadcast_to(ids[...].astype(F32), (col_s.shape[1], rows))
            col_s[j * rows : (j + 1) * rows, :] = wide.T


def each_block(seg, where, slots, rows, visit):
    per = rows // BLOCK
    for j, slot in enumerate(slots):

        def step(i, _, j=j, slot=slot):
            kb, qb = i // per, lax.rem(i, per)
            at = pl.ds(pl.multiple_of(kb * BLOCK, BLOCK), BLOCK)
            kind = block_kind(seg, where[0] * rows + qb * BLOCK, where[1 + slot] * rows + kb * BLOCK)
            visit(j, at, kb, qb, kind)
            return 0

        lax.fori_loop(0, per * per, step, 0)


def piece_copy(pieces, j, f, column, width, target, sem):
    r = pieces[0].shape[0]
    place = 0
    if len(pieces) > 1:
        core, outer = j // (len(pieces) // 2), j % (len(pieces) // 2)
        place = f ^ (2 * outer + core)
    rows = pl.ds(pl.multiple_of(place * r, r), r)
    return pltpu.make_async_copy(
        pieces[j].at[:, column * width : (column + 1) * width], target.at[rows, :], sem
    )


def lanes(index, size):
    return pl.ds(pl.multiple_of(index * size, size), size)


def forward_kernel(seg, where, *refs, slots, count):
    refs = list(refs)

    def take(count):
        taken, refs[:] = refs[:count], refs[count:]
        return taken

    x_refs = take(len(slots))
    ids_refs = take(len(slots))
    pieces = (take(count), take(count))
    bq_ref, bv_ref, sq_ref = take(3)
    q_ref, k_ref, v_ref, o_ref, lse_ref, w_ref, q_s, col_s, m_s, l_s, acc_s, ids_s, w_s, sems = refs

    @pl.when(pl.program_id(0) == 0)
    def _():
        copies = [
            piece_copy(pieces[m // 2], j, where[6], m % 2, w_s.shape[2], w_s.at[m], sems.at[m, j])
            for m in range(3)
            for j in range(count)
        ]
        for copy in copies:
            copy.start()
        for copy in copies:
            copy.wait()

    w_ref[...] = w_s[:, :, lanes(pl.program_id(0), q_ref.shape[1])]
    wq_ref, wk_ref, wv_ref = (w_ref.at[m] for m in range(3))
    rows, width = q_ref.shape
    heads = width // HD
    wide = heads * BLOCK
    q_ref[...] = (nn(x_refs[0][...], wq_ref[...]) + bq_ref[...]).astype(BF)
    m_s[...] = jnp.full(m_s.shape, MASKED, F32)
    l_s[...] = jnp.zeros(l_s.shape, F32)
    acc_s[...] = jnp.zeros(acc_s.shape, F32)
    for j, x_ref in enumerate(x_refs):
        at = slice(j * rows, (j + 1) * rows)
        k_ref[at, :] = nn(x_ref[...], wk_ref[...]).astype(BF)
        v_ref[at, :] = (nn(x_ref[...], wv_ref[...]) + bv_ref[...]).astype(BF)
    q_s[...] = stack_heads(q_ref[...])
    ids_down(ids_refs, col_s)
    ids_s[...] = sq_ref[...].astype(F32)

    def block(at, qb, masked):
        stacked, part = lanes(qb, wide), lanes(qb, BLOCK)
        s = nt(k_ref[at, :], q_s[stacked, :])
        if masked:
            same = col_s[at, 0:1] == ids_s[:, part]
            s = jnp.where(jnp.concatenate([same] * heads, axis=1), s, MASKED)
        m_old = m_s[:, stacked]
        m_new = jnp.maximum(m_old, jnp.max(s, axis=0, keepdims=True))
        alpha = jnp.exp2((m_old - m_new) * SCORE)
        p = jnp.exp2((s - m_new) * SCORE)
        p_low = p.astype(BF)
        l_s[:, stacked] = alpha * l_s[:, stacked] + jnp.sum(p, axis=0, keepdims=True)
        m_s[:, stacked] = m_new
        v_t = v_ref[at, :].T
        for h in range(heads):
            hs, qs = slice(h * HD, (h + 1) * HD), slice(h * BLOCK, (h + 1) * BLOCK)
            acc_s[hs, part] = acc_s[hs, part] * alpha[:, qs] + nn(v_t[hs], p_low[:, qs])

    def visit(j, _, kb, qb, kind):
        at = pl.ds(pl.multiple_of(j * rows + kb * BLOCK, BLOCK), BLOCK)
        pl.when(kind == 1)(lambda: block(at, qb, True))
        pl.when(kind == 2)(lambda: block(at, qb, False))

    each_block(seg, where, slots, rows, visit)
    for j in range(rows // BLOCK):
        inverse = 1.0 / l_s[:, j * wide : (j + 1) * wide]
        spread_out = jnp.concatenate(
            [jnp.broadcast_to(inverse[:, h * BLOCK : (h + 1) * BLOCK], (HD, BLOCK)) for h in range(heads)], axis=0
        )
        at = slice(j * BLOCK, (j + 1) * BLOCK)
        o_ref[at, :] = (acc_s[:, at] * spread_out).T.astype(BF)
    lse_ref[0] = m_s[...] * SCORE + jnp.log2(l_s[...])


def attend_forward(xs, pieces, biases, seg, where):
    rows, width = xs[0].shape
    slots = tuple(range(len(xs)))
    keys = rows * len(xs)
    count = len(pieces[0])
    groups, wide = width // GROUP, GROUP // HD * rows
    block_spec = pl.BlockSpec((rows, GROUP), lambda i, s, w: (0, i))
    keys_spec = pl.BlockSpec((keys, GROUP), lambda i, s, w: (0, i))
    b_spec = pl.BlockSpec((1, GROUP), lambda i, s, w: (0, i))
    row_spec = pl.BlockSpec((1, 1, wide), lambda i, s, w: (i, 0, 0))
    block_shape = jax.ShapeDtypeStruct((rows, width), BF)
    keys_shape = jax.ShapeDtypeStruct((keys, width), BF)

    def ids_spec(entry):
        return pl.BlockSpec((1, rows), lambda i, s, w: (0, w[entry]))

    in_specs = [pl.BlockSpec((rows, width), lambda i, s, w: (0, 0))] * len(xs)
    in_specs += [ids_spec(1 + s) for s in slots] + [pl.BlockSpec(memory_space=pl.ANY)] * (2 * count) + [b_spec] * 2 + [ids_spec(0)]
    return pl.pallas_call(
        partial(forward_kernel, slots=slots, count=count),
        out_shape=(
            block_shape,
            keys_shape,
            keys_shape,
            block_shape,
            jax.ShapeDtypeStruct((groups, 1, wide), F32),
            jax.ShapeDtypeStruct((3, width, width), BF),
        ),
        grid_spec=pltpu.PrefetchScalarGridSpec(
            num_scalar_prefetch=2,
            grid=(groups,),
            in_specs=in_specs,
            out_specs=[
                block_spec, keys_spec, keys_spec, block_spec, row_spec,
                pl.BlockSpec((3, width, GROUP), lambda i, s, w: (0, 0, i)),
            ],
            scratch_shapes=[
                pltpu.VMEM((wide, GROUP), BF),
                pltpu.VMEM((keys, 128), F32),
                pltpu.VMEM((1, wide), F32),
                pltpu.VMEM((1, wide), F32),
                pltpu.VMEM((GROUP, rows), F32),
                pltpu.VMEM((1, rows), F32),
                pltpu.VMEM((3, width, width), BF),
                pltpu.SemaphoreType.DMA((3, count)),
            ],
        ),
        cost_estimate=pl.CostEstimate(flops=FEW, bytes_accessed=FEW, transcendentals=0),
        name="attend_forward",
    )(seg[0], where, *xs, *([seg] * len(slots)), *pieces[0], *pieces[1], *(b[None, :] for b in biases), seg)


def backward_kernel(seg, where, *refs, slots, first, last):
    refs = list(refs)

    def take(count):
        taken, refs[:] = refs[:count], refs[count:]
        return taken

    q_ref, do_ref, o_ref, lse_ref, wk_ref, wv_ref, sq_ref = take(7)
    k_refs, v_refs, ids_refs = take(len(slots)), take(len(slots)), take(len(slots))
    if not first:
        (dq_in,) = take(1)
    if last:
        wq_ref, base_ref = take(2)
        dk_s, dv_s, dq_ref, dx_ref, q_s, do_s, delta_s, col_s, ids_s, dx_s, dq_s = refs
    else:
        dk_s, dv_s, dq_s, dx_ref, q_s, do_s, delta_s, col_s, ids_s, dx_s = refs
    g = pl.program_id(0)
    ids_down(ids_refs, col_s)
    ids_s[...] = sq_ref[...].astype(F32)
    rows, width = q_ref.shape
    heads = width // HD
    wide = heads * BLOCK
    q_s[...] = stack_heads(q_ref[...])
    do_s[...] = stack_heads(do_ref[...])
    prod = (do_ref[...].astype(F32) * o_ref[...].astype(F32)).T
    for j in range(rows // BLOCK):
        for h in range(heads):
            piece = prod[h * HD : (h + 1) * HD, j * BLOCK : (j + 1) * BLOCK]
            delta_s[:, j * wide + h * BLOCK : j * wide + (h + 1) * BLOCK] = jnp.sum(piece, axis=0, keepdims=True)
    dq_s[...] = jnp.zeros_like(dq_s) if first else dq_in[...]

    def block(j, at, out_at, qb, masked):
        stacked, part = lanes(qb, wide), lanes(qb, BLOCK)
        k = k_refs[j][at, :]
        k_t = k.T
        s = nt(k, q_s[stacked, :]) * SCORE - lse_ref[0, :, stacked]
        if masked:
            same = col_s[out_at, 0:1] == ids_s[:, part]
            s = jnp.where(jnp.concatenate([same] * heads, axis=1), s, MASKED)
        p = jnp.exp2(s)
        dp = nt(v_refs[j][at, :], do_s[stacked, :])
        ds = (p * (dp - delta_s[:, stacked])).astype(BF)
        dv = nn(p.astype(BF), do_s[stacked, :])
        dk = nn(ds, q_s[stacked, :])
        for h in range(heads):
            hs = slice(h * HD, (h + 1) * HD)
            dq_s[hs, part] += nn(k_t[hs], ds[:, h * BLOCK : (h + 1) * BLOCK])
        return dk, dv

    def visit(j, at, kb, qb, kind):
        out_at = pl.ds(pl.multiple_of(j * rows + kb * BLOCK, BLOCK), BLOCK)

        @pl.when(qb == 0)
        def _():
            acc_k[...] = jnp.zeros(acc_k.shape, F32)
            acc_v[...] = jnp.zeros(acc_v.shape, F32)

        def add(masked):
            dk, dv = block(j, at, out_at, qb, masked)
            acc_k[...] += dk
            acc_v[...] += dv

        pl.when(kind == 1)(lambda: add(True))
        pl.when(kind == 2)(lambda: add(False))

        @pl.when(qb == rows // BLOCK - 1)
        def _():
            dk_s[out_at, :] = (acc_k[...] * HD**-0.5).astype(BF)
            dv_s[out_at, :] = acc_v[...].astype(BF)

    def scoped(acc_k_ref, acc_v_ref):
        nonlocal acc_k, acc_v
        acc_k, acc_v = acc_k_ref, acc_v_ref
        each_block(seg, where, slots, rows, visit)

    acc_k = acc_v = None
    pl.run_scoped(scoped, pltpu.VMEM((BLOCK, width), F32), pltpu.VMEM((BLOCK, width), F32))

    if last:
        dq_ref[...] = (dq_s[...] * HD**-0.5).T.astype(BF)
    for j in range(len(slots)):
        at = slice(j * rows, (j + 1) * rows)
        dx = nt(dk_s[at, :], wk_ref[...]) + nt(dv_s[at, :], wv_ref[...])
        if last and j == 0:
            dx = dx + nt(dq_ref[...], wq_ref[...])

        @pl.when(g == 0)
        def _(at=at, dx=dx, j=j):
            dx_s[at, :] = dx + base_ref[...] if last and j == 0 else dx

        @pl.when(g > 0)
        def _(at=at, dx=dx):
            dx_s[at, :] += dx

    @pl.when(g == pl.num_programs(0) - 1)
    def _():
        dx_ref[...] = dx_s[...].astype(dx_ref.dtype)


def attend_backward(q, k, v, do, o, lse, slots, weights, seg, where, dq=None, base=None):
    rows, width = q.shape
    keys = rows * len(slots)
    first, last = dq is None, base is not None
    groups, wide = width // GROUP, GROUP // HD * rows
    q_spec = pl.BlockSpec((rows, GROUP), lambda i, s, w: (0, i))
    wq_spec, wk_spec, wv_spec = (
        pl.BlockSpec((None, width, GROUP), lambda i, s, w, m=m: (m, 0, i)) for _, m in weights
    )
    row_spec = pl.BlockSpec((1, 1, wide), lambda i, s, w: (i, 0, 0))
    acc_spec = pl.BlockSpec((GROUP, rows), lambda i, s, w: (i, 0))
    keys_spec = pl.BlockSpec((keys, GROUP), lambda i, s, w: (0, i))

    def ids_spec(entry):
        return pl.BlockSpec((1, rows), lambda i, s, w: (0, w[entry]))

    def slot_spec(slot):
        return pl.BlockSpec((rows, GROUP), lambda i, s, w: (slot, i))

    wq, wk, wv = (a for a, _ in weights)
    count = len(slots)
    ins = [q, do, o, lse, wk, wv, seg] + [k] * count + [v] * count + [seg] * count
    in_specs = [q_spec, q_spec, q_spec, row_spec, wk_spec, wv_spec, ids_spec(0)]
    in_specs += [slot_spec(s) for s in slots] * 2 + [ids_spec(1 + s) for s in slots]
    if not first:
        ins.append(dq)
        in_specs.append(acc_spec)
    scratch = [pltpu.VMEM((wide, GROUP), BF), pltpu.VMEM((wide, GROUP), BF), pltpu.VMEM((1, wide), F32)]
    scratch += [pltpu.VMEM((keys, 128), F32), pltpu.VMEM((1, rows), F32), pltpu.VMEM((keys, width), F32)]
    if last:
        ins += [wq, base]
        in_specs += [wq_spec, pl.BlockSpec((rows, width), lambda i, s, w: (0, 0))]
        scratch.append(pltpu.VMEM((GROUP, rows), F32))
    keys_shape = jax.ShapeDtypeStruct((keys, width), BF)
    results = [
        (keys_spec, keys_shape),
        (keys_spec, keys_shape),
        (q_spec, jax.ShapeDtypeStruct((rows, width), BF))
        if last
        else (acc_spec, jax.ShapeDtypeStruct((width, rows), F32)),
        (
            pl.BlockSpec((keys, width), lambda i, s, w: (0, 0)),
            jax.ShapeDtypeStruct((keys, width), F32 if last else BF),
        ),
    ]
    return pl.pallas_call(
        partial(backward_kernel, slots=slots, first=first, last=last),
        out_shape=tuple(r[1] for r in results),
        grid_spec=pltpu.PrefetchScalarGridSpec(
            num_scalar_prefetch=2,
            grid=(groups,),
            in_specs=in_specs,
            out_specs=[r[0] for r in results],
            scratch_shapes=scratch,
        ),
        cost_estimate=pl.CostEstimate(flops=FEW, bytes_accessed=FEW, transcendentals=0),
        name="attend_backward",
    )(seg[0], where, *ins)


def attn_grad_kernel(core_ref, *refs, calls, slots, block_rows):
    x_refs, dq_ref, extra_ref, refs = refs[:slots], refs[slots], refs[slots + 1], refs[slots + 2 :]
    dk_refs, dv_refs, refs = refs[:calls], refs[calls : 2 * calls], refs[2 * calls :]
    first_ref, second_ref, x_s, w_s = refs
    rows = dq_ref.shape[0]

    @pl.when(pl.program_id(0) == 0)
    def _():
        for j, x_ref in enumerate(x_refs):
            x_s[:, j * rows : (j + 1) * rows] = x_ref[...].T

    sums = [
        jnp.sum(dq_ref[...].astype(F32), axis=0, keepdims=True),
        sum(jnp.sum(d[...].astype(F32), axis=0, keepdims=True) for d in dv_refs),
        extra_ref[...],
        jnp.zeros((EXTRA - 2 - extra_ref.shape[0], w_s.shape[1]), F32),
    ]
    sums = jnp.concatenate(sums, axis=0)

    def over_keys(parts):
        total, start = 0.0, 0
        for d in parts:
            total = total + nn(x_s[:, start : start + d.shape[0]], d[...])
            start += d.shape[0]
        return total

    for m, parts in enumerate(((dq_ref,), dk_refs, dv_refs)):
        if not block_rows:
            first_ref[m] = over_keys(parts)
            continue
        w_s[...] = over_keys(parts)
        core = core_ref[0]
        at = slice(m * block_rows, (m + 1) * block_rows)
        for b in range(first_ref.shape[0]):
            far = pl.multiple_of((2 * b + 1 - core) * block_rows, block_rows)
            near = pl.multiple_of((2 * b + core) * block_rows, block_rows)
            first_ref[b, at] = w_s[pl.ds(far, block_rows), :].astype(BF)
            second_ref[b, at] = w_s[pl.ds(near, block_rows), :]
    if block_rows:
        for b in range(first_ref.shape[0]):
            first_ref[b, 3 * block_rows :] = sums.astype(BF)
            second_ref[b, 3 * block_rows :] = sums
    else:
        second_ref[...] = sums


def attn_grads(core, xs, dq, extra, dks, dvs, n):
    rows, width = dq.shape
    block_rows = width // n if (width // n) % 16 == 0 else 0
    x_spec = pl.BlockSpec((rows, width), lambda i, c: (0, 0))

    def d_spec(d):
        return pl.BlockSpec((d.shape[0], GROUP), lambda i, c: (0, i))

    if block_rows:
        shape = (n // 2, 3 * block_rows + EXTRA)
        spec = pl.BlockSpec((*shape, GROUP), lambda i, c: (0, 0, i))
        results = [(spec, jax.ShapeDtypeStruct((*shape, width), t)) for t in (BF, F32)]
    else:
        spec = pl.BlockSpec((3, width, GROUP), lambda i, c: (0, 0, i))
        results = [(spec, jax.ShapeDtypeStruct((3, width, width), F32))]
        spec = pl.BlockSpec((EXTRA, GROUP), lambda i, c: (0, i))
        results.append((spec, jax.ShapeDtypeStruct((EXTRA, width), F32)))
    return pl.pallas_call(
        partial(attn_grad_kernel, calls=len(dks), slots=len(xs), block_rows=block_rows),
        out_shape=tuple(r[1] for r in results),
        grid_spec=pltpu.PrefetchScalarGridSpec(
            num_scalar_prefetch=1,
            grid=(width // GROUP,),
            in_specs=[x_spec] * len(xs) + [d_spec(d) for d in (dq, extra, *dks, *dvs)],
            out_specs=[r[0] for r in results],
            scratch_shapes=[pltpu.VMEM((width, rows * len(xs)), BF), pltpu.VMEM((width, GROUP), F32)],
        ),
        cost_estimate=pl.CostEstimate(flops=FEW, bytes_accessed=FEW, transcendentals=0),
        name="attn_grads",
    )(core, *xs, dq, extra, *dks, *dvs)


def norm_parts(rows_in):
    mean = jnp.mean(rows_in, axis=-1, keepdims=True)
    centred = rows_in - mean
    spread = jnp.mean(centred * centred, axis=-1, keepdims=True)
    r = lax.rsqrt(spread + EPSILON)
    return centred * r, r


def norm_back(g_y, n, r, gain):
    e = g_y * gain
    return r * (e - jnp.mean(e, axis=-1, keepdims=True) - n * jnp.mean(e * n, axis=-1, keepdims=True))


def gelu_parts(u):
    c = 0.7978845608028654
    square = u * u
    th = jnp.tanh(c * u * (1.0 + 0.044715 * square))
    half = 0.5 * (1.0 + th)
    slope = half + 0.5 * u * (1.0 - th * th) * (c + 3 * 0.044715 * c * square)
    return u * half, slope


def down_rows(x):
    return jnp.sum(x, axis=0, keepdims=True)


def middle_kernel(known, *refs, count):
    w_refs, refs = (refs[:count], refs[count : 2 * count]), refs[2 * count :]
    ctx_ref, x_ref, grad_ref, vec_ref, bias_ref = refs[:5]
    out_ref, first_ref, gctx_ref, lefts_ref, rights_ref, sums_ref = refs[5:11]
    w_s, mix_ref, slope_s, n1_s, r1_s, acc_s, sems, mix_sems = refs[11:]
    parts, units = bias_ref.shape
    rows, width = x_ref.shape

    def copy(which, t, j):
        return piece_copy(
            w_refs[which], j, known[1], 2 * width // units + t, units, w_s.at[which, t], sems.at[which, t, j]
        )

    mix_copies = [
        piece_copy(w_refs[1], j, known[1], 1, width, mix_ref, mix_sems.at[j]) for j in range(count)
    ]
    for mix_copy in mix_copies:
        mix_copy.start()
    for which in range(2):
        for t in range(parts):
            for j in range(count):
                copy(which, t, j).start()
    for mix_copy in mix_copies:
        mix_copy.wait()

    def cols(t):
        return pl.ds(pl.multiple_of(t * units, units), units)

    first_sum = x_ref[...].astype(F32) + nt(ctx_ref[...], mix_ref[...]) + vec_ref[0:1, :]
    n1, r1 = norm_parts(first_sum)
    n1_s[...] = n1
    r1_s[...] = jnp.broadcast_to(r1, r1_s.shape)
    acc_s[...] = n1 * vec_ref[1:2, :] + vec_ref[2:3, :]
    lefts_ref[1] = acc_s[...].astype(BF)

    for which in range(2):
        for t in range(parts):
            for j in range(count):
                copy(which, t, j).wait()

    def up(t, _):
        pre = nn(lefts_ref[1], w_s[0, t]) + bias_ref[pl.ds(known[2 + t], 1), :]
        act, slope = gelu_parts(pre)
        slope_s[t] = slope
        low = act.astype(BF)
        rights_ref[:, cols(t)] = low
        acc_s[...] += nt(low, w_s[1, t])
        return 0

    lax.fori_loop(0, parts, up, 0)
    n2, r2 = norm_parts(acc_s[...] + vec_ref[3:4, :])
    out_ref[...] = (n2 * vec_ref[4:5, :] + vec_ref[5:6, :]).astype(BF)
    row = lax.broadcasted_iota(jnp.int32, (rows, width), 0)
    g_out = jnp.where(row < known[0], grad_ref[...].astype(F32), 0.0)
    g_second = norm_back(g_out, n2, r2, vec_ref[4:5, :])
    sums_ref[3:4, :] = down_rows(g_second)
    sums_ref[4:5, :] = down_rows(g_out * n2)
    sums_ref[5:6, :] = down_rows(g_out)
    lefts_ref[0] = g_second.astype(BF)
    acc_s[...] = g_second

    def back(t, _):
        g_pre = (nn(lefts_ref[0], w_s[1, t]) * slope_s[t]).astype(BF)
        rights_ref[:, cols(parts + t)] = g_pre
        sums_ref[pl.ds(6 + known[2 + t], 1), :] = down_rows(g_pre.astype(F32))
        acc_s[...] += nt(g_pre, w_s[0, t])
        return 0

    lax.fori_loop(0, parts, back, 0)
    g_normed = acc_s[...]
    n1 = n1_s[...]
    g_first = norm_back(g_normed, n1, r1_s[:, 0:1], vec_ref[1:2, :])
    sums_ref[0:1, :] = down_rows(g_first)
    sums_ref[1:2, :] = down_rows(g_normed * n1)
    sums_ref[2:3, :] = down_rows(g_normed)
    first_ref[...] = g_first
    low = g_first.astype(BF)
    lefts_ref[2] = low
    gctx_ref[...] = nn(low, mix_ref[...]).astype(BF)
    rights_ref[:, 2 * parts * units :] = ctx_ref[...]


def middle(known, pieces, ctx, x, grad, vectors, bias):
    rows, width = x.shape
    parts, units = bias.shape
    count = len(pieces[0])
    vmem = pl.BlockSpec(memory_space=pltpu.VMEM)
    shapes = [
        ((rows, width), BF),
        ((rows, width), F32),
        ((rows, width), BF),
        ((3, rows, width), BF),
        ((rows, 2 * parts * units + width), BF),
        ((6 + parts, width), F32),
    ]
    return pl.pallas_call(
        partial(middle_kernel, count=count),
        out_shape=tuple(jax.ShapeDtypeStruct(*s) for s in shapes),
        in_specs=[pl.BlockSpec(memory_space=pltpu.SMEM)] + [pl.BlockSpec(memory_space=pl.ANY)] * (2 * count) + [vmem] * 5,
        out_specs=[vmem] * len(shapes),
        scratch_shapes=[
            pltpu.VMEM((2, parts, width, units), BF),
            pltpu.VMEM((width, width), BF),
            pltpu.VMEM((parts, rows, units), F32),
            pltpu.VMEM((rows, width), F32),
            pltpu.VMEM((rows, 128), F32),
            pltpu.VMEM((rows, width), F32),
            pltpu.SemaphoreType.DMA((2, parts, count)),
            pltpu.SemaphoreType.DMA((count,)),
        ],
        compiler_params=pltpu.CompilerParams(vmem_limit_bytes=63 << 20),
        cost_estimate=pl.CostEstimate(flops=FEW, bytes_accessed=FEW, transcendentals=0),
        name="middle",
    )(known, *pieces[0], *pieces[1], ctx, x, grad, vectors, bias)


def ffn_grad_kernel(place, left_ref, right_ref, kept_ref, sent_ref, left_s, chosen_s, *, n):
    half = kept_ref.shape[0]

    @pl.when(pl.program_id(0) % 4 == 0)
    def _():
        left_s[...] = left_ref[0].T
        size = left_s.shape[0] // n
        if size % 16:
            chosen_s[...] = left_s[...]
        else:
            for j in range(n):
                core, outer = j // (n // 2), j % (n // 2)
                block = place[0] ^ (2 * outer + core)
                chosen_s[j * size : (j + 1) * size, :] = left_s[pl.ds(pl.multiple_of(block * size, size), size), :]

    total = nn(chosen_s[...], right_ref[...])
    kept_ref[...] = total[:half].astype(BF)
    sent_ref[...] = total[half:].astype(BF)


def ffn_grads(place, lefts, rights, n):
    _, rows, width = lefts.shape
    units = rights.shape[1] // 9
    out_spec = pl.BlockSpec((width // 2, units), lambda i, p: (0, i))
    out_shape = jax.ShapeDtypeStruct((width // 2, rights.shape[1]), BF)
    return pl.pallas_call(
        partial(ffn_grad_kernel, n=n),
        out_shape=(out_shape, out_shape),
        grid_spec=pltpu.PrefetchScalarGridSpec(
            num_scalar_prefetch=1,
            grid=(9,),
            in_specs=[
                pl.BlockSpec((1, rows, width), lambda i, p: (i // 4, 0, 0)),
                pl.BlockSpec((rows, units), lambda i, p: (0, i)),
            ],
            out_specs=[out_spec, out_spec],
            scratch_shapes=[pltpu.VMEM((width, rows), BF), pltpu.VMEM((width, rows), BF)],
        ),
        cost_estimate=pl.CostEstimate(flops=FEW, bytes_accessed=FEW, transcendentals=0),
        name="ffn_grads",
    )(place, lefts, rights)


def on_device(
    tokens,
    segments,
    query_weight,
    query_bias,
    key_weight,
    value_weight,
    value_bias,
    mix_weight,
    mix_bias,
    norm_gain,
    norm_shift,
    up_weight,
    up_bias,
    down_weight,
    down_bias,
    final_gain,
    final_shift,
    out_grad,
):
    t = lax.axis_index("tensor")
    f = lax.axis_index("fsdp")
    n = lax.axis_size("fsdp")
    rows, width = tokens.shape
    r, units = up_weight.shape
    cols = query_weight.shape[1]
    owner = slot_owner(t)

    def by_slot(vector):
        parts = vector.reshape(4, -1)
        return jnp.concatenate([lax.dynamic_slice_in_dim(parts, owner[i], 1, axis=0)[0] for i in range(4)])

    seg = jnp.where(segments == 0, 9, segments)
    where = jnp.concatenate([t[None], owner, (f & 1)[None], f[None]]).astype(jnp.int32)
    own_ids = lax.dynamic_slice_in_dim(seg[0], t * rows, rows)
    known = jnp.concatenate([jnp.stack([jnp.sum((own_ids < 9).astype(jnp.int32)), f]), owner]).astype(jnp.int32)
    vectors = jnp.stack([mix_bias, norm_gain, norm_shift, down_bias, final_gain, final_shift])
    shifts = (by_slot(query_bias), by_slot(value_bias))
    slot_of = owner_slot(t)
    goals = [sum(jnp.where(owner[k] == lax.rem(t + shift, 4), k, 0) for k in range(4)) for shift in SHIFTS]
    seg, where, known, vectors, shifts, slot_of, goals = lax.optimization_barrier(
        (seg, where, known, vectors, shifts, slot_of, goals)
    )
    small_operands = (seg, where, known, vectors, *shifts, *slot_of, *goals)

    shard = jnp.stack(
        [
            jnp.concatenate([query_weight, key_weight, value_weight, mix_weight.T], axis=1),
            up_weight,
            down_weight.T,
        ]
    )
    w_a, w_below, w_above = line_first(shard)
    w_c = after(line_second(w_below, w_above), *small_operands)
    w_b = line_third(w_c, w_below)
    w_slots = (shard, w_a, w_c, w_b)
    x_a, x_below, x_above = line_first(after(tokens, w_c))

    def half(first, last):
        line = [w[0][:, m * cols : (m + 1) * cols] for m in (first, first + 1) for w in w_slots]
        return jnp.concatenate(line + [w[last] for w in w_slots], axis=1)

    own = (half(0, 1), half(2, 2))
    bits = outer_bits()
    orders = (bits, bits[::-1])
    held = [{0: own[0]}, {0: own[1]}]
    passed = []

    def pass_on(step):
        arrived = []
        for i in range(2):
            bit = orders[i][step]
            for place in sorted(held[i]):
                got = lax.ppermute(held[i][place], "fsdp", partner(bit))
                arrived.append((i, place | (bit >> 1), got))
        return arrived

    def keep(arrived, *gate):
        values = after(tuple(a[2] for a in arrived), *gate)
        for (i, place, _), value in zip(arrived, values):
            held[i][place] = value
        passed.append(values)

    def to_partner(values, *gate):
        return after(tuple(lax.ppermute(v, "fsdp", partner(1)) for v in values), *gate)

    first = pass_on(0)
    direct = []
    if len(bits) == 2:
        direct = [
            (i, orders[i][1] >> 1, lax.ppermute(own[i], "fsdp", partner(orders[i][1]))) for i in range(2)
        ]
    far_own = to_partner(own)
    keep(first, x_a)
    x_c = line_second(*after((x_below, x_above), *far_own))
    if direct:
        forwarded = [
            (i, 3, lax.ppermute(held[i][orders[i][0] >> 1], "fsdp", partner(orders[i][1]))) for i in range(2)
        ]
        far_first = to_partner(passed[0])
        keep(direct, x_c, *far_own)
        x_b = line_third(x_c, x_below, *far_first)
        far_direct = to_partner(passed[1])
        keep(forwarded)
        far_last = to_partner(passed[2])
        far = [{0: far_own[i], orders[i][0] >> 1: far_first[i]} for i in range(2)]
        for i in range(2):
            far[i][orders[i][1] >> 1], far[i][3] = far_direct[i], far_last[i]
    else:
        x_b = line_third(x_c, x_below)
        for step in range(1, len(bits)):
            keep(pass_on(step))
        far = [dict(zip(sorted(h), to_partner([h[p] for p in sorted(h)]))) for h in held]
    pieces = [[h[p] for h in (near, away) for p in sorted(near)] for near, away in zip(held, far)]
    if r % 16:
        pieces = [[assembled(p)] for p in pieces]

    xs = (tokens, x_a, x_c, x_b)
    q, k, v, ctx, lse, w_all = attend_forward(xs, pieces, shifts, seg, where)
    weights = tuple((w_all, m) for m in range(3))

    layer_out, g_first, g_ctx, lefts, rights, extra = middle(
        known, pieces, ctx, tokens, out_grad, vectors, up_bias.reshape(4, units)
    )
    place = f.astype(jnp.int32)[None]
    kept, sent = ffn_grads(place, lefts, rights, n)
    if r % 16:
        full = jnp.concatenate([kept, sent]).reshape(n, r, -1)
        kept, sent = (
            jnp.concatenate([lax.dynamic_slice_in_dim(full, f ^ (2 * q + c), 1)[0] for q in range(n // 2)])
            for c in range(2)
        )
    got = lax.ppermute(sent, "fsdp", partner(1))
    g_ctx = after(g_ctx, sent)

    args = (q, k, v, g_ctx, ctx, lse)
    dk_n, dv_n, dq, dx_n = attend_backward(*args, (3, 2, 1), weights, seg, where)
    dx_b, dx_c, dx_a = (dx_n[i * rows : (i + 1) * rows] for i in range(3))
    r1 = lax.ppermute(dx_b, "tensor", [(0, 1), (3, 2)])
    steps = list(zip(outer_bits(), outer_bits()[::-1]))
    got = after(got, dx_n)
    held = [outer_axes(kept[:, : 4 * units]), outer_axes(kept[:, 4 * units :])]
    come = [outer_axes(got[:, : 4 * units])[0], outer_axes(got[:, 4 * units :])[0]]
    lefts = [h[1] for h in held]
    held = [h[0] for h in held]
    axes = [left.index(bit) for left, bit in zip(lefts, steps[0])]

    def at(blocks, index):
        return [lax.index_in_dim(b, index, axis, keepdims=False) for b, axis in zip(blocks, axes)]

    out_halves = add_low(at(held, 1), at(come, 1))
    arrived = [lax.ppermute(o, "fsdp", partner(bit)) for o, bit in zip(out_halves, steps[0])]
    dk_o, dv_o, dq, dx_own = attend_backward(
        *args, (0,), weights, seg, where, after(dq, dx_b, *out_halves), g_first
    )
    middle_x = (dx_c.astype(F32) + after(r1, dx_own).astype(F32)).astype(BF)
    rx = lax.ppermute(middle_x, "tensor", [(0, 1), (3, 2)])
    ry = lax.ppermute(middle_x, "tensor", [(1, 2), (2, 1)])

    arrived = after(arrived, dx_own)
    blocks = [
        (a.astype(F32) + b.astype(F32) + c.astype(F32)).astype(BF)
        for a, b, c in zip(at(held, 0), at(come, 0), arrived)
    ]
    lefts = [[b for b in left if b != bit] for left, bit in zip(lefts, steps[0])]
    halves, out_halves = start_halving(blocks, lefts, steps[1])

    xs = (xs[0], xs[3], xs[2], xs[1])
    dq = after(dq, middle_x, *out_halves)
    sent, kept = attn_grads(where[5:6], xs, dq, extra, (dk_o, dk_n), (dv_o, dv_n), n)
    if r % 16:
        split = sent.reshape(3, n // 2, 2, r, width)
        sums = jnp.broadcast_to(kept, (n // 2, EXTRA, width))
        sent, kept = (
            jnp.concatenate(
                [
                    lax.dynamic_index_in_dim(split, c, 2, keepdims=False)
                    .transpose(1, 0, 2, 3)
                    .reshape(n // 2, 3 * r, width),
                    sums,
                ],
                axis=1,
            )
            for c in (1 - (f & 1), f & 1)
        )
        sent = sent.astype(BF)
    got = lax.ppermute(sent, "fsdp", partner(1))
    near = (kept + got.astype(F32)).astype(BF)
    rx, ry = (a.astype(F32) for a in after((rx, ry), sent))
    up_x = (dx_a.astype(F32) + jnp.where(t == 1, rx, ry)).astype(BF)
    down_x = jnp.where(t == 3, dx_a.astype(F32), dx_b.astype(F32) + jnp.where(t == 1, ry, rx)).astype(BF)
    from_below = lax.ppermute(up_x, "tensor", [(0, 1), (1, 2), (2, 3)])
    from_above = lax.ppermute(down_x, "tensor", [(1, 0), (2, 1), (3, 2)])

    d_one, d_two = add_low(halves[0], after(halves[1], sent))
    for pair in steps[2:]:
        halves, _ = start_halving([d_one, d_two], halves[2], pair)
        d_one, d_two = add_low(halves[0], halves[1])
    early = jnp.stack(
        [
            jnp.concatenate(
                [
                    d_one[:, i * units : (i + 1) * units],
                    d_two[:, i * units : (i + 1) * units],
                    d_two[:, 4 * units + i * cols : 4 * units + (i + 1) * cols],
                ],
                axis=1,
            )
            for i in range(4)
        ]
    )

    early_own, early = early[0], spread(early, goals)
    same_core = [list(range(c, n, 2)) for c in range(2)]
    arrived = lax.all_to_all(near, "fsdp", split_axis=0, concat_axis=0, axis_index_groups=same_core, tiled=True)
    arrived = after(arrived, *early)
    late = jnp.sum(arrived.astype(F32), axis=0).astype(BF)
    count = 12
    by_head = jnp.stack([late[3 * r : 3 * r + 2, i * cols : (i + 1) * cols] for i in range(4)])
    by_head = in_line_order(by_head, slot_of).reshape(8, cols)
    whole = [late[3 * r + 2 : 3 * r + count, i * cols : (i + 1) * cols] for i in range(4)]
    below = jnp.concatenate([by_head, *whole])
    late = jnp.stack(
        [jnp.concatenate([late[: 3 * r, i * cols : (i + 1) * cols], below]) for i in range(4)]
    )
    late = total(late[0], spread(late, goals))
    early = total(early_own, early)
    tokens_grad = dx_own + from_below.astype(F32) + from_above.astype(F32)
    qv = late[3 * r : 3 * r + 8].reshape(4, 2, cols).transpose(1, 0, 2).reshape(2, width)
    sums = late[3 * r + 8 :].reshape(4, count - 2, cols).transpose(1, 0, 2).reshape(count - 2, width)
    up_sums = sums[6:].reshape(-1)
    late = late[: 3 * r].reshape(3, r, cols)

    return (
        layer_out,
        tokens_grad,
        late[0],
        qv[0],
        late[1],
        late[2],
        qv[1],
        early[:, 2 * units :].T,
        sums[0],
        sums[1],
        sums[2],
        early[:, units : 2 * units],
        up_sums,
        early[:, :units].T,
        sums[3],
        sums[4],
        sums[5],
    )


def solution(mesh):
    both, rows_f, square, flipped = (
        P(("fsdp", "tensor"), None),
        P("fsdp", None),
        P("fsdp", "tensor"),
        P("tensor", "fsdp"),
    )
    return jax.shard_map(
        on_device,
        mesh=mesh,
        in_specs=(
            both, rows_f, square, P(), square, square, P(), flipped, P(), P(), P(),
            square, P(), flipped, P(), P(), P(), both,
        ),
        out_specs=(
            both, both, square, P(), square, square, P(), flipped, P(), P(), P(),
            square, P(), flipped, P(), P(), P(),
        ),
        check_vma=False,
    )
```

```python
from functools import partial

import jax
import jax.numpy as jnp
from jax import lax
from jax.experimental import pallas as pl
from jax.experimental.pallas import tpu as pltpu
from jax.sharding import PartitionSpec as P

HD = 64
GROUP = 256
BLOCK = 256
EPSILON = 1e-05
MASKED = -1e30
LOG2E = 1.4426950408889634
SCORE = HD**-0.5 * LOG2E
EXTRA = 16
SHIFTS = (1, 3, 2)
FEW = 1000
BF = jnp.bfloat16
F32 = jnp.float32


def after(value, *others):
    return lax.optimization_barrier((value,) + others)[0] if others else value


def nt(a, b):
    return lax.dot_general(a, b, (((1,), (1,)), ((), ())), preferred_element_type=F32)


def nn(a, b):
    return lax.dot_general(a, b, (((1,), (0,)), ((), ())), preferred_element_type=F32)


def line_first(own):
    below = lax.ppermute(own, "tensor", [(0, 1), (1, 2), (2, 3)])
    above = lax.ppermute(own, "tensor", [(1, 0), (2, 1), (3, 2)])
    return jnp.where(lax.axis_index("tensor") < 3, above, below), below, above


def line_second(below, above, *gate):
    below2 = lax.ppermute(below, "tensor", [(1, 2), (2, 3)])
    above2 = lax.ppermute(above, "tensor", [(2, 1), (1, 0)])
    below2, above2 = after((below2, above2), *gate)
    return jnp.where(lax.axis_index("tensor") < 2, above2, below2)


def line_third(slot_c, below, *gate):
    far = after(lax.ppermute(slot_c, "tensor", [(1, 0), (2, 3)]), *gate)
    t = lax.axis_index("tensor")
    return jnp.where((t == 0) | (t == 3), far, below)


def slot_owner(t):
    return jnp.stack([t, jnp.where(t < 3, t + 1, 2), lax.rem(t + 2, 4), jnp.where(t == 3, 0, lax.rem(t + 3, 4))])


def owner_slot(t):
    owner = slot_owner(t)
    return [sum(jnp.where(owner[k] == j, k, 0) for k in range(4)) for j in range(4)]


def in_line_order(slots, slot_of):
    return jnp.concatenate([lax.dynamic_slice_in_dim(slots, s, 1, axis=0) for s in slot_of])


def spread(slots, goals):
    arrived = []
    for shift, slot in zip(SHIFTS, goals):
        block = lax.dynamic_index_in_dim(slots, slot, 0, keepdims=False)
        arrived.append(lax.ppermute(block, "tensor", [(i, (i + shift) % 4) for i in range(4)]))
    return arrived


def total(own, arrived):
    return own.astype(F32) + sum(a.astype(F32) for a in arrived)


def partner(bit):
    n = lax.axis_size("fsdp")
    return [(i, i ^ bit) for i in range(n)]


def outer_bits():
    n = lax.axis_size("fsdp")
    return [1 << k for k in range(1, n.bit_length() - 1)]


def assembled(pieces):
    n = len(pieces)
    f = lax.axis_index("fsdp")
    stacked = jnp.stack(pieces).reshape(2, n // 2, *pieces[0].shape)
    blocks = []
    for a in range(n):
        rel = f ^ a
        block = lax.dynamic_slice_in_dim(stacked, rel & 1, 1, axis=0)
        blocks.append(lax.dynamic_slice_in_dim(block, rel >> 1, 1, axis=1)[0, 0])
    return jnp.concatenate(blocks)


def outer_axes(block):
    n = lax.axis_size("fsdp")
    bits = outer_bits()
    return block.reshape((2,) * len(bits) + (block.shape[0] // (n // 2), block.shape[1])), sorted(bits, reverse=True)


def start_halving(blocks, lefts, pair):
    kept, arrived, rest, sent = [], [], [], []
    for block, left, bit in zip(blocks, lefts, pair):
        axis = left.index(bit)
        kept.append(lax.index_in_dim(block, 0, axis, keepdims=False))
        sent.append(lax.index_in_dim(block, 1, axis, keepdims=False))
        arrived.append(lax.ppermute(sent[-1], "fsdp", partner(bit)))
        rest.append([b for b in left if b != bit])
    return (kept, arrived, rest), sent


def add_low(kept, arrived):
    return [(a.astype(F32) + b.astype(F32)).astype(BF) for a, b in zip(kept, arrived)]


def stack_heads(x):
    lane = lax.broadcasted_iota(jnp.int32, (BLOCK, x.shape[1]), 1)
    zero = jnp.zeros((BLOCK, x.shape[1]), x.dtype)
    heads = x.shape[1] // HD
    return jnp.concatenate(
        [
            jnp.where((lane >= h * HD) & (lane < (h + 1) * HD), x[j * BLOCK : (j + 1) * BLOCK], zero)
            for j in range(x.shape[0] // BLOCK)
            for h in range(heads)
        ],
        axis=0,
    )


def block_kind(seg, q_at, k_at):
    q_lo, q_hi = seg[q_at], seg[q_at + BLOCK - 1]
    k_lo, k_hi = seg[k_at], seg[k_at + BLOCK - 1]
    meet = (q_lo <= k_hi) & (k_lo <= q_hi)
    one = (q_lo == q_hi) & (k_lo == q_lo) & (k_hi == q_lo)
    return jnp.where(one, 2, jnp.where(meet, 1, 0))


def ids_down(ids_refs, col_s):
    rows = ids_refs[0].shape[1]

    @pl.when(pl.program_id(0) == 0)
    def _():
        for j, ids in enumerate(ids_refs):
            wide = jnp.broadcast_to(ids[...].astype(F32), (col_s.shape[1], rows))
            col_s[j * rows : (j + 1) * rows, :] = wide.T


def each_block(seg, where, slots, rows, visit):
    per = rows // BLOCK
    for j, slot in enumerate(slots):

        def step(i, _, j=j, slot=slot):
            kb, qb = i // per, lax.rem(i, per)
            at = pl.ds(pl.multiple_of(kb * BLOCK, BLOCK), BLOCK)
            kind = block_kind(seg, where[0] * rows + qb * BLOCK, where[1 + slot] * rows + kb * BLOCK)
            visit(j, at, kb, qb, kind)
            return 0

        lax.fori_loop(0, per * per, step, 0)


def split_pieces(pieces):
    return [[p[0] for p in half] for half in pieces], tuple(tuple(p[1] for p in half) for half in pieces)


def piece_copy(pieces, offsets, j, f, column, width, target, sem):
    r = pieces[0].shape[0]
    place = 0
    if len(pieces) > 1:
        core, outer = j // (len(pieces) // 2), j % (len(pieces) // 2)
        place = f ^ (2 * outer + core)
    rows = pl.ds(pl.multiple_of(place * r, r), r)
    start = offsets[j] + column * width
    return pltpu.make_async_copy(
        pieces[j].at[:, start : start + width], target.at[rows, :], sem
    )


def lanes(index, size):
    return pl.ds(pl.multiple_of(index * size, size), size)


def forward_kernel(seg, where, *refs, slots, count, offsets):
    refs = list(refs)

    def take(count):
        taken, refs[:] = refs[:count], refs[count:]
        return taken

    x_refs = take(len(slots))
    ids_refs = take(len(slots))
    pieces = (take(count), take(count))
    bq_ref, bv_ref, sq_ref = take(3)
    q_ref, k_ref, v_ref, o_ref, lse_ref, w_ref, q_s, col_s, m_s, l_s, acc_s, ids_s, w_s, sems = refs

    @pl.when(pl.program_id(0) == 0)
    def _():
        copies = [
            piece_copy(pieces[m // 2], offsets[m // 2], j, where[6], m % 2, w_s.shape[2], w_s.at[m], sems.at[m, j])
            for m in range(3)
            for j in range(count)
        ]
        for copy in copies:
            copy.start()
        for copy in copies:
            copy.wait()

    w_ref[...] = w_s[:, :, lanes(pl.program_id(0), q_ref.shape[1])]
    wq_ref, wk_ref, wv_ref = (w_ref.at[m] for m in range(3))
    rows, width = q_ref.shape
    heads = width // HD
    wide = heads * BLOCK
    q_ref[...] = (nn(x_refs[0][...], wq_ref[...]) + bq_ref[...]).astype(BF)
    m_s[...] = jnp.full(m_s.shape, MASKED, F32)
    l_s[...] = jnp.zeros(l_s.shape, F32)
    acc_s[...] = jnp.zeros(acc_s.shape, F32)
    for j, x_ref in enumerate(x_refs):
        at = slice(j * rows, (j + 1) * rows)
        k_ref[at, :] = nn(x_ref[...], wk_ref[...]).astype(BF)
        v_ref[at, :] = (nn(x_ref[...], wv_ref[...]) + bv_ref[...]).astype(BF)
    q_s[...] = stack_heads(q_ref[...])
    ids_down(ids_refs, col_s)
    ids_s[...] = sq_ref[...].astype(F32)

    def block(at, qb, masked):
        stacked, part = lanes(qb, wide), lanes(qb, BLOCK)
        s = nt(k_ref[at, :], q_s[stacked, :])
        if masked:
            same = col_s[at, 0:1] == ids_s[:, part]
            s = jnp.where(jnp.concatenate([same] * heads, axis=1), s, MASKED)
        m_old = m_s[:, stacked]
        m_new = jnp.maximum(m_old, jnp.max(s, axis=0, keepdims=True))
        alpha = jnp.exp2((m_old - m_new) * SCORE)
        p = jnp.exp2((s - m_new) * SCORE)
        p_low = p.astype(BF)
        l_s[:, stacked] = alpha * l_s[:, stacked] + jnp.sum(p, axis=0, keepdims=True)
        m_s[:, stacked] = m_new
        v_t = v_ref[at, :].T
        for h in range(heads):
            hs, qs = slice(h * HD, (h + 1) * HD), slice(h * BLOCK, (h + 1) * BLOCK)
            acc_s[hs, part] = acc_s[hs, part] * alpha[:, qs] + nn(v_t[hs], p_low[:, qs])

    def visit(j, _, kb, qb, kind):
        at = pl.ds(pl.multiple_of(j * rows + kb * BLOCK, BLOCK), BLOCK)
        pl.when(kind == 1)(lambda: block(at, qb, True))
        pl.when(kind == 2)(lambda: block(at, qb, False))

    each_block(seg, where, slots, rows, visit)
    for j in range(rows // BLOCK):
        inverse = 1.0 / l_s[:, j * wide : (j + 1) * wide]
        spread_out = jnp.concatenate(
            [jnp.broadcast_to(inverse[:, h * BLOCK : (h + 1) * BLOCK], (HD, BLOCK)) for h in range(heads)], axis=0
        )
        at = slice(j * BLOCK, (j + 1) * BLOCK)
        o_ref[at, :] = (acc_s[:, at] * spread_out).T.astype(BF)
    lse_ref[0] = m_s[...] * SCORE + jnp.log2(l_s[...])


def attend_forward(xs, pieces, biases, seg, where):
    rows, width = xs[0].shape
    slots = tuple(range(len(xs)))
    keys = rows * len(xs)
    count = len(pieces[0])
    pieces, offsets = split_pieces(pieces)
    groups, wide = width // GROUP, GROUP // HD * rows
    block_spec = pl.BlockSpec((rows, GROUP), lambda i, s, w: (0, i))
    keys_spec = pl.BlockSpec((keys, GROUP), lambda i, s, w: (0, i))
    b_spec = pl.BlockSpec((1, GROUP), lambda i, s, w: (0, i))
    row_spec = pl.BlockSpec((1, 1, wide), lambda i, s, w: (i, 0, 0))
    block_shape = jax.ShapeDtypeStruct((rows, width), BF)
    keys_shape = jax.ShapeDtypeStruct((keys, width), BF)

    def ids_spec(entry):
        return pl.BlockSpec((1, rows), lambda i, s, w: (0, w[entry]))

    in_specs = [pl.BlockSpec((rows, width), lambda i, s, w: (0, 0))] * len(xs)
    in_specs += [ids_spec(1 + s) for s in slots] + [pl.BlockSpec(memory_space=pl.ANY)] * (2 * count) + [b_spec] * 2 + [ids_spec(0)]
    return pl.pallas_call(
        partial(forward_kernel, slots=slots, count=count, offsets=offsets),
        out_shape=(
            block_shape,
            keys_shape,
            keys_shape,
            block_shape,
            jax.ShapeDtypeStruct((groups, 1, wide), F32),
            jax.ShapeDtypeStruct((3, width, width), BF),
        ),
        grid_spec=pltpu.PrefetchScalarGridSpec(
            num_scalar_prefetch=2,
            grid=(groups,),
            in_specs=in_specs,
            out_specs=[
                block_spec, keys_spec, keys_spec, block_spec, row_spec,
                pl.BlockSpec((3, width, GROUP), lambda i, s, w: (0, 0, i)),
            ],
            scratch_shapes=[
                pltpu.VMEM((wide, GROUP), BF),
                pltpu.VMEM((keys, 128), F32),
                pltpu.VMEM((1, wide), F32),
                pltpu.VMEM((1, wide), F32),
                pltpu.VMEM((GROUP, rows), F32),
                pltpu.VMEM((1, rows), F32),
                pltpu.VMEM((3, width, width), BF),
                pltpu.SemaphoreType.DMA((3, count)),
            ],
        ),
        cost_estimate=pl.CostEstimate(flops=FEW, bytes_accessed=FEW, transcendentals=0),
        name="attend_forward",
    )(seg[0], where, *xs, *([seg] * len(slots)), *pieces[0], *pieces[1], *(b[None, :] for b in biases), seg)


def backward_kernel(seg, where, *refs, slots, first, last):
    refs = list(refs)

    def take(count):
        taken, refs[:] = refs[:count], refs[count:]
        return taken

    q_ref, do_ref, o_ref, lse_ref, wk_ref, wv_ref, sq_ref = take(7)
    k_refs, v_refs, ids_refs = take(len(slots)), take(len(slots)), take(len(slots))
    if not first:
        (dq_in,) = take(1)
    if last:
        wq_ref, base_ref = take(2)
        dk_s, dv_s, dq_ref, dx_ref, q_s, do_s, delta_s, col_s, ids_s, dx_s, dq_s = refs
    else:
        dk_s, dv_s, dq_s, dx_ref, q_s, do_s, delta_s, col_s, ids_s, dx_s = refs
    g = pl.program_id(0)
    ids_down(ids_refs, col_s)
    ids_s[...] = sq_ref[...].astype(F32)
    rows, width = q_ref.shape
    heads = width // HD
    wide = heads * BLOCK
    q_s[...] = stack_heads(q_ref[...])
    do_s[...] = stack_heads(do_ref[...])
    prod = (do_ref[...].astype(F32) * o_ref[...].astype(F32)).T
    for j in range(rows // BLOCK):
        for h in range(heads):
            piece = prod[h * HD : (h + 1) * HD, j * BLOCK : (j + 1) * BLOCK]
            delta_s[:, j * wide + h * BLOCK : j * wide + (h + 1) * BLOCK] = jnp.sum(piece, axis=0, keepdims=True)
    dq_s[...] = jnp.zeros_like(dq_s) if first else dq_in[...]

    def block(j, at, out_at, qb, masked):
        stacked, part = lanes(qb, wide), lanes(qb, BLOCK)
        k = k_refs[j][at, :]
        k_t = k.T
        s = nt(k, q_s[stacked, :]) * SCORE - lse_ref[0, :, stacked]
        if masked:
            same = col_s[out_at, 0:1] == ids_s[:, part]
            s = jnp.where(jnp.concatenate([same] * heads, axis=1), s, MASKED)
        p = jnp.exp2(s)
        dp = nt(v_refs[j][at, :], do_s[stacked, :])
        ds = (p * (dp - delta_s[:, stacked])).astype(BF)
        dv = nn(p.astype(BF), do_s[stacked, :])
        dk = nn(ds, q_s[stacked, :])
        for h in range(heads):
            hs = slice(h * HD, (h + 1) * HD)
            dq_s[hs, part] += nn(k_t[hs], ds[:, h * BLOCK : (h + 1) * BLOCK])
        return dk, dv

    def visit(j, at, kb, qb, kind):
        out_at = pl.ds(pl.multiple_of(j * rows + kb * BLOCK, BLOCK), BLOCK)

        @pl.when(qb == 0)
        def _():
            acc_k[...] = jnp.zeros(acc_k.shape, F32)
            acc_v[...] = jnp.zeros(acc_v.shape, F32)

        def add(masked):
            dk, dv = block(j, at, out_at, qb, masked)
            acc_k[...] += dk
            acc_v[...] += dv

        pl.when(kind == 1)(lambda: add(True))
        pl.when(kind == 2)(lambda: add(False))

        @pl.when(qb == rows // BLOCK - 1)
        def _():
            dk_s[out_at, :] = (acc_k[...] * HD**-0.5).astype(BF)
            dv_s[out_at, :] = acc_v[...].astype(BF)

    def scoped(acc_k_ref, acc_v_ref):
        nonlocal acc_k, acc_v
        acc_k, acc_v = acc_k_ref, acc_v_ref
        each_block(seg, where, slots, rows, visit)

    acc_k = acc_v = None
    pl.run_scoped(scoped, pltpu.VMEM((BLOCK, width), F32), pltpu.VMEM((BLOCK, width), F32))

    if last:
        dq_ref[...] = (dq_s[...] * HD**-0.5).T.astype(BF)
    for j in range(len(slots)):
        at = slice(j * rows, (j + 1) * rows)
        dx = nt(dk_s[at, :], wk_ref[...]) + nt(dv_s[at, :], wv_ref[...])
        if last and j == 0:
            dx = dx + nt(dq_ref[...], wq_ref[...])

        @pl.when(g == 0)
        def _(at=at, dx=dx, j=j):
            dx_s[at, :] = dx + base_ref[...] if last and j == 0 else dx

        @pl.when(g > 0)
        def _(at=at, dx=dx):
            dx_s[at, :] += dx

    @pl.when(g == pl.num_programs(0) - 1)
    def _():
        dx_ref[...] = dx_s[...].astype(dx_ref.dtype)


def attend_backward(q, k, v, do, o, lse, slots, weights, seg, where, dq=None, base=None):
    rows, width = q.shape
    keys = rows * len(slots)
    first, last = dq is None, base is not None
    groups, wide = width // GROUP, GROUP // HD * rows
    q_spec = pl.BlockSpec((rows, GROUP), lambda i, s, w: (0, i))
    wq_spec, wk_spec, wv_spec = (
        pl.BlockSpec((None, width, GROUP), lambda i, s, w, m=m: (m, 0, i)) for _, m in weights
    )
    row_spec = pl.BlockSpec((1, 1, wide), lambda i, s, w: (i, 0, 0))
    acc_spec = pl.BlockSpec((GROUP, rows), lambda i, s, w: (i, 0))
    keys_spec = pl.BlockSpec((keys, GROUP), lambda i, s, w: (0, i))

    def ids_spec(entry):
        return pl.BlockSpec((1, rows), lambda i, s, w: (0, w[entry]))

    def slot_spec(slot):
        return pl.BlockSpec((rows, GROUP), lambda i, s, w: (slot, i))

    wq, wk, wv = (a for a, _ in weights)
    count = len(slots)
    ins = [q, do, o, lse, wk, wv, seg] + [k] * count + [v] * count + [seg] * count
    in_specs = [q_spec, q_spec, q_spec, row_spec, wk_spec, wv_spec, ids_spec(0)]
    in_specs += [slot_spec(s) for s in slots] * 2 + [ids_spec(1 + s) for s in slots]
    if not first:
        ins.append(dq)
        in_specs.append(acc_spec)
    scratch = [pltpu.VMEM((wide, GROUP), BF), pltpu.VMEM((wide, GROUP), BF), pltpu.VMEM((1, wide), F32)]
    scratch += [pltpu.VMEM((keys, 128), F32), pltpu.VMEM((1, rows), F32), pltpu.VMEM((keys, width), F32)]
    if last:
        ins += [wq, base]
        in_specs += [wq_spec, pl.BlockSpec((rows, width), lambda i, s, w: (0, 0))]
        scratch.append(pltpu.VMEM((GROUP, rows), F32))
    keys_shape = jax.ShapeDtypeStruct((keys, width), BF)
    results = [
        (keys_spec, keys_shape),
        (keys_spec, keys_shape),
        (q_spec, jax.ShapeDtypeStruct((rows, width), BF))
        if last
        else (acc_spec, jax.ShapeDtypeStruct((width, rows), F32)),
        (
            pl.BlockSpec((keys, width), lambda i, s, w: (0, 0)),
            jax.ShapeDtypeStruct((keys, width), F32 if last else BF),
        ),
    ]
    return pl.pallas_call(
        partial(backward_kernel, slots=slots, first=first, last=last),
        out_shape=tuple(r[1] for r in results),
        grid_spec=pltpu.PrefetchScalarGridSpec(
            num_scalar_prefetch=2,
            grid=(groups,),
            in_specs=in_specs,
            out_specs=[r[0] for r in results],
            scratch_shapes=scratch,
        ),
        cost_estimate=pl.CostEstimate(flops=FEW, bytes_accessed=FEW, transcendentals=0),
        name="attend_backward",
    )(seg[0], where, *ins)


def attn_grad_kernel(core_ref, *refs, calls, slots, block_rows):
    x_refs, dq_ref, extra_ref, refs = refs[:slots], refs[slots], refs[slots + 1], refs[slots + 2 :]
    dk_refs, dv_refs, refs = refs[:calls], refs[calls : 2 * calls], refs[2 * calls :]
    first_ref, second_ref, x_s, w_s = refs
    rows = dq_ref.shape[0]

    @pl.when(pl.program_id(0) == 0)
    def _():
        for j, x_ref in enumerate(x_refs):
            x_s[:, j * rows : (j + 1) * rows] = x_ref[...].T

    sums = [
        jnp.sum(dq_ref[...].astype(F32), axis=0, keepdims=True),
        sum(jnp.sum(d[...].astype(F32), axis=0, keepdims=True) for d in dv_refs),
        extra_ref[...],
        jnp.zeros((EXTRA - 2 - extra_ref.shape[0], w_s.shape[1]), F32),
    ]
    sums = jnp.concatenate(sums, axis=0)

    def over_keys(parts):
        total, start = 0.0, 0
        for d in parts:
            total = total + nn(x_s[:, start : start + d.shape[0]], d[...])
            start += d.shape[0]
        return total

    for m, parts in enumerate(((dq_ref,), dk_refs, dv_refs)):
        if not block_rows:
            first_ref[m] = over_keys(parts)
            continue
        w_s[...] = over_keys(parts)
        core = core_ref[0]
        at = slice(m * block_rows, (m + 1) * block_rows)
        for b in range(first_ref.shape[0]):
            far = pl.multiple_of((2 * b + 1 - core) * block_rows, block_rows)
            near = pl.multiple_of((2 * b + core) * block_rows, block_rows)
            first_ref[b, at] = w_s[pl.ds(far, block_rows), :].astype(BF)
            second_ref[b, at] = w_s[pl.ds(near, block_rows), :]
    if block_rows:
        for b in range(first_ref.shape[0]):
            first_ref[b, 3 * block_rows :] = sums.astype(BF)
            second_ref[b, 3 * block_rows :] = sums
    else:
        second_ref[...] = sums


def attn_grads(core, xs, dq, extra, dks, dvs, n):
    rows, width = dq.shape
    block_rows = width // n if (width // n) % 16 == 0 else 0
    x_spec = pl.BlockSpec((rows, width), lambda i, c: (0, 0))

    def d_spec(d):
        return pl.BlockSpec((d.shape[0], GROUP), lambda i, c: (0, i))

    if block_rows:
        shape = (n // 2, 3 * block_rows + EXTRA)
        spec = pl.BlockSpec((*shape, GROUP), lambda i, c: (0, 0, i))
        results = [(spec, jax.ShapeDtypeStruct((*shape, width), t)) for t in (BF, F32)]
    else:
        spec = pl.BlockSpec((3, width, GROUP), lambda i, c: (0, 0, i))
        results = [(spec, jax.ShapeDtypeStruct((3, width, width), F32))]
        spec = pl.BlockSpec((EXTRA, GROUP), lambda i, c: (0, i))
        results.append((spec, jax.ShapeDtypeStruct((EXTRA, width), F32)))
    return pl.pallas_call(
        partial(attn_grad_kernel, calls=len(dks), slots=len(xs), block_rows=block_rows),
        out_shape=tuple(r[1] for r in results),
        grid_spec=pltpu.PrefetchScalarGridSpec(
            num_scalar_prefetch=1,
            grid=(width // GROUP,),
            in_specs=[x_spec] * len(xs) + [d_spec(d) for d in (dq, extra, *dks, *dvs)],
            out_specs=[r[0] for r in results],
            scratch_shapes=[pltpu.VMEM((width, rows * len(xs)), BF), pltpu.VMEM((width, GROUP), F32)],
        ),
        cost_estimate=pl.CostEstimate(flops=FEW, bytes_accessed=FEW, transcendentals=0),
        name="attn_grads",
    )(core, *xs, dq, extra, *dks, *dvs)


def norm_parts(rows_in):
    mean = jnp.mean(rows_in, axis=-1, keepdims=True)
    centred = rows_in - mean
    spread = jnp.mean(centred * centred, axis=-1, keepdims=True)
    r = lax.rsqrt(spread + EPSILON)
    return centred * r, r


def norm_back(g_y, n, r, gain):
    e = g_y * gain
    return r * (e - jnp.mean(e, axis=-1, keepdims=True) - n * jnp.mean(e * n, axis=-1, keepdims=True))


def gelu_parts(u):
    c = 0.7978845608028654
    square = u * u
    th = jnp.tanh(c * u * (1.0 + 0.044715 * square))
    half = 0.5 * (1.0 + th)
    slope = half + 0.5 * u * (1.0 - th * th) * (c + 3 * 0.044715 * c * square)
    return u * half, slope


def down_rows(x):
    return jnp.sum(x, axis=0, keepdims=True)


def middle_kernel(known, *refs, count, offsets):
    w_refs, refs = (refs[:count], refs[count : 2 * count]), refs[2 * count :]
    ctx_ref, x_ref, grad_ref, vec_ref, bias_ref = refs[:5]
    out_ref, first_ref, gctx_ref, lefts_ref, rights_ref, sums_ref = refs[5:11]
    w_s, mix_ref, slope_s, n1_s, r1_s, acc_s, sems, mix_sems = refs[11:]
    parts, units = bias_ref.shape
    rows, width = x_ref.shape

    def copy(which, t, j):
        return piece_copy(
            w_refs[which], offsets[which], j, known[1], 2 * width // units + t, units, w_s.at[which, t], sems.at[which, t, j]
        )

    mix_copies = [
        piece_copy(w_refs[1], offsets[1], j, known[1], 1, width, mix_ref, mix_sems.at[j]) for j in range(count)
    ]
    for mix_copy in mix_copies:
        mix_copy.start()
    for which in range(2):
        for t in range(parts):
            for j in range(count):
                copy(which, t, j).start()
    for mix_copy in mix_copies:
        mix_copy.wait()

    def cols(t):
        return pl.ds(pl.multiple_of(t * units, units), units)

    first_sum = x_ref[...].astype(F32) + nt(ctx_ref[...], mix_ref[...]) + vec_ref[0:1, :]
    n1, r1 = norm_parts(first_sum)
    n1_s[...] = n1
    r1_s[...] = jnp.broadcast_to(r1, r1_s.shape)
    acc_s[...] = n1 * vec_ref[1:2, :] + vec_ref[2:3, :]
    lefts_ref[1] = acc_s[...].astype(BF)

    for which in range(2):
        for t in range(parts):
            for j in range(count):
                copy(which, t, j).wait()

    def up(t, _):
        pre = nn(lefts_ref[1], w_s[0, t]) + bias_ref[pl.ds(known[2 + t], 1), :]
        act, slope = gelu_parts(pre)
        slope_s[t] = slope
        low = act.astype(BF)
        rights_ref[:, cols(t)] = low
        acc_s[...] += nt(low, w_s[1, t])
        return 0

    lax.fori_loop(0, parts, up, 0)
    n2, r2 = norm_parts(acc_s[...] + vec_ref[3:4, :])
    out_ref[...] = (n2 * vec_ref[4:5, :] + vec_ref[5:6, :]).astype(BF)
    row = lax.broadcasted_iota(jnp.int32, (rows, width), 0)
    g_out = jnp.where(row < known[0], grad_ref[...].astype(F32), 0.0)
    g_second = norm_back(g_out, n2, r2, vec_ref[4:5, :])
    sums_ref[3:4, :] = down_rows(g_second)
    sums_ref[4:5, :] = down_rows(g_out * n2)
    sums_ref[5:6, :] = down_rows(g_out)
    lefts_ref[0] = g_second.astype(BF)
    acc_s[...] = g_second

    def back(t, _):
        g_pre = (nn(lefts_ref[0], w_s[1, t]) * slope_s[t]).astype(BF)
        rights_ref[:, cols(parts + t)] = g_pre
        sums_ref[pl.ds(6 + known[2 + t], 1), :] = down_rows(g_pre.astype(F32))
        acc_s[...] += nt(g_pre, w_s[0, t])
        return 0

    lax.fori_loop(0, parts, back, 0)
    g_normed = acc_s[...]
    n1 = n1_s[...]
    g_first = norm_back(g_normed, n1, r1_s[:, 0:1], vec_ref[1:2, :])
    sums_ref[0:1, :] = down_rows(g_first)
    sums_ref[1:2, :] = down_rows(g_normed * n1)
    sums_ref[2:3, :] = down_rows(g_normed)
    first_ref[...] = g_first
    low = g_first.astype(BF)
    lefts_ref[2] = low
    gctx_ref[...] = nn(low, mix_ref[...]).astype(BF)
    rights_ref[:, 2 * parts * units :] = ctx_ref[...]


def middle(known, pieces, ctx, x, grad, vectors, bias):
    rows, width = x.shape
    parts, units = bias.shape
    count = len(pieces[0])
    pieces, offsets = split_pieces(pieces)
    vmem = pl.BlockSpec(memory_space=pltpu.VMEM)
    shapes = [
        ((rows, width), BF),
        ((rows, width), F32),
        ((rows, width), BF),
        ((3, rows, width), BF),
        ((rows, 2 * parts * units + width), BF),
        ((6 + parts, width), F32),
    ]
    return pl.pallas_call(
        partial(middle_kernel, count=count, offsets=offsets),
        out_shape=tuple(jax.ShapeDtypeStruct(*s) for s in shapes),
        in_specs=[pl.BlockSpec(memory_space=pltpu.SMEM)] + [pl.BlockSpec(memory_space=pl.ANY)] * (2 * count) + [vmem] * 5,
        out_specs=[vmem] * len(shapes),
        scratch_shapes=[
            pltpu.VMEM((2, parts, width, units), BF),
            pltpu.VMEM((width, width), BF),
            pltpu.VMEM((parts, rows, units), F32),
            pltpu.VMEM((rows, width), F32),
            pltpu.VMEM((rows, 128), F32),
            pltpu.VMEM((rows, width), F32),
            pltpu.SemaphoreType.DMA((2, parts, count)),
            pltpu.SemaphoreType.DMA((count,)),
        ],
        compiler_params=pltpu.CompilerParams(vmem_limit_bytes=63 << 20),
        cost_estimate=pl.CostEstimate(flops=FEW, bytes_accessed=FEW, transcendentals=0),
        name="middle",
    )(known, *pieces[0], *pieces[1], ctx, x, grad, vectors, bias)


def ffn_grad_kernel(place, left_ref, right_ref, kept_ref, sent_ref, left_s, chosen_s, *, n):
    half = kept_ref.shape[0]

    @pl.when(pl.program_id(0) % 4 == 0)
    def _():
        left_s[...] = left_ref[0].T
        size = left_s.shape[0] // n
        if size % 16:
            chosen_s[...] = left_s[...]
        else:
            for j in range(n):
                core, outer = j // (n // 2), j % (n // 2)
                block = place[0] ^ (2 * outer + core)
                chosen_s[j * size : (j + 1) * size, :] = left_s[pl.ds(pl.multiple_of(block * size, size), size), :]

    total = nn(chosen_s[...], right_ref[...])
    kept_ref[...] = total[:half].astype(BF)
    sent_ref[...] = total[half:].astype(BF)


def ffn_grads(place, lefts, rights, n):
    _, rows, width = lefts.shape
    units = rights.shape[1] // 9
    out_spec = pl.BlockSpec((width // 2, units), lambda i, p: (0, i))
    out_shape = jax.ShapeDtypeStruct((width // 2, rights.shape[1]), BF)
    return pl.pallas_call(
        partial(ffn_grad_kernel, n=n),
        out_shape=(out_shape, out_shape),
        grid_spec=pltpu.PrefetchScalarGridSpec(
            num_scalar_prefetch=1,
            grid=(9,),
            in_specs=[
                pl.BlockSpec((1, rows, width), lambda i, p: (i // 4, 0, 0)),
                pl.BlockSpec((rows, units), lambda i, p: (0, i)),
            ],
            out_specs=[out_spec, out_spec],
            scratch_shapes=[pltpu.VMEM((width, rows), BF), pltpu.VMEM((width, rows), BF)],
        ),
        cost_estimate=pl.CostEstimate(flops=FEW, bytes_accessed=FEW, transcendentals=0),
        name="ffn_grads",
    )(place, lefts, rights)


def finish_kernel(*refs, r):
    terms, refs = refs[:4], refs[4:]
    total = sum(t[...].astype(F32) for t in terms)
    for m in range(3):
        refs[m][...] = total[m * r : (m + 1) * r]
    base = 3 * r

    def row(*at):
        return jnp.concatenate([total[base + i : base + i + 1] for i in at], axis=1)[0]

    for w in range(2):
        refs[3 + w][...] = row(*(2 * i + w for i in range(4)))
    for j in range(6):
        refs[5 + j][...] = row(*(8 + 10 * i + j for i in range(4)))
    refs[11][...] = row(*(8 + 10 * i + j for j in range(6, 10) for i in range(4)))


def finish(terms, r, width, units):
    cols = terms[0].shape[1]
    shapes = [(r, cols)] * 3 + [(width,)] * 8 + [(4 * units,)]
    vmem = pl.BlockSpec(memory_space=pltpu.VMEM)
    return pl.pallas_call(
        partial(finish_kernel, r=r),
        out_shape=tuple(jax.ShapeDtypeStruct(x, F32) for x in shapes),
        in_specs=[vmem] * 4,
        out_specs=[vmem] * len(shapes),
        cost_estimate=pl.CostEstimate(flops=FEW, bytes_accessed=FEW, transcendentals=0),
        name="finish",
    )(*terms)


def on_device(
    tokens,
    segments,
    query_weight,
    query_bias,
    key_weight,
    value_weight,
    value_bias,
    mix_weight,
    mix_bias,
    norm_gain,
    norm_shift,
    up_weight,
    up_bias,
    down_weight,
    down_bias,
    final_gain,
    final_shift,
    out_grad,
):
    t = lax.axis_index("tensor")
    f = lax.axis_index("fsdp")
    n = lax.axis_size("fsdp")
    rows, width = tokens.shape
    r, units = up_weight.shape
    cols = query_weight.shape[1]
    owner = slot_owner(t)

    def by_slot(vector):
        parts = vector.reshape(4, -1)
        return jnp.concatenate([lax.dynamic_slice_in_dim(parts, owner[i], 1, axis=0)[0] for i in range(4)])

    seg = jnp.where(segments == 0, 9, segments)
    where = jnp.concatenate([t[None], owner, (f & 1)[None], f[None]]).astype(jnp.int32)
    own_ids = lax.dynamic_slice_in_dim(seg[0], t * rows, rows)
    known = jnp.concatenate([jnp.stack([jnp.sum((own_ids < 9).astype(jnp.int32)), f]), owner]).astype(jnp.int32)
    vectors = jnp.stack([mix_bias, norm_gain, norm_shift, down_bias, final_gain, final_shift])
    shifts = (by_slot(query_bias), by_slot(value_bias))
    slot_of = owner_slot(t)
    goals = [sum(jnp.where(owner[k] == lax.rem(t + shift, 4), k, 0) for k in range(4)) for shift in SHIFTS]
    seg, where, known, vectors, shifts, slot_of, goals = lax.optimization_barrier(
        (seg, where, known, vectors, shifts, slot_of, goals)
    )
    small_operands = (seg, where, known, vectors, *shifts, *slot_of, *goals)

    shard = jnp.stack(
        [
            jnp.concatenate([query_weight, key_weight, value_weight, mix_weight.T], axis=1),
            up_weight,
            down_weight.T,
        ]
    )
    w_a, w_below, w_above = line_first(shard)
    w_c = after(line_second(w_below, w_above), *small_operands)
    w_b = line_third(w_c, w_below)
    w_slots = (shard, w_a, w_c, w_b)
    x_a, x_below, x_above = line_first(after(tokens, w_c))

    line = []
    for first, last in ((0, 1), (2, 2)):
        line += [w[0][:, m * cols : (m + 1) * cols] for m in (first, first + 1) for w in w_slots]
        line += [w[last] for w in w_slots]
    own = jnp.concatenate(line, axis=1)
    wide = own.shape[1] // 2
    bits = outer_bits()

    def over(block, bit):
        return lax.ppermute(block, "fsdp", partner(bit))

    if len(bits) == 2:
        beside = [over(own, bit) for bit in bits]
        far_own = over(own, 1)
        x_c = line_second(*after((x_below, x_above), far_own))
        beside = after(beside, x_a, x_c)
        across = [over(beside[0][:, :wide], bits[1]), over(beside[1][:, wide:], bits[0])]
        far_beside = [over(b, 1) for b in beside]
        x_b = line_third(x_c, x_below, *far_beside)
        far_across = [over(a, 1) for a in across]
        pieces = [
            [
                piece
                for o, b, a in ((own, beside, across), (far_own, far_beside, far_across))
                for piece in ((o, i * wide), (b[0], i * wide), (b[1], i * wide), (a[i], 0))
            ]
            for i in range(2)
        ]
    else:
        x_c = line_second(x_below, x_above)
        x_b = line_third(x_c, x_below)
        held = {0: after(own, x_a)}
        for bit in bits:
            held.update({place | (bit >> 1): over(block, bit) for place, block in sorted(held.items())})
        near = [held[p] for p in sorted(held)]
        far = [over(block, 1) for block in near]
        pieces = [[(block, i * wide) for block in near + far] for i in range(2)]
    if r % 16:
        pieces = [[(assembled([p[0][:, p[1] : p[1] + wide] for p in half]), 0)] for half in pieces]

    xs = (tokens, x_a, x_c, x_b)
    q, k, v, ctx, lse, w_all = attend_forward(xs, pieces, shifts, seg, where)
    weights = tuple((w_all, m) for m in range(3))

    layer_out, g_first, g_ctx, lefts, rights, extra = middle(
        known, pieces, ctx, tokens, out_grad, vectors, up_bias.reshape(4, units)
    )
    place = f.astype(jnp.int32)[None]
    kept, sent = ffn_grads(place, lefts, rights, n)
    if r % 16:
        full = jnp.concatenate([kept, sent]).reshape(n, r, -1)
        kept, sent = (
            jnp.concatenate([lax.dynamic_slice_in_dim(full, f ^ (2 * q + c), 1)[0] for q in range(n // 2)])
            for c in range(2)
        )
    got = lax.ppermute(sent, "fsdp", partner(1))
    g_ctx = after(g_ctx, sent)

    args = (q, k, v, g_ctx, ctx, lse)
    dk_n, dv_n, dq, dx_n = attend_backward(*args, (3, 2, 1), weights, seg, where)
    dx_b, dx_c, dx_a = (dx_n[i * rows : (i + 1) * rows] for i in range(3))
    r1 = lax.ppermute(dx_b, "tensor", [(0, 1), (3, 2)])
    steps = list(zip(outer_bits(), outer_bits()[::-1]))
    got = after(got, dx_n)
    held = [outer_axes(kept[:, : 4 * units]), outer_axes(kept[:, 4 * units :])]
    come = [outer_axes(got[:, : 4 * units])[0], outer_axes(got[:, 4 * units :])[0]]
    lefts = [h[1] for h in held]
    held = [h[0] for h in held]
    axes = [left.index(bit) for left, bit in zip(lefts, steps[0])]

    def at(blocks, index):
        return [lax.index_in_dim(b, index, axis, keepdims=False) for b, axis in zip(blocks, axes)]

    out_halves = add_low(at(held, 1), at(come, 1))
    arrived = [lax.ppermute(o, "fsdp", partner(bit)) for o, bit in zip(out_halves, steps[0])]
    dk_o, dv_o, dq, dx_own = attend_backward(
        *args, (0,), weights, seg, where, after(dq, dx_b, *out_halves), g_first
    )
    middle_x = (dx_c.astype(F32) + after(r1, dx_own).astype(F32)).astype(BF)
    rx = lax.ppermute(middle_x, "tensor", [(0, 1), (3, 2)])
    ry = lax.ppermute(middle_x, "tensor", [(1, 2), (2, 1)])

    arrived = after(arrived, dx_own)
    blocks = [
        (a.astype(F32) + b.astype(F32) + c.astype(F32)).astype(BF)
        for a, b, c in zip(at(held, 0), at(come, 0), arrived)
    ]
    lefts = [[b for b in left if b != bit] for left, bit in zip(lefts, steps[0])]
    halves, out_halves = start_halving(blocks, lefts, steps[1])

    xs = (xs[0], xs[3], xs[2], xs[1])
    dq = after(dq, middle_x, *out_halves)
    sent, kept = attn_grads(where[5:6], xs, dq, extra, (dk_o, dk_n), (dv_o, dv_n), n)
    if r % 16:
        split = sent.reshape(3, n // 2, 2, r, width)
        sums = jnp.broadcast_to(kept, (n // 2, EXTRA, width))
        sent, kept = (
            jnp.concatenate(
                [
                    lax.dynamic_index_in_dim(split, c, 2, keepdims=False)
                    .transpose(1, 0, 2, 3)
                    .reshape(n // 2, 3 * r, width),
                    sums,
                ],
                axis=1,
            )
            for c in (1 - (f & 1), f & 1)
        )
        sent = sent.astype(BF)
    got = lax.ppermute(sent, "fsdp", partner(1))
    near = (kept + got.astype(F32)).astype(BF)
    rx, ry = (a.astype(F32) for a in after((rx, ry), sent))
    up_x = (dx_a.astype(F32) + jnp.where(t == 1, rx, ry)).astype(BF)
    down_x = jnp.where(t == 3, dx_a.astype(F32), dx_b.astype(F32) + jnp.where(t == 1, ry, rx)).astype(BF)
    from_below = lax.ppermute(up_x, "tensor", [(0, 1), (1, 2), (2, 3)])
    from_above = lax.ppermute(down_x, "tensor", [(1, 0), (2, 1), (3, 2)])

    d_one, d_two = add_low(halves[0], after(halves[1], sent))
    for pair in steps[2:]:
        halves, _ = start_halving([d_one, d_two], halves[2], pair)
        d_one, d_two = add_low(halves[0], halves[1])
    early = jnp.stack(
        [
            jnp.concatenate(
                [
                    d_one[:, i * units : (i + 1) * units],
                    d_two[:, i * units : (i + 1) * units],
                    d_two[:, 4 * units + i * cols : 4 * units + (i + 1) * cols],
                ],
                axis=1,
            )
            for i in range(4)
        ]
    )

    early_own, early = early[0], spread(early, goals)
    same_core = [list(range(c, n, 2)) for c in range(2)]
    arrived = lax.all_to_all(near, "fsdp", split_axis=0, concat_axis=0, axis_index_groups=same_core, tiled=True)
    arrived = after(arrived, *early)
    late = jnp.sum(arrived.astype(F32), axis=0).astype(BF)
    count = 12
    by_head = jnp.stack([late[3 * r : 3 * r + 2, i * cols : (i + 1) * cols] for i in range(4)])
    by_head = in_line_order(by_head, slot_of).reshape(8, cols)
    whole = [late[3 * r + 2 : 3 * r + count, i * cols : (i + 1) * cols] for i in range(4)]
    below = jnp.concatenate([by_head, *whole])
    late = jnp.stack(
        [jnp.concatenate([late[: 3 * r, i * cols : (i + 1) * cols], below]) for i in range(4)]
    )
    *late, qb, vb, b0, b1, b2, b3, b4, b5, up_sums = finish((late[0], *spread(late, goals)), r, width, units)
    early = total(early_own, early)
    tokens_grad = dx_own + from_below.astype(F32) + from_above.astype(F32)

    return (
        layer_out,
        tokens_grad,
        late[0],
        qb,
        late[1],
        late[2],
        vb,
        early[:, 2 * units :].T,
        b0,
        b1,
        b2,
        early[:, units : 2 * units],
        up_sums,
        early[:, :units].T,
        b3,
        b4,
        b5,
    )


def solution(mesh):
    both, rows_f, square, flipped = (
        P(("fsdp", "tensor"), None),
        P("fsdp", None),
        P("fsdp", "tensor"),
        P("tensor", "fsdp"),
    )
    return jax.shard_map(
        on_device,
        mesh=mesh,
        in_specs=(
            both, rows_f, square, P(), square, square, P(), flipped, P(), P(), P(),
            square, P(), flipped, P(), P(), P(), both,
        ),
        out_specs=(
            both, both, square, P(), square, square, P(), flipped, P(), P(), P(),
            square, P(), flipped, P(), P(), P(),
        ),
        check_vma=False,
    )
```

```python
from functools import partial

import jax
import jax.numpy as jnp
from jax import lax
from jax.experimental import pallas as pl
from jax.experimental.pallas import tpu as pltpu
from jax.sharding import PartitionSpec as P

HD = 64
GROUP = 256
BLOCK = 256
EPSILON = 1e-05
MASKED = -1e30
LOG2E = 1.4426950408889634
SCORE = HD**-0.5 * LOG2E
EXTRA = 16
SHIFTS = (1, 3, 2)
FEW = 1000
BF = jnp.bfloat16
F32 = jnp.float32


def after(value, *others):
    return lax.optimization_barrier((value,) + others)[0] if others else value


def nt(a, b):
    return lax.dot_general(a, b, (((1,), (1,)), ((), ())), preferred_element_type=F32)


def nn(a, b):
    return lax.dot_general(a, b, (((1,), (0,)), ((), ())), preferred_element_type=F32)


def line_first(own):
    below = lax.ppermute(own, "tensor", [(0, 1), (1, 2), (2, 3)])
    above = lax.ppermute(own, "tensor", [(1, 0), (2, 1), (3, 2)])
    return jnp.where(lax.axis_index("tensor") < 3, above, below), below, above


def line_second(below, above, *gate):
    below2 = lax.ppermute(below, "tensor", [(1, 2), (2, 3)])
    above2 = lax.ppermute(above, "tensor", [(2, 1), (1, 0)])
    below2, above2 = after((below2, above2), *gate)
    return jnp.where(lax.axis_index("tensor") < 2, above2, below2)


def line_third(slot_c, below, *gate):
    far = after(lax.ppermute(slot_c, "tensor", [(1, 0), (2, 3)]), *gate)
    t = lax.axis_index("tensor")
    return jnp.where((t == 0) | (t == 3), far, below)


def slot_owner(t):
    return jnp.stack([t, jnp.where(t < 3, t + 1, 2), lax.rem(t + 2, 4), jnp.where(t == 3, 0, lax.rem(t + 3, 4))])


def owner_slot(t):
    owner = slot_owner(t)
    return [sum(jnp.where(owner[k] == j, k, 0) for k in range(4)) for j in range(4)]


def in_line_order(slots, slot_of):
    return jnp.concatenate([lax.dynamic_slice_in_dim(slots, s, 1, axis=0) for s in slot_of])


def spread(slots, goals):
    arrived = []
    for shift, slot in zip(SHIFTS, goals):
        block = lax.dynamic_index_in_dim(slots, slot, 0, keepdims=False)
        arrived.append(lax.ppermute(block, "tensor", [(i, (i + shift) % 4) for i in range(4)]))
    return arrived


def total(own, arrived):
    return own.astype(F32) + sum(a.astype(F32) for a in arrived)


def partner(bit):
    n = lax.axis_size("fsdp")
    return [(i, i ^ bit) for i in range(n)]


def outer_bits():
    n = lax.axis_size("fsdp")
    return [1 << k for k in range(1, n.bit_length() - 1)]


def assembled(pieces):
    n = len(pieces)
    f = lax.axis_index("fsdp")
    stacked = jnp.stack(pieces).reshape(2, n // 2, *pieces[0].shape)
    blocks = []
    for a in range(n):
        rel = f ^ a
        block = lax.dynamic_slice_in_dim(stacked, rel & 1, 1, axis=0)
        blocks.append(lax.dynamic_slice_in_dim(block, rel >> 1, 1, axis=1)[0, 0])
    return jnp.concatenate(blocks)


def outer_axes(block):
    n = lax.axis_size("fsdp")
    bits = outer_bits()
    return block.reshape((2,) * len(bits) + (block.shape[0] // (n // 2), block.shape[1])), sorted(bits, reverse=True)


def start_halving(blocks, lefts, pair):
    kept, arrived, rest, sent = [], [], [], []
    for block, left, bit in zip(blocks, lefts, pair):
        axis = left.index(bit)
        kept.append(lax.index_in_dim(block, 0, axis, keepdims=False))
        sent.append(lax.index_in_dim(block, 1, axis, keepdims=False))
        arrived.append(lax.ppermute(sent[-1], "fsdp", partner(bit)))
        rest.append([b for b in left if b != bit])
    return (kept, arrived, rest), sent


def add_low(kept, arrived):
    return [(a.astype(F32) + b.astype(F32)).astype(BF) for a, b in zip(kept, arrived)]


def stack_heads(x):
    lane = lax.broadcasted_iota(jnp.int32, (BLOCK, x.shape[1]), 1)
    zero = jnp.zeros((BLOCK, x.shape[1]), x.dtype)
    heads = x.shape[1] // HD
    return jnp.concatenate(
        [
            jnp.where((lane >= h * HD) & (lane < (h + 1) * HD), x[j * BLOCK : (j + 1) * BLOCK], zero)
            for j in range(x.shape[0] // BLOCK)
            for h in range(heads)
        ],
        axis=0,
    )


def block_kind(seg, q_at, k_at):
    q_lo, q_hi = seg[q_at], seg[q_at + BLOCK - 1]
    k_lo, k_hi = seg[k_at], seg[k_at + BLOCK - 1]
    meet = (q_lo <= k_hi) & (k_lo <= q_hi)
    one = (q_lo == q_hi) & (k_lo == q_lo) & (k_hi == q_lo)
    return jnp.where(one, 2, jnp.where(meet, 1, 0))


def ids_down(ids_refs, col_s):
    rows = ids_refs[0].shape[1]

    @pl.when(pl.program_id(0) == 0)
    def _():
        for j, ids in enumerate(ids_refs):
            wide = jnp.broadcast_to(ids[...].astype(F32), (col_s.shape[1], rows))
            col_s[j * rows : (j + 1) * rows, :] = wide.T


def each_block(seg, where, slots, rows, visit):
    per = rows // BLOCK
    stride = slots[1] - slots[0] if len(slots) > 1 else 0

    def step(i, _):
        j, pair = i // (per * per), lax.rem(i, per * per)
        kb, qb = pair // per, lax.rem(pair, per)
        slot = slots[0] + stride * j
        kind = block_kind(seg, where[0] * rows + qb * BLOCK, where[1 + slot] * rows + kb * BLOCK)
        visit(j, slot, kb, qb, kind)
        return 0

    lax.fori_loop(0, len(slots) * per * per, step, 0)


def split_pieces(pieces):
    return [[p[0] for p in half] for half in pieces], tuple(tuple(p[1] for p in half) for half in pieces)


def piece_copy(pieces, offsets, j, f, column, width, target, sem):
    r = pieces[0].shape[0]
    place = 0
    if len(pieces) > 1:
        core, outer = j // (len(pieces) // 2), j % (len(pieces) // 2)
        place = f ^ (2 * outer + core)
    rows = pl.ds(pl.multiple_of(place * r, r), r)
    start = offsets[j] + column * width
    return pltpu.make_async_copy(
        pieces[j].at[:, start : start + width], target.at[rows, :], sem
    )


def lanes(index, size):
    return pl.ds(pl.multiple_of(index * size, size), size)


def forward_kernel(seg, where, *refs, slots, count, offsets):
    refs = list(refs)

    def take(count):
        taken, refs[:] = refs[:count], refs[count:]
        return taken

    x_refs = take(len(slots))
    ids_refs = take(len(slots))
    pieces = (take(count), take(count))
    bq_ref, bv_ref, sq_ref = take(3)
    q_ref, k_ref, v_ref, o_ref, lse_ref, w_ref, q_s, col_s, m_s, l_s, acc_s, ids_s, w_s, sems = refs

    @pl.when(pl.program_id(0) == 0)
    def _():
        copies = [
            piece_copy(pieces[m // 2], offsets[m // 2], j, where[6], m % 2, w_s.shape[2], w_s.at[m], sems.at[m, j])
            for m in range(3)
            for j in range(count)
        ]
        for copy in copies:
            copy.start()
        for copy in copies:
            copy.wait()

    w_ref[...] = w_s[:, :, lanes(pl.program_id(0), q_ref.shape[1])]
    wq_ref, wk_ref, wv_ref = (w_ref.at[m] for m in range(3))
    rows, width = q_ref.shape
    heads = width // HD
    wide = heads * BLOCK
    q_ref[...] = (nn(x_refs[0][...], wq_ref[...]) + bq_ref[...]).astype(BF)
    m_s[...] = jnp.full(m_s.shape, MASKED, F32)
    l_s[...] = jnp.zeros(l_s.shape, F32)
    acc_s[...] = jnp.zeros(acc_s.shape, F32)
    for j, x_ref in enumerate(x_refs):
        at = slice(j * rows, (j + 1) * rows)
        k_ref[at, :] = nn(x_ref[...], wk_ref[...]).astype(BF)
        v_ref[at, :] = (nn(x_ref[...], wv_ref[...]) + bv_ref[...]).astype(BF)
    q_s[...] = stack_heads(q_ref[...])
    ids_down(ids_refs, col_s)
    ids_s[...] = sq_ref[...].astype(F32)

    def block(at, qb, masked):
        stacked, part = lanes(qb, wide), lanes(qb, BLOCK)
        s = nt(k_ref[at, :], q_s[stacked, :])
        if masked:
            same = col_s[at, 0:1] == ids_s[:, part]
            s = jnp.where(jnp.concatenate([same] * heads, axis=1), s, MASKED)
        m_old = m_s[:, stacked]
        m_new = jnp.maximum(m_old, jnp.max(s, axis=0, keepdims=True))
        alpha = jnp.exp2((m_old - m_new) * SCORE)
        p = jnp.exp2((s - m_new) * SCORE)
        p_low = p.astype(BF)
        l_s[:, stacked] = alpha * l_s[:, stacked] + jnp.sum(p, axis=0, keepdims=True)
        m_s[:, stacked] = m_new
        v_t = v_ref[at, :].T
        for h in range(heads):
            hs, qs = slice(h * HD, (h + 1) * HD), slice(h * BLOCK, (h + 1) * BLOCK)
            acc_s[hs, part] = acc_s[hs, part] * alpha[:, qs] + nn(v_t[hs], p_low[:, qs])

    def visit(j, _, kb, qb, kind):
        at = pl.ds(pl.multiple_of(j * rows + kb * BLOCK, BLOCK), BLOCK)
        pl.when(kind == 1)(lambda: block(at, qb, True))
        pl.when(kind == 2)(lambda: block(at, qb, False))

    each_block(seg, where, slots, rows, visit)
    for j in range(rows // BLOCK):
        inverse = 1.0 / l_s[:, j * wide : (j + 1) * wide]
        spread_out = jnp.concatenate(
            [jnp.broadcast_to(inverse[:, h * BLOCK : (h + 1) * BLOCK], (HD, BLOCK)) for h in range(heads)], axis=0
        )
        at = slice(j * BLOCK, (j + 1) * BLOCK)
        o_ref[at, :] = (acc_s[:, at] * spread_out).T.astype(BF)
    lse_ref[0] = m_s[...] * SCORE + jnp.log2(l_s[...])


def attend_forward(xs, pieces, biases, seg, where):
    rows, width = xs[0].shape
    slots = tuple(range(len(xs)))
    keys = rows * len(xs)
    count = len(pieces[0])
    pieces, offsets = split_pieces(pieces)
    groups, wide = width // GROUP, GROUP // HD * rows
    block_spec = pl.BlockSpec((rows, GROUP), lambda i, s, w: (0, i))
    keys_spec = pl.BlockSpec((keys, GROUP), lambda i, s, w: (0, i))
    b_spec = pl.BlockSpec((1, GROUP), lambda i, s, w: (0, i))
    row_spec = pl.BlockSpec((1, 1, wide), lambda i, s, w: (i, 0, 0))
    block_shape = jax.ShapeDtypeStruct((rows, width), BF)
    keys_shape = jax.ShapeDtypeStruct((keys, width), BF)

    def ids_spec(entry):
        return pl.BlockSpec((1, rows), lambda i, s, w: (0, w[entry]))

    in_specs = [pl.BlockSpec((rows, width), lambda i, s, w: (0, 0))] * len(xs)
    in_specs += [ids_spec(1 + s) for s in slots] + [pl.BlockSpec(memory_space=pl.ANY)] * (2 * count) + [b_spec] * 2 + [ids_spec(0)]
    return pl.pallas_call(
        partial(forward_kernel, slots=slots, count=count, offsets=offsets),
        out_shape=(
            block_shape,
            keys_shape,
            keys_shape,
            block_shape,
            jax.ShapeDtypeStruct((groups, 1, wide), F32),
            jax.ShapeDtypeStruct((3, width, width), BF),
        ),
        grid_spec=pltpu.PrefetchScalarGridSpec(
            num_scalar_prefetch=2,
            grid=(groups,),
            in_specs=in_specs,
            out_specs=[
                block_spec, keys_spec, keys_spec, block_spec, row_spec,
                pl.BlockSpec((3, width, GROUP), lambda i, s, w: (0, 0, i)),
            ],
            scratch_shapes=[
                pltpu.VMEM((wide, GROUP), BF),
                pltpu.VMEM((keys, 128), F32),
                pltpu.VMEM((1, wide), F32),
                pltpu.VMEM((1, wide), F32),
                pltpu.VMEM((GROUP, rows), F32),
                pltpu.VMEM((1, rows), F32),
                pltpu.VMEM((3, width, width), BF),
                pltpu.SemaphoreType.DMA((3, count)),
            ],
        ),
        cost_estimate=pl.CostEstimate(flops=FEW, bytes_accessed=FEW, transcendentals=0),
        name="attend_forward",
    )(seg[0], where, *xs, *([seg] * len(slots)), *pieces[0], *pieces[1], *(b[None, :] for b in biases), seg)


def backward_kernel(seg, where, *refs, slots, first, last):
    refs = list(refs)

    def take(count):
        taken, refs[:] = refs[:count], refs[count:]
        return taken

    q_ref, do_ref, o_ref, lse_ref, wk_ref, wv_ref, sq_ref = take(7)
    (k_ref, v_ref), ids_refs = take(2), take(len(slots))
    if not first:
        (dq_in,) = take(1)
    if last:
        wq_ref, base_ref = take(2)
        dk_s, dv_s, dq_ref, dx_ref, q_s, do_s, delta_s, col_s, ids_s, dx_s, dq_s = refs
    else:
        dk_s, dv_s, dq_s, dx_ref, q_s, do_s, delta_s, col_s, ids_s, dx_s = refs
    g = pl.program_id(0)
    ids_down(ids_refs, col_s)
    ids_s[...] = sq_ref[...].astype(F32)
    rows, width = q_ref.shape
    heads = width // HD
    wide = heads * BLOCK
    q_s[...] = stack_heads(q_ref[...])
    do_s[...] = stack_heads(do_ref[...])
    prod = (do_ref[...].astype(F32) * o_ref[...].astype(F32)).T
    for j in range(rows // BLOCK):
        for h in range(heads):
            piece = prod[h * HD : (h + 1) * HD, j * BLOCK : (j + 1) * BLOCK]
            delta_s[:, j * wide + h * BLOCK : j * wide + (h + 1) * BLOCK] = jnp.sum(piece, axis=0, keepdims=True)
    dq_s[...] = jnp.zeros_like(dq_s) if first else dq_in[...]

    def block(j, at, out_at, qb, masked):
        stacked, part = lanes(qb, wide), lanes(qb, BLOCK)
        k = k_ref[at, :]
        k_t = k.T
        s = nt(k, q_s[stacked, :]) * SCORE - lse_ref[0, :, stacked]
        if masked:
            same = col_s[out_at, 0:1] == ids_s[:, part]
            s = jnp.where(jnp.concatenate([same] * heads, axis=1), s, MASKED)
        p = jnp.exp2(s)
        dp = nt(v_ref[at, :], do_s[stacked, :])
        ds = (p * (dp - delta_s[:, stacked])).astype(BF)
        dv = nn(p.astype(BF), do_s[stacked, :])
        dk = nn(ds, q_s[stacked, :])
        for h in range(heads):
            hs = slice(h * HD, (h + 1) * HD)
            dq_s[hs, part] += nn(k_t[hs], ds[:, h * BLOCK : (h + 1) * BLOCK])
        return dk, dv

    def visit(j, slot, kb, qb, kind):
        base = slot if len(slots) > 1 else 0
        at = pl.ds(pl.multiple_of(base * rows + kb * BLOCK, BLOCK), BLOCK)
        out_at = pl.ds(pl.multiple_of(j * rows + kb * BLOCK, BLOCK), BLOCK)

        @pl.when(qb == 0)
        def _():
            acc_k[...] = jnp.zeros(acc_k.shape, F32)
            acc_v[...] = jnp.zeros(acc_v.shape, F32)

        def add(masked):
            dk, dv = block(j, at, out_at, qb, masked)
            acc_k[...] += dk
            acc_v[...] += dv

        pl.when(kind == 1)(lambda: add(True))
        pl.when(kind == 2)(lambda: add(False))

        @pl.when(qb == rows // BLOCK - 1)
        def _():
            dk_s[out_at, :] = (acc_k[...] * HD**-0.5).astype(BF)
            dv_s[out_at, :] = acc_v[...].astype(BF)

    def scoped(acc_k_ref, acc_v_ref):
        nonlocal acc_k, acc_v
        acc_k, acc_v = acc_k_ref, acc_v_ref
        each_block(seg, where, slots, rows, visit)

    acc_k = acc_v = None
    pl.run_scoped(scoped, pltpu.VMEM((BLOCK, width), F32), pltpu.VMEM((BLOCK, width), F32))

    if last:
        dq_ref[...] = (dq_s[...] * HD**-0.5).T.astype(BF)

    @pl.when(g == 0)
    def _():
        if last:
            dx_s[:rows, :] = base_ref[...]
        else:
            dx_s[...] = jnp.zeros(dx_s.shape, F32)

    def back(j, _):
        at = pl.ds(pl.multiple_of(j * rows, rows), rows)
        dx_s[at, :] += nt(dk_s[at, :], wk_ref[...]) + nt(dv_s[at, :], wv_ref[...])
        return 0

    lax.fori_loop(0, len(slots), back, 0)
    if last:
        dx_s[:rows, :] += nt(dq_ref[...], wq_ref[...])

    @pl.when(g == pl.num_programs(0) - 1)
    def _():
        dx_ref[...] = dx_s[...].astype(dx_ref.dtype)


def attend_backward(q, k, v, do, o, lse, slots, weights, seg, where, dq=None, base=None):
    rows, width = q.shape
    keys = rows * len(slots)
    first, last = dq is None, base is not None
    groups, wide = width // GROUP, GROUP // HD * rows
    q_spec = pl.BlockSpec((rows, GROUP), lambda i, s, w: (0, i))
    wq_spec, wk_spec, wv_spec = (
        pl.BlockSpec((None, width, GROUP), lambda i, s, w, m=m: (m, 0, i)) for _, m in weights
    )
    row_spec = pl.BlockSpec((1, 1, wide), lambda i, s, w: (i, 0, 0))
    acc_spec = pl.BlockSpec((GROUP, rows), lambda i, s, w: (i, 0))
    keys_spec = pl.BlockSpec((keys, GROUP), lambda i, s, w: (0, i))

    def ids_spec(entry):
        return pl.BlockSpec((1, rows), lambda i, s, w: (0, w[entry]))

    def slot_spec(slot):
        return pl.BlockSpec((rows, GROUP), lambda i, s, w: (slot, i))

    wq, wk, wv = (a for a, _ in weights)
    count = len(slots)
    ins = [q, do, o, lse, wk, wv, seg, k, v] + [seg] * count
    in_specs = [q_spec, q_spec, q_spec, row_spec, wk_spec, wv_spec, ids_spec(0)]
    all_spec = pl.BlockSpec((k.shape[0], GROUP), lambda i, s, w: (0, i))
    in_specs += [all_spec if count > 1 else slot_spec(slots[0])] * 2 + [ids_spec(1 + s) for s in slots]
    if not first:
        ins.append(dq)
        in_specs.append(acc_spec)
    scratch = [pltpu.VMEM((wide, GROUP), BF), pltpu.VMEM((wide, GROUP), BF), pltpu.VMEM((1, wide), F32)]
    scratch += [pltpu.VMEM((keys, 128), F32), pltpu.VMEM((1, rows), F32), pltpu.VMEM((keys, width), F32)]
    if last:
        ins += [wq, base]
        in_specs += [wq_spec, pl.BlockSpec((rows, width), lambda i, s, w: (0, 0))]
        scratch.append(pltpu.VMEM((GROUP, rows), F32))
    keys_shape = jax.ShapeDtypeStruct((keys, width), BF)
    results = [
        (keys_spec, keys_shape),
        (keys_spec, keys_shape),
        (q_spec, jax.ShapeDtypeStruct((rows, width), BF))
        if last
        else (acc_spec, jax.ShapeDtypeStruct((width, rows), F32)),
        (
            pl.BlockSpec((keys, width), lambda i, s, w: (0, 0)),
            jax.ShapeDtypeStruct((keys, width), F32 if last else BF),
        ),
    ]
    return pl.pallas_call(
        partial(backward_kernel, slots=slots, first=first, last=last),
        out_shape=tuple(r[1] for r in results),
        grid_spec=pltpu.PrefetchScalarGridSpec(
            num_scalar_prefetch=2,
            grid=(groups,),
            in_specs=in_specs,
            out_specs=[r[0] for r in results],
            scratch_shapes=scratch,
        ),
        cost_estimate=pl.CostEstimate(flops=FEW, bytes_accessed=FEW, transcendentals=0),
        name="attend_backward",
    )(seg[0], where, *ins)


def attn_grad_kernel(core_ref, *refs, calls, slots, block_rows):
    x_refs, dq_ref, extra_ref, refs = refs[:slots], refs[slots], refs[slots + 1], refs[slots + 2 :]
    dk_refs, dv_refs, refs = refs[:calls], refs[calls : 2 * calls], refs[2 * calls :]
    first_ref, second_ref, x_s, w_s = refs
    rows = dq_ref.shape[0]

    @pl.when(pl.program_id(0) == 0)
    def _():
        for j, x_ref in enumerate(x_refs):
            x_s[:, j * rows : (j + 1) * rows] = x_ref[...].T

    sums = [
        jnp.sum(dq_ref[...].astype(F32), axis=0, keepdims=True),
        sum(jnp.sum(d[...].astype(F32), axis=0, keepdims=True) for d in dv_refs),
        extra_ref[...],
        jnp.zeros((EXTRA - 2 - extra_ref.shape[0], w_s.shape[1]), F32),
    ]
    sums = jnp.concatenate(sums, axis=0)

    def over_keys(parts):
        total, start = 0.0, 0
        for d in parts:
            total = total + nn(x_s[:, start : start + d.shape[0]], d[...])
            start += d.shape[0]
        return total

    for m, parts in enumerate(((dq_ref,), dk_refs, dv_refs)):
        if not block_rows:
            first_ref[m] = over_keys(parts)
            continue
        w_s[...] = over_keys(parts)
        core = core_ref[0]
        at = slice(m * block_rows, (m + 1) * block_rows)
        for b in range(first_ref.shape[0]):
            far = pl.multiple_of((2 * b + 1 - core) * block_rows, block_rows)
            near = pl.multiple_of((2 * b + core) * block_rows, block_rows)
            first_ref[b, at] = w_s[pl.ds(far, block_rows), :].astype(BF)
            second_ref[b, at] = w_s[pl.ds(near, block_rows), :]
    if block_rows:
        for b in range(first_ref.shape[0]):
            first_ref[b, 3 * block_rows :] = sums.astype(BF)
            second_ref[b, 3 * block_rows :] = sums
    else:
        second_ref[...] = sums


def attn_grads(core, xs, dq, extra, dks, dvs, n):
    rows, width = dq.shape
    block_rows = width // n if (width // n) % 16 == 0 else 0
    x_spec = pl.BlockSpec((rows, width), lambda i, c: (0, 0))

    def d_spec(d):
        return pl.BlockSpec((d.shape[0], GROUP), lambda i, c: (0, i))

    if block_rows:
        shape = (n // 2, 3 * block_rows + EXTRA)
        spec = pl.BlockSpec((*shape, GROUP), lambda i, c: (0, 0, i))
        results = [(spec, jax.ShapeDtypeStruct((*shape, width), t)) for t in (BF, F32)]
    else:
        spec = pl.BlockSpec((3, width, GROUP), lambda i, c: (0, 0, i))
        results = [(spec, jax.ShapeDtypeStruct((3, width, width), F32))]
        spec = pl.BlockSpec((EXTRA, GROUP), lambda i, c: (0, i))
        results.append((spec, jax.ShapeDtypeStruct((EXTRA, width), F32)))
    return pl.pallas_call(
        partial(attn_grad_kernel, calls=len(dks), slots=len(xs), block_rows=block_rows),
        out_shape=tuple(r[1] for r in results),
        grid_spec=pltpu.PrefetchScalarGridSpec(
            num_scalar_prefetch=1,
            grid=(width // GROUP,),
            in_specs=[x_spec] * len(xs) + [d_spec(d) for d in (dq, extra, *dks, *dvs)],
            out_specs=[r[0] for r in results],
            scratch_shapes=[pltpu.VMEM((width, rows * len(xs)), BF), pltpu.VMEM((width, GROUP), F32)],
        ),
        cost_estimate=pl.CostEstimate(flops=FEW, bytes_accessed=FEW, transcendentals=0),
        name="attn_grads",
    )(core, *xs, dq, extra, *dks, *dvs)


def norm_parts(rows_in):
    mean = jnp.mean(rows_in, axis=-1, keepdims=True)
    centred = rows_in - mean
    spread = jnp.mean(centred * centred, axis=-1, keepdims=True)
    r = lax.rsqrt(spread + EPSILON)
    return centred * r, r


def norm_back(g_y, n, r, gain):
    e = g_y * gain
    return r * (e - jnp.mean(e, axis=-1, keepdims=True) - n * jnp.mean(e * n, axis=-1, keepdims=True))


def gelu_parts(u):
    c = 0.7978845608028654
    square = u * u
    th = jnp.tanh(c * u * (1.0 + 0.044715 * square))
    half = 0.5 * (1.0 + th)
    slope = half + 0.5 * u * (1.0 - th * th) * (c + 3 * 0.044715 * c * square)
    return u * half, slope


def down_rows(x):
    return jnp.sum(x, axis=0, keepdims=True)


def middle_kernel(known, *refs, count, offsets):
    w_refs, refs = (refs[:count], refs[count : 2 * count]), refs[2 * count :]
    ctx_ref, x_ref, grad_ref, vec_ref, bias_ref = refs[:5]
    out_ref, first_ref, gctx_ref, lefts_ref, rights_ref, sums_ref = refs[5:11]
    w_s, mix_ref, slope_s, n1_s, r1_s, acc_s, sems, mix_sems = refs[11:]
    parts, units = bias_ref.shape
    rows, width = x_ref.shape

    def copy(which, t, j):
        return piece_copy(
            w_refs[which], offsets[which], j, known[1], 2 * width // units + t, units, w_s.at[which, t], sems.at[which, t, j]
        )

    mix_copies = [
        piece_copy(w_refs[1], offsets[1], j, known[1], 1, width, mix_ref, mix_sems.at[j]) for j in range(count)
    ]
    for mix_copy in mix_copies:
        mix_copy.start()
    for which in range(2):
        for t in range(parts):
            for j in range(count):
                copy(which, t, j).start()
    for mix_copy in mix_copies:
        mix_copy.wait()

    def cols(t):
        return pl.ds(pl.multiple_of(t * units, units), units)

    first_sum = x_ref[...].astype(F32) + nt(ctx_ref[...], mix_ref[...]) + vec_ref[0:1, :]
    n1, r1 = norm_parts(first_sum)
    n1_s[...] = n1
    r1_s[...] = jnp.broadcast_to(r1, r1_s.shape)
    acc_s[...] = n1 * vec_ref[1:2, :] + vec_ref[2:3, :]
    lefts_ref[1] = acc_s[...].astype(BF)

    for which in range(2):
        for t in range(parts):
            for j in range(count):
                copy(which, t, j).wait()

    def up(t, _):
        pre = nn(lefts_ref[1], w_s[0, t]) + bias_ref[pl.ds(known[2 + t], 1), :]
        act, slope = gelu_parts(pre)
        slope_s[t] = slope
        low = act.astype(BF)
        rights_ref[:, cols(t)] = low
        acc_s[...] += nt(low, w_s[1, t])
        return 0

    lax.fori_loop(0, parts, up, 0)
    n2, r2 = norm_parts(acc_s[...] + vec_ref[3:4, :])
    out_ref[...] = (n2 * vec_ref[4:5, :] + vec_ref[5:6, :]).astype(BF)
    row = lax.broadcasted_iota(jnp.int32, (rows, width), 0)
    g_out = jnp.where(row < known[0], grad_ref[...].astype(F32), 0.0)
    g_second = norm_back(g_out, n2, r2, vec_ref[4:5, :])
    sums_ref[3:4, :] = down_rows(g_second)
    sums_ref[4:5, :] = down_rows(g_out * n2)
    sums_ref[5:6, :] = down_rows(g_out)
    lefts_ref[0] = g_second.astype(BF)
    acc_s[...] = g_second

    def back(t, _):
        g_pre = (nn(lefts_ref[0], w_s[1, t]) * slope_s[t]).astype(BF)
        rights_ref[:, cols(parts + t)] = g_pre
        sums_ref[pl.ds(6 + known[2 + t], 1), :] = down_rows(g_pre.astype(F32))
        acc_s[...] += nt(g_pre, w_s[0, t])
        return 0

    lax.fori_loop(0, parts, back, 0)
    g_normed = acc_s[...]
    n1 = n1_s[...]
    g_first = norm_back(g_normed, n1, r1_s[:, 0:1], vec_ref[1:2, :])
    sums_ref[0:1, :] = down_rows(g_first)
    sums_ref[1:2, :] = down_rows(g_normed * n1)
    sums_ref[2:3, :] = down_rows(g_normed)
    first_ref[...] = g_first
    low = g_first.astype(BF)
    lefts_ref[2] = low
    gctx_ref[...] = nn(low, mix_ref[...]).astype(BF)
    rights_ref[:, 2 * parts * units :] = ctx_ref[...]


def middle(known, pieces, ctx, x, grad, vectors, bias):
    rows, width = x.shape
    parts, units = bias.shape
    count = len(pieces[0])
    pieces, offsets = split_pieces(pieces)
    vmem = pl.BlockSpec(memory_space=pltpu.VMEM)
    shapes = [
        ((rows, width), BF),
        ((rows, width), F32),
        ((rows, width), BF),
        ((3, rows, width), BF),
        ((rows, 2 * parts * units + width), BF),
        ((6 + parts, width), F32),
    ]
    return pl.pallas_call(
        partial(middle_kernel, count=count, offsets=offsets),
        out_shape=tuple(jax.ShapeDtypeStruct(*s) for s in shapes),
        in_specs=[pl.BlockSpec(memory_space=pltpu.SMEM)] + [pl.BlockSpec(memory_space=pl.ANY)] * (2 * count) + [vmem] * 5,
        out_specs=[vmem] * len(shapes),
        scratch_shapes=[
            pltpu.VMEM((2, parts, width, units), BF),
            pltpu.VMEM((width, width), BF),
            pltpu.VMEM((parts, rows, units), F32),
            pltpu.VMEM((rows, width), F32),
            pltpu.VMEM((rows, 128), F32),
            pltpu.VMEM((rows, width), F32),
            pltpu.SemaphoreType.DMA((2, parts, count)),
            pltpu.SemaphoreType.DMA((count,)),
        ],
        compiler_params=pltpu.CompilerParams(vmem_limit_bytes=63 << 20),
        cost_estimate=pl.CostEstimate(flops=FEW, bytes_accessed=FEW, transcendentals=0),
        name="middle",
    )(known, *pieces[0], *pieces[1], ctx, x, grad, vectors, bias)


def ffn_grad_kernel(place, left_ref, right_ref, kept_ref, sent_ref, left_s, chosen_s, *, n):
    half = kept_ref.shape[0]

    @pl.when(pl.program_id(0) % 4 == 0)
    def _():
        left_s[...] = left_ref[0].T
        size = left_s.shape[0] // n
        if size % 16:
            chosen_s[...] = left_s[...]
        else:
            for j in range(n):
                core, outer = j // (n // 2), j % (n // 2)
                block = place[0] ^ (2 * outer + core)
                chosen_s[j * size : (j + 1) * size, :] = left_s[pl.ds(pl.multiple_of(block * size, size), size), :]

    total = nn(chosen_s[...], right_ref[...])
    kept_ref[...] = total[:half].astype(BF)
    sent_ref[...] = total[half:].astype(BF)


def ffn_grads(place, lefts, rights, n):
    _, rows, width = lefts.shape
    units = rights.shape[1] // 9
    out_spec = pl.BlockSpec((width // 2, units), lambda i, p: (0, i))
    out_shape = jax.ShapeDtypeStruct((width // 2, rights.shape[1]), BF)
    return pl.pallas_call(
        partial(ffn_grad_kernel, n=n),
        out_shape=(out_shape, out_shape),
        grid_spec=pltpu.PrefetchScalarGridSpec(
            num_scalar_prefetch=1,
            grid=(9,),
            in_specs=[
                pl.BlockSpec((1, rows, width), lambda i, p: (i // 4, 0, 0)),
                pl.BlockSpec((rows, units), lambda i, p: (0, i)),
            ],
            out_specs=[out_spec, out_spec],
            scratch_shapes=[pltpu.VMEM((width, rows), BF), pltpu.VMEM((width, rows), BF)],
        ),
        cost_estimate=pl.CostEstimate(flops=FEW, bytes_accessed=FEW, transcendentals=0),
        name="ffn_grads",
    )(place, lefts, rights)


def finish_kernel(*refs, r):
    terms, refs = refs[:4], refs[4:]
    total = sum(t[...].astype(F32) for t in terms)
    for m in range(3):
        refs[m][...] = total[m * r : (m + 1) * r]
    base = 3 * r

    def row(*at):
        return jnp.concatenate([total[base + i : base + i + 1] for i in at], axis=1)[0]

    for w in range(2):
        refs[3 + w][...] = row(*(2 * i + w for i in range(4)))
    for j in range(6):
        refs[5 + j][...] = row(*(8 + 10 * i + j for i in range(4)))
    refs[11][...] = row(*(8 + 10 * i + j for j in range(6, 10) for i in range(4)))


def finish(terms, r, width, units):
    cols = terms[0].shape[1]
    shapes = [(r, cols)] * 3 + [(width,)] * 8 + [(4 * units,)]
    vmem = pl.BlockSpec(memory_space=pltpu.VMEM)
    return pl.pallas_call(
        partial(finish_kernel, r=r),
        out_shape=tuple(jax.ShapeDtypeStruct(x, F32) for x in shapes),
        in_specs=[vmem] * 4,
        out_specs=[vmem] * len(shapes),
        cost_estimate=pl.CostEstimate(flops=FEW, bytes_accessed=FEW, transcendentals=0),
        name="finish",
    )(*terms)


def on_device(
    tokens,
    segments,
    query_weight,
    query_bias,
    key_weight,
    value_weight,
    value_bias,
    mix_weight,
    mix_bias,
    norm_gain,
    norm_shift,
    up_weight,
    up_bias,
    down_weight,
    down_bias,
    final_gain,
    final_shift,
    out_grad,
):
    t = lax.axis_index("tensor")
    f = lax.axis_index("fsdp")
    n = lax.axis_size("fsdp")
    rows, width = tokens.shape
    r, units = up_weight.shape
    cols = query_weight.shape[1]
    owner = slot_owner(t)

    def by_slot(vector):
        parts = vector.reshape(4, -1)
        return jnp.concatenate([lax.dynamic_slice_in_dim(parts, owner[i], 1, axis=0)[0] for i in range(4)])

    seg = jnp.where(segments == 0, 9, segments)
    where = jnp.concatenate([t[None], owner, (f & 1)[None], f[None]]).astype(jnp.int32)
    own_ids = lax.dynamic_slice_in_dim(seg[0], t * rows, rows)
    known = jnp.concatenate([jnp.stack([jnp.sum((own_ids < 9).astype(jnp.int32)), f]), owner]).astype(jnp.int32)
    vectors = jnp.stack([mix_bias, norm_gain, norm_shift, down_bias, final_gain, final_shift])
    shifts = (by_slot(query_bias), by_slot(value_bias))
    slot_of = owner_slot(t)
    goals = [sum(jnp.where(owner[k] == lax.rem(t + shift, 4), k, 0) for k in range(4)) for shift in SHIFTS]
    seg, where, known, vectors, shifts, slot_of, goals = lax.optimization_barrier(
        (seg, where, known, vectors, shifts, slot_of, goals)
    )
    small_operands = (seg, where, known, vectors, *shifts, *slot_of, *goals)

    shard = jnp.stack(
        [
            jnp.concatenate([query_weight, key_weight, value_weight, mix_weight.T], axis=1),
            up_weight,
            down_weight.T,
        ]
    )
    w_a, w_below, w_above = line_first(shard)
    w_c = after(line_second(w_below, w_above), *small_operands)
    w_b = line_third(w_c, w_below)
    w_slots = (shard, w_a, w_c, w_b)
    x_a, x_below, x_above = line_first(after(tokens, w_c))

    line = []
    for first, last in ((0, 1), (2, 2)):
        line += [w[0][:, m * cols : (m + 1) * cols] for m in (first, first + 1) for w in w_slots]
        line += [w[last] for w in w_slots]
    own = jnp.concatenate(line, axis=1)
    wide = own.shape[1] // 2
    bits = outer_bits()

    def over(block, bit):
        return lax.ppermute(block, "fsdp", partner(bit))

    if len(bits) == 2:
        beside = [over(own, bit) for bit in bits]
        far_own = over(own, 1)
        x_c = line_second(*after((x_below, x_above), far_own))
        beside = after(beside, x_a, x_c)
        across = [over(beside[0][:, :wide], bits[1]), over(beside[1][:, wide:], bits[0])]
        far_beside = [over(b, 1) for b in beside]
        x_b = line_third(x_c, x_below, *far_beside)
        far_across = [over(a, 1) for a in across]
        pieces = [
            [
                piece
                for o, b, a in ((own, beside, across), (far_own, far_beside, far_across))
                for piece in ((o, i * wide), (b[0], i * wide), (b[1], i * wide), (a[i], 0))
            ]
            for i in range(2)
        ]
    else:
        x_c = line_second(x_below, x_above)
        x_b = line_third(x_c, x_below)
        held = {0: after(own, x_a)}
        for bit in bits:
            held.update({place | (bit >> 1): over(block, bit) for place, block in sorted(held.items())})
        near = [held[p] for p in sorted(held)]
        far = [over(block, 1) for block in near]
        pieces = [[(block, i * wide) for block in near + far] for i in range(2)]
    if r % 16:
        pieces = [[(assembled([p[0][:, p[1] : p[1] + wide] for p in half]), 0)] for half in pieces]

    xs = (tokens, x_a, x_c, x_b)
    q, k, v, ctx, lse, w_all = attend_forward(xs, pieces, shifts, seg, where)
    weights = tuple((w_all, m) for m in range(3))

    layer_out, g_first, g_ctx, lefts, rights, extra = middle(
        known, pieces, ctx, tokens, out_grad, vectors, up_bias.reshape(4, units)
    )
    place = f.astype(jnp.int32)[None]
    kept, sent = ffn_grads(place, lefts, rights, n)
    if r % 16:
        full = jnp.concatenate([kept, sent]).reshape(n, r, -1)
        kept, sent = (
            jnp.concatenate([lax.dynamic_slice_in_dim(full, f ^ (2 * q + c), 1)[0] for q in range(n // 2)])
            for c in range(2)
        )
    got = lax.ppermute(sent, "fsdp", partner(1))
    g_ctx = after(g_ctx, sent)

    args = (q, k, v, g_ctx, ctx, lse)
    dk_n, dv_n, dq, dx_n = attend_backward(*args, (3, 2, 1), weights, seg, where)
    dx_b, dx_c, dx_a = (dx_n[i * rows : (i + 1) * rows] for i in range(3))
    r1 = lax.ppermute(dx_b, "tensor", [(0, 1), (3, 2)])
    steps = list(zip(outer_bits(), outer_bits()[::-1]))
    got = after(got, dx_n)
    held = [outer_axes(kept[:, : 4 * units]), outer_axes(kept[:, 4 * units :])]
    come = [outer_axes(got[:, : 4 * units])[0], outer_axes(got[:, 4 * units :])[0]]
    lefts = [h[1] for h in held]
    held = [h[0] for h in held]
    axes = [left.index(bit) for left, bit in zip(lefts, steps[0])]

    def at(blocks, index):
        return [lax.index_in_dim(b, index, axis, keepdims=False) for b, axis in zip(blocks, axes)]

    out_halves = add_low(at(held, 1), at(come, 1))
    arrived = [lax.ppermute(o, "fsdp", partner(bit)) for o, bit in zip(out_halves, steps[0])]
    dk_o, dv_o, dq, dx_own = attend_backward(
        *args, (0,), weights, seg, where, after(dq, dx_b, *out_halves), g_first
    )
    middle_x = (dx_c.astype(F32) + after(r1, dx_own).astype(F32)).astype(BF)
    rx = lax.ppermute(middle_x, "tensor", [(0, 1), (3, 2)])
    ry = lax.ppermute(middle_x, "tensor", [(1, 2), (2, 1)])

    arrived = after(arrived, dx_own)
    blocks = [
        (a.astype(F32) + b.astype(F32) + c.astype(F32)).astype(BF)
        for a, b, c in zip(at(held, 0), at(come, 0), arrived)
    ]
    lefts = [[b for b in left if b != bit] for left, bit in zip(lefts, steps[0])]
    halves, out_halves = start_halving(blocks, lefts, steps[1])

    xs = (xs[0], xs[3], xs[2], xs[1])
    dq = after(dq, middle_x, *out_halves)
    sent, kept = attn_grads(where[5:6], xs, dq, extra, (dk_o, dk_n), (dv_o, dv_n), n)
    if r % 16:
        split = sent.reshape(3, n // 2, 2, r, width)
        sums = jnp.broadcast_to(kept, (n // 2, EXTRA, width))
        sent, kept = (
            jnp.concatenate(
                [
                    lax.dynamic_index_in_dim(split, c, 2, keepdims=False)
                    .transpose(1, 0, 2, 3)
                    .reshape(n // 2, 3 * r, width),
                    sums,
                ],
                axis=1,
            )
            for c in (1 - (f & 1), f & 1)
        )
        sent = sent.astype(BF)
    got = lax.ppermute(sent, "fsdp", partner(1))
    near = (kept + got.astype(F32)).astype(BF)
    rx, ry = (a.astype(F32) for a in after((rx, ry), sent))
    up_x = (dx_a.astype(F32) + jnp.where(t == 1, rx, ry)).astype(BF)
    down_x = jnp.where(t == 3, dx_a.astype(F32), dx_b.astype(F32) + jnp.where(t == 1, ry, rx)).astype(BF)
    from_below = lax.ppermute(up_x, "tensor", [(0, 1), (1, 2), (2, 3)])
    from_above = lax.ppermute(down_x, "tensor", [(1, 0), (2, 1), (3, 2)])

    d_one, d_two = add_low(halves[0], after(halves[1], sent))
    for pair in steps[2:]:
        halves, _ = start_halving([d_one, d_two], halves[2], pair)
        d_one, d_two = add_low(halves[0], halves[1])
    early = jnp.stack(
        [
            jnp.concatenate(
                [
                    d_one[:, i * units : (i + 1) * units],
                    d_two[:, i * units : (i + 1) * units],
                    d_two[:, 4 * units + i * cols : 4 * units + (i + 1) * cols],
                ],
                axis=1,
            )
            for i in range(4)
        ]
    )

    early_own, early = early[0], spread(early, goals)
    same_core = [list(range(c, n, 2)) for c in range(2)]
    arrived = lax.all_to_all(near, "fsdp", split_axis=0, concat_axis=0, axis_index_groups=same_core, tiled=True)
    arrived = after(arrived, *early)
    late = jnp.sum(arrived.astype(F32), axis=0).astype(BF)
    count = 12
    by_head = jnp.stack([late[3 * r : 3 * r + 2, i * cols : (i + 1) * cols] for i in range(4)])
    by_head = in_line_order(by_head, slot_of).reshape(8, cols)
    whole = [late[3 * r + 2 : 3 * r + count, i * cols : (i + 1) * cols] for i in range(4)]
    below = jnp.concatenate([by_head, *whole])
    late = jnp.stack(
        [jnp.concatenate([late[: 3 * r, i * cols : (i + 1) * cols], below]) for i in range(4)]
    )
    *late, qb, vb, b0, b1, b2, b3, b4, b5, up_sums = finish((late[0], *spread(late, goals)), r, width, units)
    early = total(early_own, early)
    tokens_grad = dx_own + from_below.astype(F32) + from_above.astype(F32)

    return (
        layer_out,
        tokens_grad,
        late[0],
        qb,
        late[1],
        late[2],
        vb,
        early[:, 2 * units :].T,
        b0,
        b1,
        b2,
        early[:, units : 2 * units],
        up_sums,
        early[:, :units].T,
        b3,
        b4,
        b5,
    )


def solution(mesh):
    both, rows_f, square, flipped = (
        P(("fsdp", "tensor"), None),
        P("fsdp", None),
        P("fsdp", "tensor"),
        P("tensor", "fsdp"),
    )
    return jax.shard_map(
        on_device,
        mesh=mesh,
        in_specs=(
            both, rows_f, square, P(), square, square, P(), flipped, P(), P(), P(),
            square, P(), flipped, P(), P(), P(), both,
        ),
        out_specs=(
            both, both, square, P(), square, square, P(), flipped, P(), P(), P(),
            square, P(), flipped, P(), P(), P(),
        ),
        check_vma=False,
    )
```

```python
from functools import partial

import jax
import jax.numpy as jnp
from jax import lax
from jax.experimental import pallas as pl
from jax.experimental.pallas import tpu as pltpu
from jax.sharding import PartitionSpec as P

HD = 64
GROUP = 256
BLOCK = 256
EPSILON = 1e-05
MASKED = -1e30
LOG2E = 1.4426950408889634
SCORE = HD**-0.5 * LOG2E
EXTRA = 16
SHIFTS = (1, 3, 2)
FEW = 1000
BF = jnp.bfloat16
F32 = jnp.float32


def after(value, *others):
    return lax.optimization_barrier((value,) + others)[0] if others else value


def nt(a, b):
    return lax.dot_general(a, b, (((1,), (1,)), ((), ())), preferred_element_type=F32)


def nn(a, b):
    return lax.dot_general(a, b, (((1,), (0,)), ((), ())), preferred_element_type=F32)


def line_first(own):
    below = lax.ppermute(own, "tensor", [(0, 1), (1, 2), (2, 3)])
    above = lax.ppermute(own, "tensor", [(1, 0), (2, 1), (3, 2)])
    return jnp.where(lax.axis_index("tensor") < 3, above, below), below, above


def line_second(below, above, *gate):
    below2 = lax.ppermute(below, "tensor", [(1, 2), (2, 3)])
    above2 = lax.ppermute(above, "tensor", [(2, 1), (1, 0)])
    below2, above2 = after((below2, above2), *gate)
    return jnp.where(lax.axis_index("tensor") < 2, above2, below2)


def line_third(slot_c, below, *gate):
    far = after(lax.ppermute(slot_c, "tensor", [(1, 0), (2, 3)]), *gate)
    t = lax.axis_index("tensor")
    return jnp.where((t == 0) | (t == 3), far, below)


def slot_owner(t):
    return jnp.stack([t, jnp.where(t < 3, t + 1, 2), lax.rem(t + 2, 4), jnp.where(t == 3, 0, lax.rem(t + 3, 4))])


def owner_slot(t):
    owner = slot_owner(t)
    return [sum(jnp.where(owner[k] == j, k, 0) for k in range(4)) for j in range(4)]


def in_line_order(slots, slot_of):
    return jnp.concatenate([lax.dynamic_slice_in_dim(slots, s, 1, axis=0) for s in slot_of])


def spread(slots, goals):
    arrived = []
    for shift, slot in zip(SHIFTS, goals):
        block = lax.dynamic_index_in_dim(slots, slot, 0, keepdims=False)
        arrived.append(lax.ppermute(block, "tensor", [(i, (i + shift) % 4) for i in range(4)]))
    return arrived


def total(own, arrived):
    return own.astype(F32) + sum(a.astype(F32) for a in arrived)


def partner(bit):
    n = lax.axis_size("fsdp")
    return [(i, i ^ bit) for i in range(n)]


def outer_bits():
    n = lax.axis_size("fsdp")
    return [1 << k for k in range(1, n.bit_length() - 1)]


def assembled(pieces):
    n = len(pieces)
    f = lax.axis_index("fsdp")
    stacked = jnp.stack(pieces).reshape(2, n // 2, *pieces[0].shape)
    blocks = []
    for a in range(n):
        rel = f ^ a
        block = lax.dynamic_slice_in_dim(stacked, rel & 1, 1, axis=0)
        blocks.append(lax.dynamic_slice_in_dim(block, rel >> 1, 1, axis=1)[0, 0])
    return jnp.concatenate(blocks)


def outer_axes(block):
    n = lax.axis_size("fsdp")
    bits = outer_bits()
    return block.reshape((2,) * len(bits) + (block.shape[0] // (n // 2), block.shape[1])), sorted(bits, reverse=True)


def start_halving(blocks, lefts, pair):
    kept, arrived, rest, sent = [], [], [], []
    for block, left, bit in zip(blocks, lefts, pair):
        axis = left.index(bit)
        kept.append(lax.index_in_dim(block, 0, axis, keepdims=False))
        sent.append(lax.index_in_dim(block, 1, axis, keepdims=False))
        arrived.append(lax.ppermute(sent[-1], "fsdp", partner(bit)))
        rest.append([b for b in left if b != bit])
    return (kept, arrived, rest), sent


def add_low(kept, arrived):
    return [(a.astype(F32) + b.astype(F32)).astype(BF) for a, b in zip(kept, arrived)]


def stack_heads(x):
    lane = lax.broadcasted_iota(jnp.int32, (BLOCK, x.shape[1]), 1)
    zero = jnp.zeros((BLOCK, x.shape[1]), x.dtype)
    heads = x.shape[1] // HD
    return jnp.concatenate(
        [
            jnp.where((lane >= h * HD) & (lane < (h + 1) * HD), x[j * BLOCK : (j + 1) * BLOCK], zero)
            for j in range(x.shape[0] // BLOCK)
            for h in range(heads)
        ],
        axis=0,
    )


def block_kind(seg, q_at, k_at):
    q_lo, q_hi = seg[q_at], seg[q_at + BLOCK - 1]
    k_lo, k_hi = seg[k_at], seg[k_at + BLOCK - 1]
    meet = (q_lo <= k_hi) & (k_lo <= q_hi)
    one = (q_lo == q_hi) & (k_lo == q_lo) & (k_hi == q_lo)
    return jnp.where(one, 2, jnp.where(meet, 1, 0))


def ids_down(ids_refs, col_s):
    rows = ids_refs[0].shape[1]

    @pl.when(pl.program_id(0) == 0)
    def _():
        for j, ids in enumerate(ids_refs):
            wide = jnp.broadcast_to(ids[...].astype(F32), (col_s.shape[1], rows))
            col_s[j * rows : (j + 1) * rows, :] = wide.T


def each_block(seg, where, slots, rows, visit):
    per = rows // BLOCK
    stride = slots[1] - slots[0] if len(slots) > 1 else 0

    def step(i, _):
        j, pair = i // (per * per), lax.rem(i, per * per)
        kb, qb = pair // per, lax.rem(pair, per)
        slot = slots[0] + stride * j
        kind = block_kind(seg, where[0] * rows + qb * BLOCK, where[1 + slot] * rows + kb * BLOCK)
        visit(j, slot, kb, qb, kind)
        return 0

    lax.fori_loop(0, len(slots) * per * per, step, 0)


def split_pieces(pieces):
    return [[p[0] for p in half] for half in pieces], tuple(tuple(p[1] for p in half) for half in pieces)


def piece_copy(pieces, offsets, j, f, column, width, target, sem):
    r = pieces[0].shape[0]
    place = 0
    if len(pieces) > 1:
        core, outer = j // (len(pieces) // 2), j % (len(pieces) // 2)
        place = f ^ (2 * outer + core)
    rows = pl.ds(pl.multiple_of(place * r, r), r)
    start = offsets[j] + column * width
    return pltpu.make_async_copy(
        pieces[j].at[:, start : start + width], target.at[rows, :], sem
    )


def lanes(index, size):
    return pl.ds(pl.multiple_of(index * size, size), size)


def forward_kernel(seg, where, *refs, slots, count, offsets):
    refs = list(refs)

    def take(count):
        taken, refs[:] = refs[:count], refs[count:]
        return taken

    x_refs = take(len(slots))
    ids_refs = take(len(slots))
    pieces = (take(count), take(count))
    bq_ref, bv_ref, sq_ref = take(3)
    q_ref, k_ref, v_ref, o_ref, lse_ref, w_ref, q_s, col_s, m_s, l_s, acc_s, ids_s, w_s, sems = refs

    @pl.when(pl.program_id(0) == 0)
    def _():
        copies = [
            piece_copy(pieces[m // 2], offsets[m // 2], j, where[6], m % 2, w_s.shape[2], w_s.at[m], sems.at[m, j])
            for m in range(3)
            for j in range(count)
        ]
        for copy in copies:
            copy.start()
        for copy in copies:
            copy.wait()

    w_ref[...] = w_s[:, :, lanes(pl.program_id(0), q_ref.shape[1])]
    wq_ref, wk_ref, wv_ref = (w_ref.at[m] for m in range(3))
    rows, width = q_ref.shape
    heads = width // HD
    wide = heads * BLOCK
    q_ref[...] = (nn(x_refs[0][...], wq_ref[...]) + bq_ref[...]).astype(BF)
    m_s[...] = jnp.full(m_s.shape, MASKED, F32)
    l_s[...] = jnp.zeros(l_s.shape, F32)
    acc_s[...] = jnp.zeros(acc_s.shape, F32)
    for j, x_ref in enumerate(x_refs):
        at = slice(j * rows, (j + 1) * rows)
        k_ref[at, :] = nn(x_ref[...], wk_ref[...]).astype(BF)
        v_ref[at, :] = (nn(x_ref[...], wv_ref[...]) + bv_ref[...]).astype(BF)
    q_s[...] = stack_heads(q_ref[...])
    ids_down(ids_refs, col_s)
    ids_s[...] = sq_ref[...].astype(F32)

    def block(at, qb, masked):
        stacked, part = lanes(qb, wide), lanes(qb, BLOCK)
        s = nt(k_ref[at, :], q_s[stacked, :])
        if masked:
            same = col_s[at, 0:1] == ids_s[:, part]
            s = jnp.where(jnp.concatenate([same] * heads, axis=1), s, MASKED)
        m_old = m_s[:, stacked]
        m_new = jnp.maximum(m_old, jnp.max(s, axis=0, keepdims=True))
        alpha = jnp.exp2((m_old - m_new) * SCORE)
        p = jnp.exp2((s - m_new) * SCORE)
        p_low = p.astype(BF)
        l_s[:, stacked] = alpha * l_s[:, stacked] + jnp.sum(p, axis=0, keepdims=True)
        m_s[:, stacked] = m_new
        v_t = v_ref[at, :].T
        for h in range(heads):
            hs, qs = slice(h * HD, (h + 1) * HD), slice(h * BLOCK, (h + 1) * BLOCK)
            acc_s[hs, part] = acc_s[hs, part] * alpha[:, qs] + nn(v_t[hs], p_low[:, qs])

    def visit(j, _, kb, qb, kind):
        at = pl.ds(pl.multiple_of(j * rows + kb * BLOCK, BLOCK), BLOCK)
        pl.when(kind == 1)(lambda: block(at, qb, True))
        pl.when(kind == 2)(lambda: block(at, qb, False))

    each_block(seg, where, slots, rows, visit)
    for j in range(rows // BLOCK):
        inverse = 1.0 / l_s[:, j * wide : (j + 1) * wide]
        spread_out = jnp.concatenate(
            [jnp.broadcast_to(inverse[:, h * BLOCK : (h + 1) * BLOCK], (HD, BLOCK)) for h in range(heads)], axis=0
        )
        at = slice(j * BLOCK, (j + 1) * BLOCK)
        o_ref[at, :] = (acc_s[:, at] * spread_out).T.astype(BF)
    lse_ref[0] = m_s[...] * SCORE + jnp.log2(l_s[...])


def attend_forward(xs, pieces, biases, seg, where):
    rows, width = xs[0].shape
    slots = tuple(range(len(xs)))
    keys = rows * len(xs)
    count = len(pieces[0])
    pieces, offsets = split_pieces(pieces)
    groups, wide = width // GROUP, GROUP // HD * rows
    block_spec = pl.BlockSpec((rows, GROUP), lambda i, s, w: (0, i))
    keys_spec = pl.BlockSpec((keys, GROUP), lambda i, s, w: (0, i))
    b_spec = pl.BlockSpec((1, GROUP), lambda i, s, w: (0, i))
    row_spec = pl.BlockSpec((1, 1, wide), lambda i, s, w: (i, 0, 0))
    block_shape = jax.ShapeDtypeStruct((rows, width), BF)
    keys_shape = jax.ShapeDtypeStruct((keys, width), BF)

    def ids_spec(entry):
        return pl.BlockSpec((1, rows), lambda i, s, w: (0, w[entry]))

    in_specs = [pl.BlockSpec((rows, width), lambda i, s, w: (0, 0))] * len(xs)
    in_specs += [ids_spec(1 + s) for s in slots] + [pl.BlockSpec(memory_space=pl.ANY)] * (2 * count) + [b_spec] * 2 + [ids_spec(0)]
    return pl.pallas_call(
        partial(forward_kernel, slots=slots, count=count, offsets=offsets),
        out_shape=(
            block_shape,
            keys_shape,
            keys_shape,
            block_shape,
            jax.ShapeDtypeStruct((groups, 1, wide), F32),
            jax.ShapeDtypeStruct((3, width, width), BF),
        ),
        grid_spec=pltpu.PrefetchScalarGridSpec(
            num_scalar_prefetch=2,
            grid=(groups,),
            in_specs=in_specs,
            out_specs=[
                block_spec, keys_spec, keys_spec, block_spec, row_spec,
                pl.BlockSpec((3, width, GROUP), lambda i, s, w: (0, 0, i)),
            ],
            scratch_shapes=[
                pltpu.VMEM((wide, GROUP), BF),
                pltpu.VMEM((keys, 128), F32),
                pltpu.VMEM((1, wide), F32),
                pltpu.VMEM((1, wide), F32),
                pltpu.VMEM((GROUP, rows), F32),
                pltpu.VMEM((1, rows), F32),
                pltpu.VMEM((3, width, width), BF),
                pltpu.SemaphoreType.DMA((3, count)),
            ],
        ),
        cost_estimate=pl.CostEstimate(flops=FEW, bytes_accessed=FEW, transcendentals=0),
        name="attend_forward",
    )(seg[0], where, *xs, *([seg] * len(slots)), *pieces[0], *pieces[1], *(b[None, :] for b in biases), seg)


def backward_kernel(seg, where, *refs, slots, first, last):
    refs = list(refs)

    def take(count):
        taken, refs[:] = refs[:count], refs[count:]
        return taken

    q_ref, do_ref, o_ref, lse_ref, wk_ref, wv_ref, sq_ref = take(7)
    (k_ref, v_ref), ids_refs = take(2), take(len(slots))
    if not first:
        (dq_in,) = take(1)
    if last:
        wq_ref, base_ref = take(2)
        dk_s, dv_s, dq_ref = take(3)
        dx_refs = take(len(slots))
        q_s, do_s, delta_s, col_s, ids_s, dx_s, dq_s = refs
    else:
        dk_s, dv_s, dq_s = take(3)
        dx_refs = take(len(slots))
        q_s, do_s, delta_s, col_s, ids_s, dx_s = refs
    g = pl.program_id(0)
    ids_down(ids_refs, col_s)
    ids_s[...] = sq_ref[...].astype(F32)
    rows, width = q_ref.shape
    heads = width // HD
    wide = heads * BLOCK
    q_s[...] = stack_heads(q_ref[...])
    do_s[...] = stack_heads(do_ref[...])
    prod = (do_ref[...].astype(F32) * o_ref[...].astype(F32)).T
    for j in range(rows // BLOCK):
        for h in range(heads):
            piece = prod[h * HD : (h + 1) * HD, j * BLOCK : (j + 1) * BLOCK]
            delta_s[:, j * wide + h * BLOCK : j * wide + (h + 1) * BLOCK] = jnp.sum(piece, axis=0, keepdims=True)
    dq_s[...] = jnp.zeros_like(dq_s) if first else dq_in[...]

    def block(j, at, out_at, qb, masked):
        stacked, part = lanes(qb, wide), lanes(qb, BLOCK)
        k = k_ref[at, :]
        k_t = k.T
        s = nt(k, q_s[stacked, :]) * SCORE - lse_ref[0, :, stacked]
        if masked:
            same = col_s[out_at, 0:1] == ids_s[:, part]
            s = jnp.where(jnp.concatenate([same] * heads, axis=1), s, MASKED)
        p = jnp.exp2(s)
        dp = nt(v_ref[at, :], do_s[stacked, :])
        ds = (p * (dp - delta_s[:, stacked])).astype(BF)
        dv = nn(p.astype(BF), do_s[stacked, :])
        dk = nn(ds, q_s[stacked, :])
        for h in range(heads):
            hs = slice(h * HD, (h + 1) * HD)
            dq_s[hs, part] += nn(k_t[hs], ds[:, h * BLOCK : (h + 1) * BLOCK])
        return dk, dv

    def visit(j, slot, kb, qb, kind):
        base = slot if len(slots) > 1 else 0
        at = pl.ds(pl.multiple_of(base * rows + kb * BLOCK, BLOCK), BLOCK)
        out_at = pl.ds(pl.multiple_of(j * rows + kb * BLOCK, BLOCK), BLOCK)

        @pl.when(qb == 0)
        def _():
            acc_k[...] = jnp.zeros(acc_k.shape, F32)
            acc_v[...] = jnp.zeros(acc_v.shape, F32)

        def add(masked):
            dk, dv = block(j, at, out_at, qb, masked)
            acc_k[...] += dk
            acc_v[...] += dv

        pl.when(kind == 1)(lambda: add(True))
        pl.when(kind == 2)(lambda: add(False))

        @pl.when(qb == rows // BLOCK - 1)
        def _():
            dk_s[out_at, :] = (acc_k[...] * HD**-0.5).astype(BF)
            dv_s[out_at, :] = acc_v[...].astype(BF)

    def scoped(acc_k_ref, acc_v_ref):
        nonlocal acc_k, acc_v
        acc_k, acc_v = acc_k_ref, acc_v_ref
        each_block(seg, where, slots, rows, visit)

    acc_k = acc_v = None
    pl.run_scoped(scoped, pltpu.VMEM((BLOCK, width), F32), pltpu.VMEM((BLOCK, width), F32))

    if last:
        dq_ref[...] = (dq_s[...] * HD**-0.5).T.astype(BF)

    @pl.when(g == 0)
    def _():
        if last:
            dx_s[:rows, :] = base_ref[...]
        else:
            dx_s[...] = jnp.zeros(dx_s.shape, F32)

    def back(j, _):
        at = pl.ds(pl.multiple_of(j * rows, rows), rows)
        dx_s[at, :] += nt(dk_s[at, :], wk_ref[...]) + nt(dv_s[at, :], wv_ref[...])
        return 0

    lax.fori_loop(0, len(slots), back, 0)
    if last:
        dx_s[:rows, :] += nt(dq_ref[...], wq_ref[...])

    @pl.when(g == pl.num_programs(0) - 1)
    def _():
        for j, dx_ref in enumerate(dx_refs):
            dx_ref[...] = dx_s[j * rows : (j + 1) * rows, :].astype(dx_ref.dtype)


def attend_backward(q, k, v, do, o, lse, slots, weights, seg, where, dq=None, base=None):
    rows, width = q.shape
    keys = rows * len(slots)
    first, last = dq is None, base is not None
    groups, wide = width // GROUP, GROUP // HD * rows
    q_spec = pl.BlockSpec((rows, GROUP), lambda i, s, w: (0, i))
    wq_spec, wk_spec, wv_spec = (
        pl.BlockSpec((None, width, GROUP), lambda i, s, w, m=m: (m, 0, i)) for _, m in weights
    )
    row_spec = pl.BlockSpec((1, 1, wide), lambda i, s, w: (i, 0, 0))
    acc_spec = pl.BlockSpec((GROUP, rows), lambda i, s, w: (i, 0))
    keys_spec = pl.BlockSpec((keys, GROUP), lambda i, s, w: (0, i))

    def ids_spec(entry):
        return pl.BlockSpec((1, rows), lambda i, s, w: (0, w[entry]))

    def slot_spec(slot):
        return pl.BlockSpec((rows, GROUP), lambda i, s, w: (slot, i))

    wq, wk, wv = (a for a, _ in weights)
    count = len(slots)
    ins = [q, do, o, lse, wk, wv, seg, k, v] + [seg] * count
    in_specs = [q_spec, q_spec, q_spec, row_spec, wk_spec, wv_spec, ids_spec(0)]
    all_spec = pl.BlockSpec((k.shape[0], GROUP), lambda i, s, w: (0, i))
    in_specs += [all_spec if count > 1 else slot_spec(slots[0])] * 2 + [ids_spec(1 + s) for s in slots]
    if not first:
        ins.append(dq)
        in_specs.append(acc_spec)
    scratch = [pltpu.VMEM((wide, GROUP), BF), pltpu.VMEM((wide, GROUP), BF), pltpu.VMEM((1, wide), F32)]
    scratch += [pltpu.VMEM((keys, 128), F32), pltpu.VMEM((1, rows), F32), pltpu.VMEM((keys, width), F32)]
    if last:
        ins += [wq, base]
        in_specs += [wq_spec, pl.BlockSpec((rows, width), lambda i, s, w: (0, 0))]
        scratch.append(pltpu.VMEM((GROUP, rows), F32))
    keys_shape = jax.ShapeDtypeStruct((keys, width), BF)
    results = [
        (keys_spec, keys_shape),
        (keys_spec, keys_shape),
        (q_spec, jax.ShapeDtypeStruct((rows, width), BF))
        if last
        else (acc_spec, jax.ShapeDtypeStruct((width, rows), F32)),
    ]
    results += [
        (
            pl.BlockSpec((rows, width), lambda i, s, w: (0, 0)),
            jax.ShapeDtypeStruct((rows, width), F32 if last else BF),
        )
    ] * count
    return pl.pallas_call(
        partial(backward_kernel, slots=slots, first=first, last=last),
        out_shape=tuple(r[1] for r in results),
        grid_spec=pltpu.PrefetchScalarGridSpec(
            num_scalar_prefetch=2,
            grid=(groups,),
            in_specs=in_specs,
            out_specs=[r[0] for r in results],
            scratch_shapes=scratch,
        ),
        cost_estimate=pl.CostEstimate(flops=FEW, bytes_accessed=FEW, transcendentals=0),
        name="attend_backward",
    )(seg[0], where, *ins)


def attn_grad_kernel(core_ref, *refs, calls, slots, block_rows):
    x_refs, dq_ref, extra_ref, refs = refs[:slots], refs[slots], refs[slots + 1], refs[slots + 2 :]
    dk_refs, dv_refs, refs = refs[:calls], refs[calls : 2 * calls], refs[2 * calls :]
    first_ref, second_ref, x_s, w_s = refs
    rows = dq_ref.shape[0]

    @pl.when(pl.program_id(0) == 0)
    def _():
        for j, x_ref in enumerate(x_refs):
            x_s[:, j * rows : (j + 1) * rows] = x_ref[...].T

    sums = [
        jnp.sum(dq_ref[...].astype(F32), axis=0, keepdims=True),
        sum(jnp.sum(d[...].astype(F32), axis=0, keepdims=True) for d in dv_refs),
        extra_ref[...],
        jnp.zeros((EXTRA - 2 - extra_ref.shape[0], w_s.shape[1]), F32),
    ]
    sums = jnp.concatenate(sums, axis=0)

    def over_keys(parts):
        total, start = 0.0, 0
        for d in parts:
            total = total + nn(x_s[:, start : start + d.shape[0]], d[...])
            start += d.shape[0]
        return total

    for m, parts in enumerate(((dq_ref,), dk_refs, dv_refs)):
        if not block_rows:
            first_ref[m] = over_keys(parts)
            continue
        w_s[...] = over_keys(parts)
        core = core_ref[0]
        at = slice(m * block_rows, (m + 1) * block_rows)
        for b in range(first_ref.shape[0]):
            far = pl.multiple_of((2 * b + 1 - core) * block_rows, block_rows)
            near = pl.multiple_of((2 * b + core) * block_rows, block_rows)
            first_ref[b, at] = w_s[pl.ds(far, block_rows), :].astype(BF)
            second_ref[b, at] = w_s[pl.ds(near, block_rows), :]
    if block_rows:
        for b in range(first_ref.shape[0]):
            first_ref[b, 3 * block_rows :] = sums.astype(BF)
            second_ref[b, 3 * block_rows :] = sums
    else:
        second_ref[...] = sums


def attn_grads(core, xs, dq, extra, dks, dvs, n):
    rows, width = dq.shape
    block_rows = width // n if (width // n) % 16 == 0 else 0
    x_spec = pl.BlockSpec((rows, width), lambda i, c: (0, 0))

    def d_spec(d):
        return pl.BlockSpec((d.shape[0], GROUP), lambda i, c: (0, i))

    if block_rows:
        shape = (n // 2, 3 * block_rows + EXTRA)
        spec = pl.BlockSpec((*shape, GROUP), lambda i, c: (0, 0, i))
        results = [(spec, jax.ShapeDtypeStruct((*shape, width), t)) for t in (BF, F32)]
    else:
        spec = pl.BlockSpec((3, width, GROUP), lambda i, c: (0, 0, i))
        results = [(spec, jax.ShapeDtypeStruct((3, width, width), F32))]
        spec = pl.BlockSpec((EXTRA, GROUP), lambda i, c: (0, i))
        results.append((spec, jax.ShapeDtypeStruct((EXTRA, width), F32)))
    return pl.pallas_call(
        partial(attn_grad_kernel, calls=len(dks), slots=len(xs), block_rows=block_rows),
        out_shape=tuple(r[1] for r in results),
        grid_spec=pltpu.PrefetchScalarGridSpec(
            num_scalar_prefetch=1,
            grid=(width // GROUP,),
            in_specs=[x_spec] * len(xs) + [d_spec(d) for d in (dq, extra, *dks, *dvs)],
            out_specs=[r[0] for r in results],
            scratch_shapes=[pltpu.VMEM((width, rows * len(xs)), BF), pltpu.VMEM((width, GROUP), F32)],
        ),
        cost_estimate=pl.CostEstimate(flops=FEW, bytes_accessed=FEW, transcendentals=0),
        name="attn_grads",
    )(core, *xs, dq, extra, *dks, *dvs)


def norm_parts(rows_in):
    mean = jnp.mean(rows_in, axis=-1, keepdims=True)
    centred = rows_in - mean
    spread = jnp.mean(centred * centred, axis=-1, keepdims=True)
    r = lax.rsqrt(spread + EPSILON)
    return centred * r, r


def norm_back(g_y, n, r, gain):
    e = g_y * gain
    return r * (e - jnp.mean(e, axis=-1, keepdims=True) - n * jnp.mean(e * n, axis=-1, keepdims=True))


def gelu_parts(u):
    c = 0.7978845608028654
    square = u * u
    th = jnp.tanh(c * u * (1.0 + 0.044715 * square))
    half = 0.5 * (1.0 + th)
    slope = half + 0.5 * u * (1.0 - th * th) * (c + 3 * 0.044715 * c * square)
    return u * half, slope


def down_rows(x):
    return jnp.sum(x, axis=0, keepdims=True)


def middle_kernel(known, *refs, count, offsets):
    w_refs, refs = (refs[:count], refs[count : 2 * count]), refs[2 * count :]
    ctx_ref, x_ref, grad_ref, vec_ref, bias_ref = refs[:5]
    out_ref, first_ref, gctx_ref, lefts_ref, rights_ref, sums_ref = refs[5:11]
    w_s, mix_ref, slope_s, n1_s, r1_s, acc_s, sems, mix_sems = refs[11:]
    parts, units = bias_ref.shape
    rows, width = x_ref.shape

    def copy(which, t, j):
        return piece_copy(
            w_refs[which], offsets[which], j, known[1], 2 * width // units + t, units, w_s.at[which, t], sems.at[which, t, j]
        )

    mix_copies = [
        piece_copy(w_refs[1], offsets[1], j, known[1], 1, width, mix_ref, mix_sems.at[j]) for j in range(count)
    ]
    for mix_copy in mix_copies:
        mix_copy.start()
    for which in range(2):
        for t in range(parts):
            for j in range(count):
                copy(which, t, j).start()
    for mix_copy in mix_copies:
        mix_copy.wait()

    def cols(t):
        return pl.ds(pl.multiple_of(t * units, units), units)

    first_sum = x_ref[...].astype(F32) + nt(ctx_ref[...], mix_ref[...]) + vec_ref[0:1, :]
    n1, r1 = norm_parts(first_sum)
    n1_s[...] = n1
    r1_s[...] = jnp.broadcast_to(r1, r1_s.shape)
    acc_s[...] = n1 * vec_ref[1:2, :] + vec_ref[2:3, :]
    lefts_ref[1] = acc_s[...].astype(BF)

    for which in range(2):
        for t in range(parts):
            for j in range(count):
                copy(which, t, j).wait()

    def up(t, _):
        pre = nn(lefts_ref[1], w_s[0, t]) + bias_ref[pl.ds(known[2 + t], 1), :]
        act, slope = gelu_parts(pre)
        slope_s[t] = slope
        low = act.astype(BF)
        rights_ref[:, cols(t)] = low
        acc_s[...] += nt(low, w_s[1, t])
        return 0

    lax.fori_loop(0, parts, up, 0)
    n2, r2 = norm_parts(acc_s[...] + vec_ref[3:4, :])
    out_ref[...] = (n2 * vec_ref[4:5, :] + vec_ref[5:6, :]).astype(BF)
    row = lax.broadcasted_iota(jnp.int32, (rows, width), 0)
    g_out = jnp.where(row < known[0], grad_ref[...].astype(F32), 0.0)
    g_second = norm_back(g_out, n2, r2, vec_ref[4:5, :])
    sums_ref[3:4, :] = down_rows(g_second)
    sums_ref[4:5, :] = down_rows(g_out * n2)
    sums_ref[5:6, :] = down_rows(g_out)
    lefts_ref[0] = g_second.astype(BF)
    acc_s[...] = g_second

    def back(t, _):
        g_pre = (nn(lefts_ref[0], w_s[1, t]) * slope_s[t]).astype(BF)
        rights_ref[:, cols(parts + t)] = g_pre
        sums_ref[pl.ds(6 + known[2 + t], 1), :] = down_rows(g_pre.astype(F32))
        acc_s[...] += nt(g_pre, w_s[0, t])
        return 0

    lax.fori_loop(0, parts, back, 0)
    g_normed = acc_s[...]
    n1 = n1_s[...]
    g_first = norm_back(g_normed, n1, r1_s[:, 0:1], vec_ref[1:2, :])
    sums_ref[0:1, :] = down_rows(g_first)
    sums_ref[1:2, :] = down_rows(g_normed * n1)
    sums_ref[2:3, :] = down_rows(g_normed)
    first_ref[...] = g_first
    low = g_first.astype(BF)
    lefts_ref[2] = low
    gctx_ref[...] = nn(low, mix_ref[...]).astype(BF)
    rights_ref[:, 2 * parts * units :] = ctx_ref[...]


def middle(known, pieces, ctx, x, grad, vectors, bias):
    rows, width = x.shape
    parts, units = bias.shape
    count = len(pieces[0])
    pieces, offsets = split_pieces(pieces)
    vmem = pl.BlockSpec(memory_space=pltpu.VMEM)
    shapes = [
        ((rows, width), BF),
        ((rows, width), F32),
        ((rows, width), BF),
        ((3, rows, width), BF),
        ((rows, 2 * parts * units + width), BF),
        ((6 + parts, width), F32),
    ]
    return pl.pallas_call(
        partial(middle_kernel, count=count, offsets=offsets),
        out_shape=tuple(jax.ShapeDtypeStruct(*s) for s in shapes),
        in_specs=[pl.BlockSpec(memory_space=pltpu.SMEM)] + [pl.BlockSpec(memory_space=pl.ANY)] * (2 * count) + [vmem] * 5,
        out_specs=[vmem] * len(shapes),
        scratch_shapes=[
            pltpu.VMEM((2, parts, width, units), BF),
            pltpu.VMEM((width, width), BF),
            pltpu.VMEM((parts, rows, units), F32),
            pltpu.VMEM((rows, width), F32),
            pltpu.VMEM((rows, 128), F32),
            pltpu.VMEM((rows, width), F32),
            pltpu.SemaphoreType.DMA((2, parts, count)),
            pltpu.SemaphoreType.DMA((count,)),
        ],
        compiler_params=pltpu.CompilerParams(vmem_limit_bytes=63 << 20),
        cost_estimate=pl.CostEstimate(flops=FEW, bytes_accessed=FEW, transcendentals=0),
        name="middle",
    )(known, *pieces[0], *pieces[1], ctx, x, grad, vectors, bias)


def ffn_grad_kernel(place, left_ref, right_ref, kept_1, kept_2, sent_1, sent_2, left_s, chosen_s, *, n):
    half = kept_1.shape[0]

    @pl.when(pl.program_id(0) % 4 == 0)
    def _():
        left_s[...] = left_ref[0].T
        size = left_s.shape[0] // n
        if size % 16:
            chosen_s[...] = left_s[...]
        else:
            for j in range(n):
                core, outer = j // (n // 2), j % (n // 2)
                block = place[0] ^ (2 * outer + core)
                chosen_s[j * size : (j + 1) * size, :] = left_s[pl.ds(pl.multiple_of(block * size, size), size), :]

    total = nn(chosen_s[...], right_ref[...])

    def put(kept_ref, sent_ref):
        kept_ref[...] = total[:half].astype(BF)
        sent_ref[...] = total[half:].astype(BF)

    pl.when(pl.program_id(0) < 4)(lambda: put(kept_1, sent_1))
    pl.when(pl.program_id(0) >= 4)(lambda: put(kept_2, sent_2))


def ffn_grads(place, lefts, rights, n):
    _, rows, width = lefts.shape
    units = rights.shape[1] // 9
    first_spec = pl.BlockSpec((width // 2, units), lambda i, p: (0, jnp.minimum(i, 3)))
    second_spec = pl.BlockSpec((width // 2, units), lambda i, p: (0, jnp.maximum(i - 4, 0)))
    first_shape, second_shape = (jax.ShapeDtypeStruct((width // 2, k * units), BF) for k in (4, 5))
    return pl.pallas_call(
        partial(ffn_grad_kernel, n=n),
        out_shape=(first_shape, second_shape) * 2,
        grid_spec=pltpu.PrefetchScalarGridSpec(
            num_scalar_prefetch=1,
            grid=(9,),
            in_specs=[
                pl.BlockSpec((1, rows, width), lambda i, p: (i // 4, 0, 0)),
                pl.BlockSpec((rows, units), lambda i, p: (0, i)),
            ],
            out_specs=[first_spec, second_spec] * 2,
            scratch_shapes=[pltpu.VMEM((width, rows), BF), pltpu.VMEM((width, rows), BF)],
        ),
        cost_estimate=pl.CostEstimate(flops=FEW, bytes_accessed=FEW, transcendentals=0),
        name="ffn_grads",
    )(place, lefts, rights)


def finish_kernel(*refs, r):
    terms, refs = refs[:4], refs[4:]
    total = sum(t[...].astype(F32) for t in terms)
    for m in range(3):
        refs[m][...] = total[m * r : (m + 1) * r]
    base = 3 * r

    def row(*at):
        return jnp.concatenate([total[base + i : base + i + 1] for i in at], axis=1)[0]

    for w in range(2):
        refs[3 + w][...] = row(*(2 * i + w for i in range(4)))
    for j in range(6):
        refs[5 + j][...] = row(*(8 + 10 * i + j for i in range(4)))
    refs[11][...] = row(*(8 + 10 * i + j for j in range(6, 10) for i in range(4)))


def finish(terms, r, width, units):
    cols = terms[0].shape[1]
    shapes = [(r, cols)] * 3 + [(width,)] * 8 + [(4 * units,)]
    vmem = pl.BlockSpec(memory_space=pltpu.VMEM)
    return pl.pallas_call(
        partial(finish_kernel, r=r),
        out_shape=tuple(jax.ShapeDtypeStruct(x, F32) for x in shapes),
        in_specs=[vmem] * 4,
        out_specs=[vmem] * len(shapes),
        cost_estimate=pl.CostEstimate(flops=FEW, bytes_accessed=FEW, transcendentals=0),
        name="finish",
    )(*terms)


def on_device(
    tokens,
    segments,
    query_weight,
    query_bias,
    key_weight,
    value_weight,
    value_bias,
    mix_weight,
    mix_bias,
    norm_gain,
    norm_shift,
    up_weight,
    up_bias,
    down_weight,
    down_bias,
    final_gain,
    final_shift,
    out_grad,
):
    t = lax.axis_index("tensor")
    f = lax.axis_index("fsdp")
    n = lax.axis_size("fsdp")
    rows, width = tokens.shape
    r, units = up_weight.shape
    cols = query_weight.shape[1]
    owner = slot_owner(t)

    def by_slot(vector):
        parts = vector.reshape(4, -1)
        return jnp.concatenate([lax.dynamic_slice_in_dim(parts, owner[i], 1, axis=0)[0] for i in range(4)])

    seg = jnp.where(segments == 0, 9, segments)
    where = jnp.concatenate([t[None], owner, (f & 1)[None], f[None]]).astype(jnp.int32)
    own_ids = lax.dynamic_slice_in_dim(seg[0], t * rows, rows)
    known = jnp.concatenate([jnp.stack([jnp.sum((own_ids < 9).astype(jnp.int32)), f]), owner]).astype(jnp.int32)
    vectors = jnp.stack([mix_bias, norm_gain, norm_shift, down_bias, final_gain, final_shift])
    shifts = (by_slot(query_bias), by_slot(value_bias))
    slot_of = owner_slot(t)
    goals = [sum(jnp.where(owner[k] == lax.rem(t + shift, 4), k, 0) for k in range(4)) for shift in SHIFTS]
    seg, where, known, vectors, shifts, slot_of, goals = lax.optimization_barrier(
        (seg, where, known, vectors, shifts, slot_of, goals)
    )
    small_operands = (seg, where, known, vectors, *shifts, *slot_of, *goals)

    shard = jnp.stack(
        [
            jnp.concatenate([query_weight, key_weight, value_weight, mix_weight.T], axis=1),
            up_weight,
            down_weight.T,
        ]
    )
    w_a, w_below, w_above = line_first(shard)
    w_c = after(line_second(w_below, w_above), *small_operands)
    w_b = line_third(w_c, w_below)
    w_slots = (shard, w_a, w_c, w_b)
    x_a, x_below, x_above = line_first(after(tokens, w_c))

    line = []
    for first, last in ((0, 1), (2, 2)):
        line += [w[0][:, m * cols : (m + 1) * cols] for m in (first, first + 1) for w in w_slots]
        line += [w[last] for w in w_slots]
    own = jnp.concatenate(line, axis=1)
    wide = own.shape[1] // 2
    bits = outer_bits()

    def over(block, bit):
        return lax.ppermute(block, "fsdp", partner(bit))

    if len(bits) == 2:
        beside = [over(own, bit) for bit in bits]
        far_own = over(own, 1)
        x_c = line_second(*after((x_below, x_above), far_own))
        beside = after(beside, x_a, x_c)
        across = [over(beside[0][:, :wide], bits[1]), over(beside[1][:, wide:], bits[0])]
        far_beside = [over(b, 1) for b in beside]
        x_b = line_third(x_c, x_below, *far_beside)
        far_across = [over(a, 1) for a in across]
        pieces = [
            [
                piece
                for o, b, a in ((own, beside, across), (far_own, far_beside, far_across))
                for piece in ((o, i * wide), (b[0], i * wide), (b[1], i * wide), (a[i], 0))
            ]
            for i in range(2)
        ]
    else:
        x_c = line_second(x_below, x_above)
        x_b = line_third(x_c, x_below)
        held = {0: after(own, x_a)}
        for bit in bits:
            held.update({place | (bit >> 1): over(block, bit) for place, block in sorted(held.items())})
        near = [held[p] for p in sorted(held)]
        far = [over(block, 1) for block in near]
        pieces = [[(block, i * wide) for block in near + far] for i in range(2)]
    if r % 16:
        pieces = [[(assembled([p[0][:, p[1] : p[1] + wide] for p in half]), 0)] for half in pieces]

    xs = (tokens, x_a, x_c, x_b)
    q, k, v, ctx, lse, w_all = attend_forward(xs, pieces, shifts, seg, where)
    weights = tuple((w_all, m) for m in range(3))

    layer_out, g_first, g_ctx, lefts, rights, extra = middle(
        known, pieces, ctx, tokens, out_grad, vectors, up_bias.reshape(4, units)
    )
    place = f.astype(jnp.int32)[None]
    *kept, sent_1, sent_2 = ffn_grads(place, lefts, rights, n)
    sent = [sent_1, sent_2]
    if r % 16:
        full = [jnp.concatenate(pair).reshape(n, r, -1) for pair in zip(kept, sent)]
        kept, sent = (
            [
                jnp.concatenate([lax.dynamic_slice_in_dim(x, f ^ (2 * q + c), 1)[0] for q in range(n // 2)])
                for x in full
            ]
            for c in range(2)
        )
    got = [lax.ppermute(x, "fsdp", partner(1)) for x in sent]
    g_ctx = after(g_ctx, *sent)

    args = (q, k, v, g_ctx, ctx, lse)
    dk_n, dv_n, dq, dx_b, dx_c, dx_a = attend_backward(*args, (3, 2, 1), weights, seg, where)
    r1 = lax.ppermute(dx_b, "tensor", [(0, 1), (3, 2)])
    steps = list(zip(outer_bits(), outer_bits()[::-1]))
    got = after(got, dx_b)
    held = [outer_axes(x) for x in kept]
    come = [outer_axes(x)[0] for x in got]
    lefts = [h[1] for h in held]
    held = [h[0] for h in held]
    axes = [left.index(bit) for left, bit in zip(lefts, steps[0])]

    def at(blocks, index):
        return [lax.index_in_dim(b, index, axis, keepdims=False) for b, axis in zip(blocks, axes)]

    out_halves = add_low(at(held, 1), at(come, 1))
    arrived = [lax.ppermute(o, "fsdp", partner(bit)) for o, bit in zip(out_halves, steps[0])]
    dk_o, dv_o, dq, dx_own = attend_backward(
        *args, (0,), weights, seg, where, after(dq, dx_b, *out_halves), g_first
    )
    middle_x = (dx_c.astype(F32) + after(r1, dx_own).astype(F32)).astype(BF)
    rx = lax.ppermute(middle_x, "tensor", [(0, 1), (3, 2)])
    ry = lax.ppermute(middle_x, "tensor", [(1, 2), (2, 1)])

    arrived, held, come = after((arrived, held, come), dx_own)
    blocks = [
        (a.astype(F32) + b.astype(F32) + c.astype(F32)).astype(BF)
        for a, b, c in zip(at(held, 0), at(come, 0), arrived)
    ]
    lefts = [[b for b in left if b != bit] for left, bit in zip(lefts, steps[0])]
    halves, out_halves = start_halving(blocks, lefts, steps[1])

    xs = (xs[0], xs[3], xs[2], xs[1])
    dq = after(dq, middle_x, *out_halves)
    sent, kept = attn_grads(where[5:6], xs, dq, extra, (dk_o, dk_n), (dv_o, dv_n), n)
    if r % 16:
        split = sent.reshape(3, n // 2, 2, r, width)
        sums = jnp.broadcast_to(kept, (n // 2, EXTRA, width))
        sent, kept = (
            jnp.concatenate(
                [
                    lax.dynamic_index_in_dim(split, c, 2, keepdims=False)
                    .transpose(1, 0, 2, 3)
                    .reshape(n // 2, 3 * r, width),
                    sums,
                ],
                axis=1,
            )
            for c in (1 - (f & 1), f & 1)
        )
        sent = sent.astype(BF)
    got = lax.ppermute(sent, "fsdp", partner(1))
    near = (kept + got.astype(F32)).astype(BF)
    rx, ry = (a.astype(F32) for a in after((rx, ry), sent))
    up_x = (dx_a.astype(F32) + jnp.where(t == 1, rx, ry)).astype(BF)
    down_x = jnp.where(t == 3, dx_a.astype(F32), dx_b.astype(F32) + jnp.where(t == 1, ry, rx)).astype(BF)
    from_below = lax.ppermute(up_x, "tensor", [(0, 1), (1, 2), (2, 3)])
    from_above = lax.ppermute(down_x, "tensor", [(1, 0), (2, 1), (3, 2)])

    d_one, d_two = add_low(halves[0], after(halves[1], sent))
    for pair in steps[2:]:
        halves, _ = start_halving([d_one, d_two], halves[2], pair)
        d_one, d_two = add_low(halves[0], halves[1])
    early = jnp.stack(
        [
            jnp.concatenate(
                [
                    d_one[:, i * units : (i + 1) * units],
                    d_two[:, i * units : (i + 1) * units],
                    d_two[:, 4 * units + i * cols : 4 * units + (i + 1) * cols],
                ],
                axis=1,
            )
            for i in range(4)
        ]
    )

    early_own, early = early[0], spread(early, goals)
    same_core = [list(range(c, n, 2)) for c in range(2)]
    arrived = lax.all_to_all(near, "fsdp", split_axis=0, concat_axis=0, axis_index_groups=same_core, tiled=True)
    arrived = after(arrived, *early)
    late = jnp.sum(arrived.astype(F32), axis=0).astype(BF)
    count = 12
    by_head = jnp.stack([late[3 * r : 3 * r + 2, i * cols : (i + 1) * cols] for i in range(4)])
    by_head = in_line_order(by_head, slot_of).reshape(8, cols)
    whole = [late[3 * r + 2 : 3 * r + count, i * cols : (i + 1) * cols] for i in range(4)]
    below = jnp.concatenate([by_head, *whole])
    late = jnp.stack(
        [jnp.concatenate([late[: 3 * r, i * cols : (i + 1) * cols], below]) for i in range(4)]
    )
    *late, qb, vb, b0, b1, b2, b3, b4, b5, up_sums = finish((late[0], *spread(late, goals)), r, width, units)
    early = total(early_own, early)
    tokens_grad = dx_own + from_below.astype(F32) + from_above.astype(F32)

    return (
        layer_out,
        tokens_grad,
        late[0],
        qb,
        late[1],
        late[2],
        vb,
        early[:, 2 * units :].T,
        b0,
        b1,
        b2,
        early[:, units : 2 * units],
        up_sums,
        early[:, :units].T,
        b3,
        b4,
        b5,
    )


def solution(mesh):
    both, rows_f, square, flipped = (
        P(("fsdp", "tensor"), None),
        P("fsdp", None),
        P("fsdp", "tensor"),
        P("tensor", "fsdp"),
    )
    return jax.shard_map(
        on_device,
        mesh=mesh,
        in_specs=(
            both, rows_f, square, P(), square, square, P(), flipped, P(), P(), P(),
            square, P(), flipped, P(), P(), P(), both,
        ),
        out_specs=(
            both, both, square, P(), square, square, P(), flipped, P(), P(), P(),
            square, P(), flipped, P(), P(), P(),
        ),
        check_vma=False,
    )
```

```python
from functools import partial

import jax
import jax.numpy as jnp
from jax import lax
from jax.experimental import pallas as pl
from jax.experimental.pallas import tpu as pltpu
from jax.sharding import PartitionSpec as P

HD = 64
GROUP = 256
BLOCK = 256
EPSILON = 1e-05
MASKED = -1e30
LOG2E = 1.4426950408889634
SCORE = HD**-0.5 * LOG2E
EXTRA = 16
SHIFTS = (1, 3, 2)
FEW = 1000
BF = jnp.bfloat16
F32 = jnp.float32


def after(value, *others):
    return lax.optimization_barrier((value,) + others)[0] if others else value


def nt(a, b):
    return lax.dot_general(a, b, (((1,), (1,)), ((), ())), preferred_element_type=F32)


def nn(a, b):
    return lax.dot_general(a, b, (((1,), (0,)), ((), ())), preferred_element_type=F32)


def line_first(own):
    below = lax.ppermute(own, "tensor", [(0, 1), (1, 2), (2, 3)])
    above = lax.ppermute(own, "tensor", [(1, 0), (2, 1), (3, 2)])
    return jnp.where(lax.axis_index("tensor") < 3, above, below), below, above


def line_second(below, above, *gate):
    below2 = lax.ppermute(below, "tensor", [(1, 2), (2, 3)])
    above2 = lax.ppermute(above, "tensor", [(2, 1), (1, 0)])
    below2, above2 = after((below2, above2), *gate)
    return jnp.where(lax.axis_index("tensor") < 2, above2, below2)


def line_third(slot_c, below, *gate):
    far = after(lax.ppermute(slot_c, "tensor", [(1, 0), (2, 3)]), *gate)
    t = lax.axis_index("tensor")
    return jnp.where((t == 0) | (t == 3), far, below)


def slot_owner(t):
    return jnp.stack([t, jnp.where(t < 3, t + 1, 2), lax.rem(t + 2, 4), jnp.where(t == 3, 0, lax.rem(t + 3, 4))])


def owner_slot(t):
    owner = slot_owner(t)
    return [sum(jnp.where(owner[k] == j, k, 0) for k in range(4)) for j in range(4)]


def in_line_order(slots, slot_of):
    return jnp.concatenate([lax.dynamic_slice_in_dim(slots, s, 1, axis=0) for s in slot_of])


def spread(slots, goals):
    arrived = []
    for shift, slot in zip(SHIFTS, goals):
        block = lax.dynamic_index_in_dim(slots, slot, 0, keepdims=False)
        arrived.append(lax.ppermute(block, "tensor", [(i, (i + shift) % 4) for i in range(4)]))
    return arrived


def total(own, arrived):
    return own.astype(F32) + sum(a.astype(F32) for a in arrived)


def partner(bit):
    n = lax.axis_size("fsdp")
    return [(i, i ^ bit) for i in range(n)]


def outer_bits():
    n = lax.axis_size("fsdp")
    return [1 << k for k in range(1, n.bit_length() - 1)]


def assembled(pieces):
    n = len(pieces)
    f = lax.axis_index("fsdp")
    stacked = jnp.stack(pieces).reshape(2, n // 2, *pieces[0].shape)
    blocks = []
    for a in range(n):
        rel = f ^ a
        block = lax.dynamic_slice_in_dim(stacked, rel & 1, 1, axis=0)
        blocks.append(lax.dynamic_slice_in_dim(block, rel >> 1, 1, axis=1)[0, 0])
    return jnp.concatenate(blocks)


def outer_axes(block):
    n = lax.axis_size("fsdp")
    bits = outer_bits()
    return block.reshape((2,) * len(bits) + (block.shape[0] // (n // 2), block.shape[1])), sorted(bits, reverse=True)


def start_halving(blocks, lefts, pair):
    kept, arrived, rest, sent = [], [], [], []
    for block, left, bit in zip(blocks, lefts, pair):
        axis = left.index(bit)
        kept.append(lax.index_in_dim(block, 0, axis, keepdims=False))
        sent.append(lax.index_in_dim(block, 1, axis, keepdims=False))
        arrived.append(lax.ppermute(sent[-1], "fsdp", partner(bit)))
        rest.append([b for b in left if b != bit])
    return (kept, arrived, rest), sent


def add_low(kept, arrived):
    return [(a.astype(F32) + b.astype(F32)).astype(BF) for a, b in zip(kept, arrived)]


def stack_heads(x):
    lane = lax.broadcasted_iota(jnp.int32, (BLOCK, x.shape[1]), 1)
    zero = jnp.zeros((BLOCK, x.shape[1]), x.dtype)
    heads = x.shape[1] // HD
    return jnp.concatenate(
        [
            jnp.where((lane >= h * HD) & (lane < (h + 1) * HD), x[j * BLOCK : (j + 1) * BLOCK], zero)
            for j in range(x.shape[0] // BLOCK)
            for h in range(heads)
        ],
        axis=0,
    )


def block_kind(seg, q_at, k_at):
    q_lo, q_hi = seg[q_at], seg[q_at + BLOCK - 1]
    k_lo, k_hi = seg[k_at], seg[k_at + BLOCK - 1]
    meet = (q_lo <= k_hi) & (k_lo <= q_hi)
    one = (q_lo == q_hi) & (k_lo == q_lo) & (k_hi == q_lo)
    return jnp.where(one, 2, jnp.where(meet, 1, 0))


def ids_down(ids_refs, col_s):
    rows = ids_refs[0].shape[1]

    @pl.when(pl.program_id(0) == 0)
    def _():
        for j, ids in enumerate(ids_refs):
            wide = jnp.broadcast_to(ids[...].astype(F32), (col_s.shape[1], rows))
            col_s[j * rows : (j + 1) * rows, :] = wide.T


def each_block(seg, where, slots, rows, visit):
    per = rows // BLOCK
    stride = slots[1] - slots[0] if len(slots) > 1 else 0

    def step(i, _):
        j, pair = i // (per * per), lax.rem(i, per * per)
        kb, qb = pair // per, lax.rem(pair, per)
        slot = slots[0] + stride * j
        kind = block_kind(seg, where[0] * rows + qb * BLOCK, where[1 + slot] * rows + kb * BLOCK)
        visit(j, slot, kb, qb, kind)
        return 0

    lax.fori_loop(0, len(slots) * per * per, step, 0)


def split_pieces(pieces):
    return [[p[0] for p in half] for half in pieces], tuple(tuple(p[1] for p in half) for half in pieces)


def piece_copy(pieces, offsets, j, f, column, width, target, sem):
    r = pieces[0].shape[0]
    place = 0
    if len(pieces) > 1:
        core, outer = j // (len(pieces) // 2), j % (len(pieces) // 2)
        place = f ^ (2 * outer + core)
    rows = pl.ds(pl.multiple_of(place * r, r), r)
    start = offsets[j] + column * width
    return pltpu.make_async_copy(
        pieces[j].at[:, start : start + width], target.at[rows, :], sem
    )


def lanes(index, size):
    return pl.ds(pl.multiple_of(index * size, size), size)


def forward_kernel(seg, where, *refs, slots, count, offsets):
    refs = list(refs)

    def take(count):
        taken, refs[:] = refs[:count], refs[count:]
        return taken

    x_refs = take(len(slots))
    ids_refs = take(len(slots))
    pieces = (take(count), take(count))
    bq_ref, bv_ref, sq_ref = take(3)
    q_ref, k_ref, v_ref, o_ref, lse_ref, w_ref, q_s, col_s, m_s, l_s, acc_s, ids_s, w_s, sems = refs

    @pl.when(pl.program_id(0) == 0)
    def _():
        copies = [
            piece_copy(pieces[m // 2], offsets[m // 2], j, where[6], m % 2, w_s.shape[2], w_s.at[m], sems.at[m, j])
            for m in range(3)
            for j in range(count)
        ]
        for copy in copies:
            copy.start()
        for copy in copies:
            copy.wait()

    w_ref[...] = w_s[:, :, lanes(pl.program_id(0), q_ref.shape[1])]
    wq_ref, wk_ref, wv_ref = (w_ref.at[m] for m in range(3))
    rows, width = q_ref.shape
    heads = width // HD
    wide = heads * BLOCK
    q_ref[...] = (nn(x_refs[0][...], wq_ref[...]) + bq_ref[...]).astype(BF)
    m_s[...] = jnp.full(m_s.shape, MASKED, F32)
    l_s[...] = jnp.zeros(l_s.shape, F32)
    acc_s[...] = jnp.zeros(acc_s.shape, F32)
    for j, x_ref in enumerate(x_refs):
        at = slice(j * rows, (j + 1) * rows)
        k_ref[at, :] = nn(x_ref[...], wk_ref[...]).astype(BF)
        v_ref[at, :] = (nn(x_ref[...], wv_ref[...]) + bv_ref[...]).astype(BF)
    q_s[...] = stack_heads(q_ref[...])
    ids_down(ids_refs, col_s)
    ids_s[...] = sq_ref[...].astype(F32)

    def block(at, qb, masked):
        stacked, part = lanes(qb, wide), lanes(qb, BLOCK)
        s = nt(k_ref[at, :], q_s[stacked, :])
        if masked:
            same = col_s[at, 0:1] == ids_s[:, part]
            s = jnp.where(jnp.concatenate([same] * heads, axis=1), s, MASKED)
        m_old = m_s[:, stacked]
        m_new = jnp.maximum(m_old, jnp.max(s, axis=0, keepdims=True))
        alpha = jnp.exp2((m_old - m_new) * SCORE)
        p = jnp.exp2((s - m_new) * SCORE)
        p_low = p.astype(BF)
        l_s[:, stacked] = alpha * l_s[:, stacked] + jnp.sum(p, axis=0, keepdims=True)
        m_s[:, stacked] = m_new
        v_t = v_ref[at, :].T
        for h in range(heads):
            hs, qs = slice(h * HD, (h + 1) * HD), slice(h * BLOCK, (h + 1) * BLOCK)
            acc_s[hs, part] = acc_s[hs, part] * alpha[:, qs] + nn(v_t[hs], p_low[:, qs])

    def visit(j, _, kb, qb, kind):
        at = pl.ds(pl.multiple_of(j * rows + kb * BLOCK, BLOCK), BLOCK)
        pl.when(kind == 1)(lambda: block(at, qb, True))
        pl.when(kind == 2)(lambda: block(at, qb, False))

    each_block(seg, where, slots, rows, visit)
    for j in range(rows // BLOCK):
        inverse = 1.0 / l_s[:, j * wide : (j + 1) * wide]
        spread_out = jnp.concatenate(
            [jnp.broadcast_to(inverse[:, h * BLOCK : (h + 1) * BLOCK], (HD, BLOCK)) for h in range(heads)], axis=0
        )
        at = slice(j * BLOCK, (j + 1) * BLOCK)
        o_ref[at, :] = (acc_s[:, at] * spread_out).T.astype(BF)
    lse_ref[0] = m_s[...] * SCORE + jnp.log2(l_s[...])


def attend_forward(xs, pieces, biases, seg, where):
    rows, width = xs[0].shape
    slots = tuple(range(len(xs)))
    keys = rows * len(xs)
    count = len(pieces[0])
    pieces, offsets = split_pieces(pieces)
    groups, wide = width // GROUP, GROUP // HD * rows
    block_spec = pl.BlockSpec((rows, GROUP), lambda i, s, w: (0, i))
    keys_spec = pl.BlockSpec((keys, GROUP), lambda i, s, w: (0, i))
    b_spec = pl.BlockSpec((1, GROUP), lambda i, s, w: (0, i))
    row_spec = pl.BlockSpec((1, 1, wide), lambda i, s, w: (i, 0, 0))
    block_shape = jax.ShapeDtypeStruct((rows, width), BF)
    keys_shape = jax.ShapeDtypeStruct((keys, width), BF)

    def ids_spec(entry):
        return pl.BlockSpec((1, rows), lambda i, s, w: (0, w[entry]))

    in_specs = [pl.BlockSpec((rows, width), lambda i, s, w: (0, 0))] * len(xs)
    in_specs += [ids_spec(1 + s) for s in slots] + [pl.BlockSpec(memory_space=pl.ANY)] * (2 * count) + [b_spec] * 2 + [ids_spec(0)]
    return pl.pallas_call(
        partial(forward_kernel, slots=slots, count=count, offsets=offsets),
        out_shape=(
            block_shape,
            keys_shape,
            keys_shape,
            block_shape,
            jax.ShapeDtypeStruct((groups, 1, wide), F32),
            jax.ShapeDtypeStruct((3, width, width), BF),
        ),
        grid_spec=pltpu.PrefetchScalarGridSpec(
            num_scalar_prefetch=2,
            grid=(groups,),
            in_specs=in_specs,
            out_specs=[
                block_spec, keys_spec, keys_spec, block_spec, row_spec,
                pl.BlockSpec((3, width, GROUP), lambda i, s, w: (0, 0, i)),
            ],
            scratch_shapes=[
                pltpu.VMEM((wide, GROUP), BF),
                pltpu.VMEM((keys, 128), F32),
                pltpu.VMEM((1, wide), F32),
                pltpu.VMEM((1, wide), F32),
                pltpu.VMEM((GROUP, rows), F32),
                pltpu.VMEM((1, rows), F32),
                pltpu.VMEM((3, width, width), BF),
                pltpu.SemaphoreType.DMA((3, count)),
            ],
        ),
        cost_estimate=pl.CostEstimate(flops=FEW, bytes_accessed=FEW, transcendentals=0),
        name="attend_forward",
    )(seg[0], where, *xs, *([seg] * len(slots)), *pieces[0], *pieces[1], *(b[None, :] for b in biases), seg)


def backward_kernel(seg, where, *refs, slots, first, last):
    refs = list(refs)

    def take(count):
        taken, refs[:] = refs[:count], refs[count:]
        return taken

    q_ref, do_ref, o_ref, lse_ref, wk_ref, wv_ref, sq_ref = take(7)
    (k_ref, v_ref), ids_refs = take(2), take(len(slots))
    if not first:
        (dq_in,) = take(1)
    if last:
        wq_ref, base_ref = take(2)
        dk_s, dv_s, dq_ref = take(3)
        dx_refs = take(len(slots))
        q_s, do_s, delta_s, col_s, ids_s, dx_s, dq_s = refs
    else:
        dk_s, dv_s, dq_s = take(3)
        dx_refs = take(len(slots))
        q_s, do_s, delta_s, col_s, ids_s, dx_s = refs
    g = pl.program_id(0)
    ids_down(ids_refs, col_s)
    ids_s[...] = sq_ref[...].astype(F32)
    rows, width = q_ref.shape
    heads = width // HD
    wide = heads * BLOCK
    q_s[...] = stack_heads(q_ref[...])
    do_s[...] = stack_heads(do_ref[...])
    prod = (do_ref[...].astype(F32) * o_ref[...].astype(F32)).T
    for j in range(rows // BLOCK):
        for h in range(heads):
            piece = prod[h * HD : (h + 1) * HD, j * BLOCK : (j + 1) * BLOCK]
            delta_s[:, j * wide + h * BLOCK : j * wide + (h + 1) * BLOCK] = jnp.sum(piece, axis=0, keepdims=True)
    dq_s[...] = jnp.zeros_like(dq_s) if first else dq_in[...]

    def block(j, at, out_at, qb, masked):
        stacked, part = lanes(qb, wide), lanes(qb, BLOCK)
        k = k_ref[at, :]
        k_t = k.T
        s = nt(k, q_s[stacked, :]) * SCORE - lse_ref[0, :, stacked]
        if masked:
            same = col_s[out_at, 0:1] == ids_s[:, part]
            s = jnp.where(jnp.concatenate([same] * heads, axis=1), s, MASKED)
        p = jnp.exp2(s)
        dp = nt(v_ref[at, :], do_s[stacked, :])
        ds = (p * (dp - delta_s[:, stacked])).astype(BF)
        dv = nn(p.astype(BF), do_s[stacked, :])
        dk = nn(ds, q_s[stacked, :])
        for h in range(heads):
            hs = slice(h * HD, (h + 1) * HD)
            dq_s[hs, part] += nn(k_t[hs], ds[:, h * BLOCK : (h + 1) * BLOCK])
        return dk, dv

    def visit(j, slot, kb, qb, kind):
        base = slot if len(slots) > 1 else 0
        at = pl.ds(pl.multiple_of(base * rows + kb * BLOCK, BLOCK), BLOCK)
        out_at = pl.ds(pl.multiple_of(j * rows + kb * BLOCK, BLOCK), BLOCK)

        @pl.when(qb == 0)
        def _():
            acc_k[...] = jnp.zeros(acc_k.shape, F32)
            acc_v[...] = jnp.zeros(acc_v.shape, F32)

        def add(masked):
            dk, dv = block(j, at, out_at, qb, masked)
            acc_k[...] += dk
            acc_v[...] += dv

        pl.when(kind == 1)(lambda: add(True))
        pl.when(kind == 2)(lambda: add(False))

        @pl.when(qb == rows // BLOCK - 1)
        def _():
            dk_s[out_at, :] = (acc_k[...] * HD**-0.5).astype(BF)
            dv_s[out_at, :] = acc_v[...].astype(BF)

    def scoped(acc_k_ref, acc_v_ref):
        nonlocal acc_k, acc_v
        acc_k, acc_v = acc_k_ref, acc_v_ref
        each_block(seg, where, slots, rows, visit)

    acc_k = acc_v = None
    pl.run_scoped(scoped, pltpu.VMEM((BLOCK, width), F32), pltpu.VMEM((BLOCK, width), F32))

    if last:
        dq_ref[...] = (dq_s[...] * HD**-0.5).T.astype(BF)

    @pl.when(g == 0)
    def _():
        if last:
            dx_s[:rows, :] = base_ref[...]
        else:
            dx_s[...] = jnp.zeros(dx_s.shape, F32)

    def back(j, _):
        at = pl.ds(pl.multiple_of(j * rows, rows), rows)
        dx_s[at, :] += nt(dk_s[at, :], wk_ref[...]) + nt(dv_s[at, :], wv_ref[...])
        return 0

    lax.fori_loop(0, len(slots), back, 0)
    if last:
        dx_s[:rows, :] += nt(dq_ref[...], wq_ref[...])

    @pl.when(g == pl.num_programs(0) - 1)
    def _():
        for j, dx_ref in enumerate(dx_refs):
            dx_ref[...] = dx_s[j * rows : (j + 1) * rows, :].astype(dx_ref.dtype)


def attend_backward(q, k, v, do, o, lse, slots, weights, seg, where, dq=None, base=None):
    rows, width = q.shape
    keys = rows * len(slots)
    first, last = dq is None, base is not None
    groups, wide = width // GROUP, GROUP // HD * rows
    q_spec = pl.BlockSpec((rows, GROUP), lambda i, s, w: (0, i))
    wq_spec, wk_spec, wv_spec = (
        pl.BlockSpec((None, width, GROUP), lambda i, s, w, m=m: (m, 0, i)) for _, m in weights
    )
    row_spec = pl.BlockSpec((1, 1, wide), lambda i, s, w: (i, 0, 0))
    acc_spec = pl.BlockSpec((GROUP, rows), lambda i, s, w: (i, 0))
    keys_spec = pl.BlockSpec((keys, GROUP), lambda i, s, w: (0, i))

    def ids_spec(entry):
        return pl.BlockSpec((1, rows), lambda i, s, w: (0, w[entry]))

    def slot_spec(slot):
        return pl.BlockSpec((rows, GROUP), lambda i, s, w: (slot, i))

    wq, wk, wv = (a for a, _ in weights)
    count = len(slots)
    ins = [q, do, o, lse, wk, wv, seg, k, v] + [seg] * count
    in_specs = [q_spec, q_spec, q_spec, row_spec, wk_spec, wv_spec, ids_spec(0)]
    all_spec = pl.BlockSpec((k.shape[0], GROUP), lambda i, s, w: (0, i))
    in_specs += [all_spec if count > 1 else slot_spec(slots[0])] * 2 + [ids_spec(1 + s) for s in slots]
    if not first:
        ins.append(dq)
        in_specs.append(acc_spec)
    scratch = [pltpu.VMEM((wide, GROUP), BF), pltpu.VMEM((wide, GROUP), BF), pltpu.VMEM((1, wide), F32)]
    scratch += [pltpu.VMEM((keys, 128), F32), pltpu.VMEM((1, rows), F32), pltpu.VMEM((keys, width), F32)]
    if last:
        ins += [wq, base]
        in_specs += [wq_spec, pl.BlockSpec((rows, width), lambda i, s, w: (0, 0))]
        scratch.append(pltpu.VMEM((GROUP, rows), F32))
    keys_shape = jax.ShapeDtypeStruct((keys, width), BF)
    results = [
        (keys_spec, keys_shape),
        (keys_spec, keys_shape),
        (q_spec, jax.ShapeDtypeStruct((rows, width), BF))
        if last
        else (acc_spec, jax.ShapeDtypeStruct((width, rows), F32)),
    ]
    results += [
        (
            pl.BlockSpec((rows, width), lambda i, s, w: (0, 0)),
            jax.ShapeDtypeStruct((rows, width), F32 if last else BF),
        )
    ] * count
    return pl.pallas_call(
        partial(backward_kernel, slots=slots, first=first, last=last),
        out_shape=tuple(r[1] for r in results),
        grid_spec=pltpu.PrefetchScalarGridSpec(
            num_scalar_prefetch=2,
            grid=(groups,),
            in_specs=in_specs,
            out_specs=[r[0] for r in results],
            scratch_shapes=scratch,
        ),
        cost_estimate=pl.CostEstimate(flops=FEW, bytes_accessed=FEW, transcendentals=0),
        name="attend_backward",
    )(seg[0], where, *ins)


def attn_grad_kernel(core_ref, *refs, calls, slots, block_rows):
    x_refs, dq_ref, extra_ref, refs = refs[:slots], refs[slots], refs[slots + 1], refs[slots + 2 :]
    dk_refs, dv_refs, refs = refs[:calls], refs[calls : 2 * calls], refs[2 * calls :]
    first_ref, second_ref, x_s, w_s = refs
    rows = dq_ref.shape[0]

    @pl.when(pl.program_id(0) == 0)
    def _():
        for j, x_ref in enumerate(x_refs):
            x_s[:, j * rows : (j + 1) * rows] = x_ref[...].T

    sums = [
        jnp.sum(dq_ref[...].astype(F32), axis=0, keepdims=True),
        sum(jnp.sum(d[...].astype(F32), axis=0, keepdims=True) for d in dv_refs),
        extra_ref[...],
        jnp.zeros((EXTRA - 2 - extra_ref.shape[0], w_s.shape[1]), F32),
    ]
    sums = jnp.concatenate(sums, axis=0)

    def over_keys(parts):
        total, start = 0.0, 0
        for d in parts:
            total = total + nn(x_s[:, start : start + d.shape[0]], d[...])
            start += d.shape[0]
        return total

    for m, parts in enumerate(((dq_ref,), dk_refs, dv_refs)):
        if not block_rows:
            first_ref[m] = over_keys(parts)
            continue
        w_s[...] = over_keys(parts)
        core = core_ref[0]
        at = slice(m * block_rows, (m + 1) * block_rows)
        for b in range(first_ref.shape[0]):
            far = pl.multiple_of((2 * b + 1 - core) * block_rows, block_rows)
            near = pl.multiple_of((2 * b + core) * block_rows, block_rows)
            first_ref[b, at] = w_s[pl.ds(far, block_rows), :].astype(BF)
            second_ref[b, at] = w_s[pl.ds(near, block_rows), :]
    if block_rows:
        for b in range(first_ref.shape[0]):
            first_ref[b, 3 * block_rows :] = sums.astype(BF)
            second_ref[b, 3 * block_rows :] = sums
    else:
        second_ref[...] = sums


def attn_grads(core, xs, dq, extra, dks, dvs, n):
    rows, width = dq.shape
    block_rows = width // n if (width // n) % 16 == 0 else 0
    x_spec = pl.BlockSpec((rows, width), lambda i, c: (0, 0))

    def d_spec(d):
        return pl.BlockSpec((d.shape[0], GROUP), lambda i, c: (0, i))

    if block_rows:
        shape = (n // 2, 3 * block_rows + EXTRA)
        spec = pl.BlockSpec((*shape, GROUP), lambda i, c: (0, 0, i))
        results = [(spec, jax.ShapeDtypeStruct((*shape, width), t)) for t in (BF, F32)]
    else:
        spec = pl.BlockSpec((3, width, GROUP), lambda i, c: (0, 0, i))
        results = [(spec, jax.ShapeDtypeStruct((3, width, width), F32))]
        spec = pl.BlockSpec((EXTRA, GROUP), lambda i, c: (0, i))
        results.append((spec, jax.ShapeDtypeStruct((EXTRA, width), F32)))
    return pl.pallas_call(
        partial(attn_grad_kernel, calls=len(dks), slots=len(xs), block_rows=block_rows),
        out_shape=tuple(r[1] for r in results),
        grid_spec=pltpu.PrefetchScalarGridSpec(
            num_scalar_prefetch=1,
            grid=(width // GROUP,),
            in_specs=[x_spec] * len(xs) + [d_spec(d) for d in (dq, extra, *dks, *dvs)],
            out_specs=[r[0] for r in results],
            scratch_shapes=[pltpu.VMEM((width, rows * len(xs)), BF), pltpu.VMEM((width, GROUP), F32)],
        ),
        cost_estimate=pl.CostEstimate(flops=FEW, bytes_accessed=FEW, transcendentals=0),
        name="attn_grads",
    )(core, *xs, dq, extra, *dks, *dvs)


def norm_parts(rows_in):
    mean = jnp.mean(rows_in, axis=-1, keepdims=True)
    centred = rows_in - mean
    spread = jnp.mean(centred * centred, axis=-1, keepdims=True)
    r = lax.rsqrt(spread + EPSILON)
    return centred * r, r


def norm_back(g_y, n, r, gain):
    e = g_y * gain
    return r * (e - jnp.mean(e, axis=-1, keepdims=True) - n * jnp.mean(e * n, axis=-1, keepdims=True))


def gelu_parts(u):
    c = 0.7978845608028654
    square = u * u
    th = jnp.tanh(c * u * (1.0 + 0.044715 * square))
    half = 0.5 * (1.0 + th)
    slope = half + 0.5 * u * (1.0 - th * th) * (c + 3 * 0.044715 * c * square)
    return u * half, slope


def down_rows(x):
    return jnp.sum(x, axis=0, keepdims=True)


def middle_kernel(known, *refs, count, offsets):
    w_refs, refs = (refs[:count], refs[count : 2 * count]), refs[2 * count :]
    ctx_ref, x_ref, grad_ref, vec_ref, bias_ref = refs[:5]
    out_ref, first_ref, gctx_ref, lefts_ref, rights_ref, sums_ref = refs[5:11]
    w_s, mix_ref, slope_s, n1_s, r1_s, acc_s, sems, mix_sems = refs[11:]
    parts, units = bias_ref.shape
    rows, width = x_ref.shape

    def copy(which, t, j):
        return piece_copy(
            w_refs[which], offsets[which], j, known[1], 2 * width // units + t, units, w_s.at[which, t], sems.at[which, t, j]
        )

    mix_copies = [
        piece_copy(w_refs[1], offsets[1], j, known[1], 1, width, mix_ref, mix_sems.at[j]) for j in range(count)
    ]
    for mix_copy in mix_copies:
        mix_copy.start()
    for which in range(2):
        for t in range(parts):
            for j in range(count):
                copy(which, t, j).start()
    for mix_copy in mix_copies:
        mix_copy.wait()

    def cols(t):
        return pl.ds(pl.multiple_of(t * units, units), units)

    first_sum = x_ref[...].astype(F32) + nt(ctx_ref[...], mix_ref[...]) + vec_ref[0:1, :]
    n1, r1 = norm_parts(first_sum)
    n1_s[...] = n1
    r1_s[...] = jnp.broadcast_to(r1, r1_s.shape)
    acc_s[...] = n1 * vec_ref[1:2, :] + vec_ref[2:3, :]
    lefts_ref[1] = acc_s[...].astype(BF)

    for which in range(2):
        for t in range(parts):
            for j in range(count):
                copy(which, t, j).wait()

    def up(t, _):
        pre = nn(lefts_ref[1], w_s[0, t]) + bias_ref[pl.ds(known[2 + t], 1), :]
        act, slope = gelu_parts(pre)
        slope_s[t] = slope
        low = act.astype(BF)
        rights_ref[:, cols(t)] = low
        acc_s[...] += nt(low, w_s[1, t])
        return 0

    lax.fori_loop(0, parts, up, 0)
    n2, r2 = norm_parts(acc_s[...] + vec_ref[3:4, :])
    out_ref[...] = (n2 * vec_ref[4:5, :] + vec_ref[5:6, :]).astype(BF)
    row = lax.broadcasted_iota(jnp.int32, (rows, width), 0)
    g_out = jnp.where(row < known[0], grad_ref[...].astype(F32), 0.0)
    g_second = norm_back(g_out, n2, r2, vec_ref[4:5, :])
    sums_ref[3:4, :] = down_rows(g_second)
    sums_ref[4:5, :] = down_rows(g_out * n2)
    sums_ref[5:6, :] = down_rows(g_out)
    lefts_ref[0] = g_second.astype(BF)
    acc_s[...] = g_second

    def back(t, _):
        g_pre = (nn(lefts_ref[0], w_s[1, t]) * slope_s[t]).astype(BF)
        rights_ref[:, cols(parts + t)] = g_pre
        sums_ref[pl.ds(6 + known[2 + t], 1), :] = down_rows(g_pre.astype(F32))
        acc_s[...] += nt(g_pre, w_s[0, t])
        return 0

    lax.fori_loop(0, parts, back, 0, unroll=2)
    g_normed = acc_s[...]
    n1 = n1_s[...]
    g_first = norm_back(g_normed, n1, r1_s[:, 0:1], vec_ref[1:2, :])
    sums_ref[0:1, :] = down_rows(g_first)
    sums_ref[1:2, :] = down_rows(g_normed * n1)
    sums_ref[2:3, :] = down_rows(g_normed)
    first_ref[...] = g_first
    low = g_first.astype(BF)
    lefts_ref[2] = low
    gctx_ref[...] = nn(low, mix_ref[...]).astype(BF)
    rights_ref[:, 2 * parts * units :] = ctx_ref[...]


def middle(known, pieces, ctx, x, grad, vectors, bias):
    rows, width = x.shape
    parts, units = bias.shape
    count = len(pieces[0])
    pieces, offsets = split_pieces(pieces)
    vmem = pl.BlockSpec(memory_space=pltpu.VMEM)
    shapes = [
        ((rows, width), BF),
        ((rows, width), F32),
        ((rows, width), BF),
        ((3, rows, width), BF),
        ((rows, 2 * parts * units + width), BF),
        ((6 + parts, width), F32),
    ]
    return pl.pallas_call(
        partial(middle_kernel, count=count, offsets=offsets),
        out_shape=tuple(jax.ShapeDtypeStruct(*s) for s in shapes),
        in_specs=[pl.BlockSpec(memory_space=pltpu.SMEM)] + [pl.BlockSpec(memory_space=pl.ANY)] * (2 * count) + [vmem] * 5,
        out_specs=[vmem] * len(shapes),
        scratch_shapes=[
            pltpu.VMEM((2, parts, width, units), BF),
            pltpu.VMEM((width, width), BF),
            pltpu.VMEM((parts, rows, units), F32),
            pltpu.VMEM((rows, width), F32),
            pltpu.VMEM((rows, 128), F32),
            pltpu.VMEM((rows, width), F32),
            pltpu.SemaphoreType.DMA((2, parts, count)),
            pltpu.SemaphoreType.DMA((count,)),
        ],
        compiler_params=pltpu.CompilerParams(vmem_limit_bytes=63 << 20),
        cost_estimate=pl.CostEstimate(flops=FEW, bytes_accessed=FEW, transcendentals=0),
        name="middle",
    )(known, *pieces[0], *pieces[1], ctx, x, grad, vectors, bias)


def ffn_grad_kernel(place, left_ref, right_ref, kept_1, kept_2, sent_1, sent_2, left_s, chosen_s, *, n):
    half = kept_1.shape[0]

    @pl.when(pl.program_id(0) % 4 == 0)
    def _():
        left_s[...] = left_ref[0].T
        size = left_s.shape[0] // n
        if size % 16:
            chosen_s[...] = left_s[...]
        else:
            for j in range(n):
                core, outer = j // (n // 2), j % (n // 2)
                block = place[0] ^ (2 * outer + core)
                chosen_s[j * size : (j + 1) * size, :] = left_s[pl.ds(pl.multiple_of(block * size, size), size), :]

    total = nn(chosen_s[...], right_ref[...])

    def put(kept_ref, sent_ref):
        kept_ref[...] = total[:half].astype(BF)
        sent_ref[...] = total[half:].astype(BF)

    pl.when(pl.program_id(0) < 4)(lambda: put(kept_1, sent_1))
    pl.when(pl.program_id(0) >= 4)(lambda: put(kept_2, sent_2))


def ffn_grads(place, lefts, rights, n):
    _, rows, width = lefts.shape
    units = rights.shape[1] // 9
    first_spec = pl.BlockSpec((width // 2, units), lambda i, p: (0, jnp.minimum(i, 3)))
    second_spec = pl.BlockSpec((width // 2, units), lambda i, p: (0, jnp.maximum(i - 4, 0)))
    first_shape, second_shape = (jax.ShapeDtypeStruct((width // 2, k * units), BF) for k in (4, 5))
    return pl.pallas_call(
        partial(ffn_grad_kernel, n=n),
        out_shape=(first_shape, second_shape) * 2,
        grid_spec=pltpu.PrefetchScalarGridSpec(
            num_scalar_prefetch=1,
            grid=(9,),
            in_specs=[
                pl.BlockSpec((1, rows, width), lambda i, p: (i // 4, 0, 0)),
                pl.BlockSpec((rows, units), lambda i, p: (0, i)),
            ],
            out_specs=[first_spec, second_spec] * 2,
            scratch_shapes=[pltpu.VMEM((width, rows), BF), pltpu.VMEM((width, rows), BF)],
        ),
        cost_estimate=pl.CostEstimate(flops=FEW, bytes_accessed=FEW, transcendentals=0),
        name="ffn_grads",
    )(place, lefts, rights)


def finish_kernel(*refs, r):
    terms, refs = refs[:4], refs[4:]
    total = sum(t[...].astype(F32) for t in terms)
    for m in range(3):
        refs[m][...] = total[m * r : (m + 1) * r]
    base = 3 * r

    def row(*at):
        return jnp.concatenate([total[base + i : base + i + 1] for i in at], axis=1)[0]

    for w in range(2):
        refs[3 + w][...] = row(*(2 * i + w for i in range(4)))
    for j in range(6):
        refs[5 + j][...] = row(*(8 + 10 * i + j for i in range(4)))
    refs[11][...] = row(*(8 + 10 * i + j for j in range(6, 10) for i in range(4)))


def finish(terms, r, width, units):
    cols = terms[0].shape[1]
    shapes = [(r, cols)] * 3 + [(width,)] * 8 + [(4 * units,)]
    vmem = pl.BlockSpec(memory_space=pltpu.VMEM)
    return pl.pallas_call(
        partial(finish_kernel, r=r),
        out_shape=tuple(jax.ShapeDtypeStruct(x, F32) for x in shapes),
        in_specs=[vmem] * 4,
        out_specs=[vmem] * len(shapes),
        cost_estimate=pl.CostEstimate(flops=FEW, bytes_accessed=FEW, transcendentals=0),
        name="finish",
    )(*terms)


def on_device(
    tokens,
    segments,
    query_weight,
    query_bias,
    key_weight,
    value_weight,
    value_bias,
    mix_weight,
    mix_bias,
    norm_gain,
    norm_shift,
    up_weight,
    up_bias,
    down_weight,
    down_bias,
    final_gain,
    final_shift,
    out_grad,
):
    t = lax.axis_index("tensor")
    f = lax.axis_index("fsdp")
    n = lax.axis_size("fsdp")
    rows, width = tokens.shape
    r, units = up_weight.shape
    cols = query_weight.shape[1]
    owner = slot_owner(t)

    def by_slot(vector):
        parts = vector.reshape(4, -1)
        return jnp.concatenate([lax.dynamic_slice_in_dim(parts, owner[i], 1, axis=0)[0] for i in range(4)])

    seg = jnp.where(segments == 0, 9, segments)
    where = jnp.concatenate([t[None], owner, (f & 1)[None], f[None]]).astype(jnp.int32)
    own_ids = lax.dynamic_slice_in_dim(seg[0], t * rows, rows)
    known = jnp.concatenate([jnp.stack([jnp.sum((own_ids < 9).astype(jnp.int32)), f]), owner]).astype(jnp.int32)
    vectors = jnp.stack([mix_bias, norm_gain, norm_shift, down_bias, final_gain, final_shift])
    shifts = (by_slot(query_bias), by_slot(value_bias))
    slot_of = owner_slot(t)
    goals = [sum(jnp.where(owner[k] == lax.rem(t + shift, 4), k, 0) for k in range(4)) for shift in SHIFTS]
    seg, where, known, vectors, shifts, slot_of, goals = lax.optimization_barrier(
        (seg, where, known, vectors, shifts, slot_of, goals)
    )
    small_operands = (seg, where, known, vectors, *shifts, *slot_of, *goals)

    shard = jnp.stack(
        [
            jnp.concatenate([query_weight, key_weight, value_weight, mix_weight.T], axis=1),
            up_weight,
            down_weight.T,
        ]
    )
    w_a, w_below, w_above = line_first(shard)
    w_c = after(line_second(w_below, w_above), *small_operands)
    w_b = line_third(w_c, w_below)
    w_slots = (shard, w_a, w_c, w_b)
    x_a, x_below, x_above = line_first(after(tokens, w_c))

    line = []
    for first, last in ((0, 1), (2, 2)):
        line += [w[0][:, m * cols : (m + 1) * cols] for m in (first, first + 1) for w in w_slots]
        line += [w[last] for w in w_slots]
    own = jnp.concatenate(line, axis=1)
    wide = own.shape[1] // 2
    bits = outer_bits()

    def over(block, bit):
        return lax.ppermute(block, "fsdp", partner(bit))

    if len(bits) == 2:
        beside = [over(own, bit) for bit in bits]
        far_own = over(own, 1)
        x_c = line_second(*after((x_below, x_above), far_own))
        beside = after(beside, x_a, x_c)
        across = [over(beside[0][:, :wide], bits[1]), over(beside[1][:, wide:], bits[0])]
        far_beside = [over(b, 1) for b in beside]
        x_b = line_third(x_c, x_below, *far_beside)
        far_across = [over(a, 1) for a in across]
        pieces = [
            [
                piece
                for o, b, a in ((own, beside, across), (far_own, far_beside, far_across))
                for piece in ((o, i * wide), (b[0], i * wide), (b[1], i * wide), (a[i], 0))
            ]
            for i in range(2)
        ]
    else:
        x_c = line_second(x_below, x_above)
        x_b = line_third(x_c, x_below)
        held = {0: after(own, x_a)}
        for bit in bits:
            held.update({place | (bit >> 1): over(block, bit) for place, block in sorted(held.items())})
        near = [held[p] for p in sorted(held)]
        far = [over(block, 1) for block in near]
        pieces = [[(block, i * wide) for block in near + far] for i in range(2)]
    if r % 16:
        pieces = [[(assembled([p[0][:, p[1] : p[1] + wide] for p in half]), 0)] for half in pieces]

    xs = (tokens, x_a, x_c, x_b)
    q, k, v, ctx, lse, w_all = attend_forward(xs, pieces, shifts, seg, where)
    weights = tuple((w_all, m) for m in range(3))

    layer_out, g_first, g_ctx, lefts, rights, extra = middle(
        known, pieces, ctx, tokens, out_grad, vectors, up_bias.reshape(4, units)
    )
    place = f.astype(jnp.int32)[None]
    *kept, sent_1, sent_2 = ffn_grads(place, lefts, rights, n)
    sent = [sent_1, sent_2]
    if r % 16:
        full = [jnp.concatenate(pair).reshape(n, r, -1) for pair in zip(kept, sent)]
        kept, sent = (
            [
                jnp.concatenate([lax.dynamic_slice_in_dim(x, f ^ (2 * q + c), 1)[0] for q in range(n // 2)])
                for x in full
            ]
            for c in range(2)
        )
    got = [lax.ppermute(x, "fsdp", partner(1)) for x in sent]
    g_ctx = after(g_ctx, *sent)

    args = (q, k, v, g_ctx, ctx, lse)
    dk_n, dv_n, dq, dx_b, dx_c, dx_a = attend_backward(*args, (3, 2, 1), weights, seg, where)
    r1 = lax.ppermute(dx_b, "tensor", [(0, 1), (3, 2)])
    steps = list(zip(outer_bits(), outer_bits()[::-1]))
    got = after(got, dx_b)
    held = [outer_axes(x) for x in kept]
    come = [outer_axes(x)[0] for x in got]
    lefts = [h[1] for h in held]
    held = [h[0] for h in held]
    axes = [left.index(bit) for left, bit in zip(lefts, steps[0])]

    def at(blocks, index):
        return [lax.index_in_dim(b, index, axis, keepdims=False) for b, axis in zip(blocks, axes)]

    out_halves = add_low(at(held, 1), at(come, 1))
    arrived = [lax.ppermute(o, "fsdp", partner(bit)) for o, bit in zip(out_halves, steps[0])]
    dk_o, dv_o, dq, dx_own = attend_backward(
        *args, (0,), weights, seg, where, after(dq, dx_b, *out_halves), g_first
    )
    middle_x = (dx_c.astype(F32) + after(r1, dx_own).astype(F32)).astype(BF)
    rx = lax.ppermute(middle_x, "tensor", [(0, 1), (3, 2)])
    ry = lax.ppermute(middle_x, "tensor", [(1, 2), (2, 1)])

    arrived, held, come = after((arrived, held, come), dx_own)
    blocks = [
        (a.astype(F32) + b.astype(F32) + c.astype(F32)).astype(BF)
        for a, b, c in zip(at(held, 0), at(come, 0), arrived)
    ]
    lefts = [[b for b in left if b != bit] for left, bit in zip(lefts, steps[0])]
    halves, out_halves = start_halving(blocks, lefts, steps[1])

    xs = (xs[0], xs[3], xs[2], xs[1])
    dq = after(dq, middle_x, *out_halves)
    sent, kept = attn_grads(where[5:6], xs, dq, extra, (dk_o, dk_n), (dv_o, dv_n), n)
    if r % 16:
        split = sent.reshape(3, n // 2, 2, r, width)
        sums = jnp.broadcast_to(kept, (n // 2, EXTRA, width))
        sent, kept = (
            jnp.concatenate(
                [
                    lax.dynamic_index_in_dim(split, c, 2, keepdims=False)
                    .transpose(1, 0, 2, 3)
                    .reshape(n // 2, 3 * r, width),
                    sums,
                ],
                axis=1,
            )
            for c in (1 - (f & 1), f & 1)
        )
        sent = sent.astype(BF)
    got = lax.ppermute(sent, "fsdp", partner(1))
    near = (kept + got.astype(F32)).astype(BF)
    rx, ry = (a.astype(F32) for a in after((rx, ry), sent))
    up_x = (dx_a.astype(F32) + jnp.where(t == 1, rx, ry)).astype(BF)
    down_x = jnp.where(t == 3, dx_a.astype(F32), dx_b.astype(F32) + jnp.where(t == 1, ry, rx)).astype(BF)
    from_below = lax.ppermute(up_x, "tensor", [(0, 1), (1, 2), (2, 3)])
    from_above = lax.ppermute(down_x, "tensor", [(1, 0), (2, 1), (3, 2)])

    d_one, d_two = add_low(halves[0], after(halves[1], sent))
    for pair in steps[2:]:
        halves, _ = start_halving([d_one, d_two], halves[2], pair)
        d_one, d_two = add_low(halves[0], halves[1])
    early = jnp.stack(
        [
            jnp.concatenate(
                [
                    d_one[:, i * units : (i + 1) * units],
                    d_two[:, i * units : (i + 1) * units],
                    d_two[:, 4 * units + i * cols : 4 * units + (i + 1) * cols],
                ],
                axis=1,
            )
            for i in range(4)
        ]
    )

    early_own, early = early[0], spread(early, goals)
    same_core = [list(range(c, n, 2)) for c in range(2)]
    arrived = lax.all_to_all(near, "fsdp", split_axis=0, concat_axis=0, axis_index_groups=same_core, tiled=True)
    arrived = after(arrived, *early)
    late = jnp.sum(arrived.astype(F32), axis=0).astype(BF)
    count = 12
    by_head = jnp.stack([late[3 * r : 3 * r + 2, i * cols : (i + 1) * cols] for i in range(4)])
    by_head = in_line_order(by_head, slot_of).reshape(8, cols)
    whole = [late[3 * r + 2 : 3 * r + count, i * cols : (i + 1) * cols] for i in range(4)]
    below = jnp.concatenate([by_head, *whole])
    late = jnp.stack(
        [jnp.concatenate([late[: 3 * r, i * cols : (i + 1) * cols], below]) for i in range(4)]
    )
    *late, qb, vb, b0, b1, b2, b3, b4, b5, up_sums = finish((late[0], *spread(late, goals)), r, width, units)
    early = total(early_own, early)
    tokens_grad = dx_own + from_below.astype(F32) + from_above.astype(F32)

    return (
        layer_out,
        tokens_grad,
        late[0],
        qb,
        late[1],
        late[2],
        vb,
        early[:, 2 * units :].T,
        b0,
        b1,
        b2,
        early[:, units : 2 * units],
        up_sums,
        early[:, :units].T,
        b3,
        b4,
        b5,
    )


def solution(mesh):
    both, rows_f, square, flipped = (
        P(("fsdp", "tensor"), None),
        P("fsdp", None),
        P("fsdp", "tensor"),
        P("tensor", "fsdp"),
    )
    return jax.shard_map(
        on_device,
        mesh=mesh,
        in_specs=(
            both, rows_f, square, P(), square, square, P(), flipped, P(), P(), P(),
            square, P(), flipped, P(), P(), P(), both,
        ),
        out_specs=(
            both, both, square, P(), square, square, P(), flipped, P(), P(), P(),
            square, P(), flipped, P(), P(), P(),
        ),
        check_vma=False,
    )
```
